32 devices in a mesh: ctx: 8 (over z, y), head: 4 (over x, core).
Axes of the slice: x: 2, y: 2, z: 4, core: 2. Of those that a mesh axis runs over, the one named last changes fastest.
Arguments:
- queries: bfloat16 [4096, 32, 128], P(('ctx', 'head')), may hold values from -6 to 6
- key_states: bfloat16 [4096, 4, 128], P(('ctx', 'head')), may hold values from -6 to 6
- value_states: bfloat16 [4096, 4, 128], P(('ctx', 'head')), may hold values from -6 to 6
- out_grad: bfloat16 [4096, 32, 128], P(('ctx', 'head')), may hold values from -6 to 6
- log_sums: float32 [32, 4096], P('head', 'ctx'), may hold values from 3 to 6
- row_deltas: float32 [32, 4096], P('head', 'ctx'), may hold values from -10 to 10
- block_pairs: int32 [64, 4], replicated, may hold values from 0 to 63, as said below
- pair_kinds: int32 [64, 4], replicated, may hold values from 0 to 2, as said below
Outputs:
- query_grad: bfloat16 [4096, 32, 128], P(('ctx', 'head'))
- key_grad: bfloat16 [4096, 4, 128], P(('ctx', 'head'))
- value_grad: bfloat16 [4096, 4, 128], P(('ctx', 'head'))
The draws below stay inside these ranges and needn't reach their ends.
Inputs may be any that keep to these rules, and one draw needn't show every extreme that they name: `block_pairs`: row g lists the key blocks of query block g. Slot 0 names g itself, slot 1 names g - 1, slot 2 names key block 0; slots 3 and up name blocks of shards at least two shards before the shard of g, never of shard 0. The blocks of the live slots of a row are distinct and none is later than g; a slot of kind 0 names block 0. Counting shards of 8 consecutive query blocks, the query blocks of one shard name at most one key block held by any other single shard, and this is reached. `pair_kinds`: 1 marks a full block pair, 2 the pair of a block with itself, 0 an unused slot. Slot 0 is always 2 and no other slot is 2; slot 1 is 0 only for g = 0; slot 2 is 0 exactly for g < 2 and for the query blocks of the second shard.
All inputs are finite; a program needn't handle non-finite values.
Results may differ from the reference program's by a relative error of at most 0.0012.
The reference program's roundings to bfloat16 on the way count: a program that leaves them out, or rounds other values in their place, can miss the bound.
Values may be sent and summed in bfloat16 or wider, within the bound.
A program may use at most 64 MiB of HBM per device.

```python
import jax
import jax.numpy as jnp
from jax import lax

HD = 128
QH = 32
KVH = 4
BLOCK = 64
REMOTE = 1
TOKENS = 4096
QB_DEV = 8
NQB = 64


def pair_table(key):
    base_key = jax.random.fold_in(key, 4711)
    shards = NQB // QB_DEV
    spread = QB_DEV * REMOTE
    pool = max(spread, shards)
    order_keys = jax.random.split(jax.random.fold_in(base_key, 1), shards)
    orders = jax.vmap(lambda sub_key: jax.random.permutation(sub_key, pool)[:spread])(order_keys).astype(jnp.int32)
    links = jax.random.randint(jax.random.fold_in(base_key, 2), (shards, shards), 0, QB_DEV).astype(jnp.int32)
    dropped = jax.random.randint(jax.random.fold_in(base_key, 3), (shards, spread), 0, 4)
    shard_ids = jnp.arange(shards, dtype=jnp.int32)[:, None]
    owners = jnp.minimum(orders, shards - 1).astype(jnp.int32)
    is_live = (orders >= 1) & (orders <= shard_ids - 2) & (dropped > 0)
    chosen = jnp.take_along_axis(links, owners, axis=1)
    far_blocks = jnp.where(is_live, owners * QB_DEV + chosen, 0).astype(jnp.int32).reshape(NQB, REMOTE)
    far_kinds = is_live.astype(jnp.int32).reshape(NQB, REMOTE)
    query_ids = jnp.arange(NQB, dtype=jnp.int32)
    shard_of = query_ids // QB_DEV
    prev_kind = (query_ids >= 1).astype(jnp.int32)
    hub_kind = ((query_ids >= 2) & (shard_of != 1)).astype(jnp.int32)
    near_blocks = jnp.stack([query_ids, jnp.where(prev_kind > 0, query_ids - 1, 0), jnp.zeros_like(query_ids)], axis=1)
    near_kinds = jnp.stack([jnp.full_like(query_ids, 2), prev_kind, hub_kind], axis=1)
    blocks_all = jnp.concatenate([near_blocks, far_blocks], axis=1).astype(jnp.int32)
    kinds_all = jnp.concatenate([near_kinds, far_kinds], axis=1).astype(jnp.int32)
    return (blocks_all, kinds_all)


def draw_block_pairs(key, part):
    return pair_table(key)[0]


def draw_pair_kinds(key, part):
    return pair_table(key)[1]


def block_levels(own_key, shape, cuts, smallest, top_value):
    level = 1.0
    for position, parts in cuts:
        draws = jax.random.uniform(jax.random.fold_in(jax.random.fold_in(own_key, 6), position), (parts,), jnp.float32, smallest / len(cuts), top_value / len(cuts))
        level = level * jnp.repeat(jnp.exp(draws), shape[position] // parts).reshape((-1,) + (1,) * (len(shape) - 1 - position))
    return level


def bell_draw(stream_key, extent, width, limit, cuts=(), held_as=jnp.bfloat16):
    result = width * jax.random.normal(stream_key, extent, jnp.float32)
    if cuts:
        result = result * block_levels(stream_key, extent, cuts, -0.22, 0.18)
    return jnp.clip(result, -limit, limit).astype(held_as)


def setup_inputs(seed: int = 0) -> dict:
    key_list = jax.random.split(jax.random.key(seed), 9)
    queries = bell_draw(key_list[0], (TOKENS, QH, HD), 1.0, 6.0, ((0, 32),))
    key_states = bell_draw(key_list[1], (TOKENS, KVH, HD), 1.0, 6.0, ((0, 32),))
    value_states = bell_draw(key_list[2], (TOKENS, KVH, HD), 1.0, 6.0, ((0, 32),))
    out_grad = bell_draw(key_list[3], (TOKENS, QH, HD), 1.0, 6.0, ((0, 32),))
    log_sums = jnp.clip(3.0 + 3.0 * jax.random.uniform(key_list[4], (QH, TOKENS), jnp.float32) ** block_levels(key_list[4], (QH, TOKENS), ((0, 4), (1, 8)), -0.2, 0.2), 3.0, 6.0)
    row_deltas = bell_draw(key_list[5], (QH, TOKENS), 2.0, 10.0, ((0, 4), (1, 8)), jnp.float32)
    block_pairs = draw_block_pairs(jax.random.fold_in(key_list[8], 71), 0)
    pair_kinds = draw_pair_kinds(jax.random.fold_in(key_list[8], 71), 0)
    return {"queries": queries, "key_states": key_states, "value_states": value_states, "out_grad": out_grad, "log_sums": log_sums, "row_deltas": row_deltas, "block_pairs": block_pairs, "pair_kinds": pair_kinds}


def reference(queries, key_states, value_states, out_grad, log_sums, row_deltas, block_pairs, pair_kinds):
    head_group = QH // KVH
    score_scale = HD ** -0.5
    causal = jnp.arange(BLOCK)[:, None] >= jnp.arange(BLOCK)[None, :]
    query_all = queries.astype(jnp.float32).reshape(NQB, BLOCK, KVH, head_group, HD).transpose(2, 0, 1, 3, 4)
    grad_all = out_grad.astype(jnp.float32).reshape(NQB, BLOCK, KVH, head_group, HD).transpose(2, 0, 1, 3, 4)
    key_all = key_states.astype(jnp.float32).reshape(NQB, BLOCK, KVH, HD).transpose(2, 0, 1, 3)
    value_all = value_states.astype(jnp.float32).reshape(NQB, BLOCK, KVH, HD).transpose(2, 0, 1, 3)
    log_all = log_sums.reshape(KVH, head_group, NQB, BLOCK).transpose(0, 2, 1, 3)
    delta_all = row_deltas.reshape(KVH, head_group, NQB, BLOCK).transpose(0, 2, 1, 3)

    def per_head(inputs):
        head_queries, head_grads, head_keys, head_values, head_logs, head_deltas = inputs

        def per_slot(running, column):
            query_acc, key_acc, value_acc = running
            slot_blocks, slot_kinds = column
            key_tile = head_keys[slot_blocks]
            value_tile = head_values[slot_blocks]
            scores = jnp.einsum("nbgd,nkd->ngbk", head_queries, key_tile) * score_scale
            weights = jnp.exp(scores - head_logs[..., None])
            full_pair = (slot_kinds == 1)[:, None, None, None]
            diagonal_pair = (slot_kinds == 2)[:, None, None, None]
            weights = jnp.where(full_pair | (diagonal_pair & causal), weights, 0.0)
            rounded = lax.optimization_barrier(weights.astype(jnp.bfloat16)).astype(jnp.float32)
            value_term = jnp.einsum("ngbk,nbgd->nkd", rounded, head_grads)
            prob_grad = jnp.einsum("nbgd,nkd->ngbk", head_grads, value_tile)
            dscore = weights * (prob_grad - head_deltas[..., None])
            dscore = lax.optimization_barrier(dscore.astype(jnp.bfloat16)).astype(jnp.float32)
            query_acc = query_acc + jnp.einsum("ngbk,nkd->nbgd", dscore, key_tile) * score_scale
            key_term = jnp.einsum("ngbk,nbgd->nkd", dscore, head_queries) * score_scale
            key_acc = key_acc.at[slot_blocks].add(key_term)
            value_acc = value_acc.at[slot_blocks].add(value_term)
            return (query_acc, key_acc, value_acc), None

        initial = (jnp.zeros((NQB, BLOCK, head_group, HD), jnp.float32),
                   jnp.zeros((NQB, BLOCK, HD), jnp.float32),
                   jnp.zeros((NQB, BLOCK, HD), jnp.float32))
        finals, unused = lax.scan(per_slot, initial, (block_pairs.T, pair_kinds.T))
        return finals

    query_acc, key_acc, value_acc = lax.map(per_head, (query_all, grad_all, key_all, value_all, log_all, delta_all))
    query_grad = query_acc.transpose(1, 2, 0, 3, 4).reshape(TOKENS, QH, HD).astype(jnp.bfloat16)
    key_grad = key_acc.transpose(1, 2, 0, 3).reshape(TOKENS, KVH, HD).astype(jnp.bfloat16)
    value_grad = value_acc.transpose(1, 2, 0, 3).reshape(TOKENS, KVH, HD).astype(jnp.bfloat16)
    return query_grad, key_grad, value_grad
```

```python
from functools import partial

import jax
import jax.numpy as jnp
from jax import lax
from jax.experimental import pallas as pl
from jax.experimental.pallas import tpu as pltpu
from jax.sharding import PartitionSpec as P

BLOCK = 64
NEAR = 3
MESH = pl.DeviceIdType.MESH
NT = (((1,), (1,)), ((), ()))
TN = (((0,), (0,)), ((), ()))


def tile_grads(keys, values, q, g, log_row, delta_row, live, scale):
    scores = lax.dot_general(keys, q, NT, preferred_element_type=jnp.float32) * scale
    weights = jnp.where(live, jnp.exp(scores - log_row), 0.0)
    prob_grad = lax.dot_general(values, g, NT, preferred_element_type=jnp.float32)
    dscore = (weights * (prob_grad - delta_row)).astype(jnp.bfloat16)
    dv = jnp.dot(weights.astype(jnp.bfloat16), g, preferred_element_type=jnp.float32)
    dk = jnp.dot(dscore, q, preferred_element_type=jnp.float32)
    dq = lax.dot_general(dscore, keys, TN, preferred_element_type=jnp.float32)
    return dq, dk, dv


def kernel(
    n_ctx,
    n_head,
    n_slot,
    pair_tab,
    kind_tab,
    q_hbm,
    g_hbm,
    k_ref,
    v_ref,
    log_ref,
    delta_ref,
    dq_out,
    dk_out,
    dv_out,
    wide,
    kv_own,
    kv_loc,
    kv_prev,
    outgoing,
    arrived,
    late_send,
    late_kv,
    q_raw,
    g_raw,
    q_flat,
    g_flat,
    stat_land,
    stat_rows,
    dq_acc,
    dq_buf,
    own_acc,
    prev_part,
    prev_land,
    late_part,
    late_land,
    part,
    ret,
    blk_part,
    blk_land,
    want,
    owner,
    load_sem,
    kv_send,
    kv_recv,
    stat_send,
    stat_recv,
    prev_send,
    prev_recv,
    arr_send,
    arr_recv,
    late_ssem,
    late_rsem,
    dq_sem,
    back_send,
    back_recv,
    red_send,
    red_recv,
    ret_send,
    ret_recv,
    blk_send,
    blk_recv,
):
    rank = lax.axis_index("ctx")
    me = lax.axis_index("head")
    rows = q_hbm.shape[0]
    width = q_hbm.shape[2]
    heads = q_hbm.shape[1] // n_head
    per = rows // BLOCK
    blocks = per * n_head
    lanes = BLOCK * heads
    n_far = n_slot - NEAR
    n_late = 1 + n_far
    scale = width ** (-0.5)
    first = rank * blocks
    bf16, f32 = jnp.bfloat16, jnp.float32

    def peer(d):
        return lax.rem(me // 2 + d // 2, n_head // 2) * 2 + lax.rem(
            lax.rem(me, 2) + lax.rem(d, 2), 2
        )

    far_first = list(range(2, n_head)) + [1]
    has_prev = (rank > 0) | (me > 0)
    has_next = (rank < n_ctx - 1) | (me < n_head - 1)
    prev_dev = (jnp.where(me > 0, rank, rank - 1), jnp.where(me > 0, me - 1, n_head - 1))
    next_dev = (
        jnp.where(me < n_head - 1, rank, rank + 1),
        jnp.where(me < n_head - 1, me + 1, 0),
    )
    outer_prev = (me == 0) & (rank > 0)
    outer_next = (me == n_head - 1) & (rank < n_ctx - 1)
    take_lo = jnp.where(rank == 0, 1, rank + 2)
    owes = (rank == 0) | (rank < n_ctx - 2)

    barrier = pltpu.get_barrier_semaphore()
    for d in range(1, n_head):
        pl.semaphore_signal(barrier, inc=1, device_id=(rank, peer(d)), device_id_type=MESH)

    def greet(k, c):
        pl.semaphore_signal(
            barrier, inc=1, device_id=(lax.rem(rank + k, n_ctx), me), device_id_type=MESH
        )
        return c

    lax.fori_loop(1, n_ctx, greet, 0)

    @pl.when(outer_prev)
    def _():
        pl.semaphore_signal(barrier, inc=1, device_id=prev_dev, device_id_type=MESH)

    @pl.when(outer_next)
    def _():
        pl.semaphore_signal(barrier, inc=1, device_id=next_dev, device_id_type=MESH)

    def load_copy(u, k, j):
        return pltpu.make_async_copy(
            (q_hbm, g_hbm)[u].at[
                pl.ds(j * BLOCK, BLOCK), pl.ds(pl.multiple_of(k * heads, heads), heads)
            ],
            (q_raw, g_raw)[u].at[k, j],
            load_sem.at[u, k, j],
        )

    for u in range(2):
        for k in range(n_head):
            for j in range(per):
                load_copy(u, k, j).start()

    for at, source in ((0, k_ref), (width, v_ref)):
        wide[...] = source[...].astype(f32)
        for h in range(n_head):
            head_rows = wide[pl.ds(h, rows, stride=n_head), :]
            kv_own[h, :, :, at : at + width] = head_rows.reshape(per, BLOCK, width).astype(bf16)

    def wanted_by(s, c):
        best = jnp.int32(0)
        for i in range(blocks):
            at = s * blocks + i
            for j in range(NEAR, n_slot):
                local = pair_tab[j, at] - first
                named = (kind_tab[j, at] > 0) & (local >= 0) & (local < blocks)
                best = jnp.where(named, jnp.maximum(best, local), best)
        want[s] = best
        return c

    lax.fori_loop(take_lo, n_ctx, wanted_by, 0)
    for i in range(blocks):
        for f in range(n_far):
            at = first + i
            owner[i * n_far + f] = jnp.where(
                kind_tab[NEAR + f, at] > 0, lax.div(pair_tab[NEAR + f, at], blocks), rank
            )

    @pl.when(jnp.logical_not(has_prev))
    def _():
        kv_prev[...] = jnp.zeros_like(kv_prev)

    def flatten(t, c):
        k, j = t // per, lax.rem(t, per)
        for u, (raw, flat) in enumerate(((q_raw, q_flat), (g_raw, g_flat))):
            load_copy(u, k, j).wait()
            flat[k, j] = raw[k, j].astype(f32).reshape(lanes, width).astype(bf16)
        return c

    lax.fori_loop(0, n_head * per, flatten, 0)

    extra = outer_prev.astype(jnp.int32) + outer_next.astype(jnp.int32)
    pl.semaphore_wait(barrier, n_ctx + n_head - 2 + extra)

    def kv_copy(p):
        return pltpu.make_async_remote_copy(
            src_ref=kv_own.at[p],
            dst_ref=kv_loc.at[pl.ds(me * per, per)],
            send_sem=kv_send.at[p],
            recv_sem=kv_recv.at[me],
            device_id=(rank, p),
            device_id_type=MESH,
        )

    def stat_copy(u, p):
        return pltpu.make_async_remote_copy(
            src_ref=(log_ref, delta_ref)[u].at[:, pl.ds(pl.multiple_of(p * rows, rows), rows)],
            dst_ref=stat_land.at[u, me],
            send_sem=stat_send.at[u, p],
            recv_sem=stat_recv.at[u, me],
            device_id=(rank, p),
            device_id_type=MESH,
        )

    def prev_copy():
        return pltpu.make_async_remote_copy(
            src_ref=kv_own.at[:, per - 1],
            dst_ref=kv_prev,
            send_sem=prev_send.at[0],
            recv_sem=prev_recv.at[0],
            device_id=next_dev,
            device_id_type=MESH,
        )

    for d in far_first:
        kv_copy(peer(d)).start()
    for u in range(2):
        for d in far_first:
            stat_copy(u, peer(d)).start()

    @pl.when(has_next)
    def _():
        prev_copy().start()

    kv_loc[pl.ds(me * per, per)] = kv_own[me]
    for u, source in enumerate((log_ref, delta_ref)):
        stat_land[u, me] = source[:, pl.ds(pl.multiple_of(me * rows, rows), rows)]

    for d in range(1, n_head):
        p = peer(d)
        kv_here = kv_loc.at[pl.ds(p * per, per)]
        pltpu.make_async_copy(kv_here, kv_here, kv_recv.at[p]).wait()

    def arr_copy(s):
        return pltpu.make_async_remote_copy(
            src_ref=outgoing.at[s],
            dst_ref=arrived.at[rank],
            send_sem=arr_send.at[s],
            recv_sem=arr_recv.at[rank],
            device_id=(s, me),
            device_id_type=MESH,
        )

    def send_block(s, c):
        outgoing[s] = kv_loc[want[s]]
        arr_copy(s).start()
        return c

    lax.fori_loop(take_lo, n_ctx, send_block, 0)
    arrived[rank] = kv_loc[0]

    for d in range(1, n_head):
        p = peer(d)
        for u in range(2):
            here = stat_land.at[u, p]
            pltpu.make_async_copy(here, here, stat_recv.at[u, p]).wait()
    spread = (
        lax.broadcasted_iota(jnp.int32, (BLOCK, lanes), 1) // heads
        == lax.broadcasted_iota(jnp.int32, (BLOCK, lanes), 0)
    ).astype(bf16)
    own_row = lax.broadcasted_iota(jnp.int32, (heads, lanes), 1) % heads == lax.broadcasted_iota(
        jnp.int32, (heads, lanes), 0
    )
    stats = stat_land[...].reshape(2 * n_head * heads, rows)
    high = stats.astype(bf16)
    rest = stats - high.astype(f32)
    mid = rest.astype(bf16)
    low = (rest - mid.astype(f32)).astype(bf16)
    for j in range(per):
        at = slice(j * BLOCK, (j + 1) * BLOCK)
        by_lane = sum(
            jnp.dot(piece[:, at], spread, preferred_element_type=f32) for piece in (high, mid, low)
        ).reshape(2 * n_head, heads, lanes)
        stat_rows[j] = jnp.sum(jnp.where(own_row[None], by_lane, 0.0), axis=1)

    @pl.when(has_prev)
    def _():
        pltpu.make_async_copy(kv_prev, kv_prev, prev_recv.at[0]).wait()

    def back_copy(k):
        return pltpu.make_async_remote_copy(
            src_ref=prev_part.at[k],
            dst_ref=prev_land.at[k],
            send_sem=back_send.at[k],
            recv_sem=back_recv.at[k],
            device_id=prev_dev,
            device_id_type=MESH,
        )

    key_row = lax.broadcasted_iota(jnp.int32, (2 * BLOCK, lanes), 0)
    causal = (key_row >= BLOCK) | (
        key_row <= lax.broadcasted_iota(jnp.int32, (2 * BLOCK, lanes), 1) // heads
    )
    pair_row = lax.broadcasted_iota(jnp.int32, (2 * BLOCK, 1), 0)

    for j in range(per):
        prev_kind = kind_tab[1, first + me * per + j]
        near_live = causal & (jnp.where(pair_row < BLOCK, 1, prev_kind) > 0)

        def near_step(k, c, j=j, near_live=near_live):
            before = kv_prev[k] if j == 0 else kv_own[k, j - 1]
            kv = jnp.concatenate([kv_own[k, j], before], axis=0)
            dq, dk, dv = tile_grads(
                kv[:, :width],
                kv[:, width:],
                q_flat[k, j],
                g_flat[k, j],
                stat_rows[j, pl.ds(k, 1)],
                stat_rows[j, pl.ds(n_head + k, 1)],
                near_live,
                scale,
            )
            dq_acc[k, j] = dq
            for u, terms in enumerate((dk, dv)):
                own_acc[u, k, j] = terms[:BLOCK]
                if j == 0:
                    prev_part[k, u] = terms[BLOCK:]
                else:
                    own_acc[u, k, j - 1] += terms[BLOCK:]
            if j == 0:

                @pl.when(has_prev)
                def _():
                    back_copy(k).start()

            return c

        lax.fori_loop(0, n_head, near_step, 0, unroll=2)

    def arr_wait(o, c):
        pltpu.make_async_copy(arrived.at[o], arrived.at[o], arr_recv.at[o]).wait()
        return c

    @pl.when(rank > 0)
    def _():
        arr_wait(0, 0)

    lax.fori_loop(1, rank - 1, arr_wait, 0)

    def late_copy(p):
        return pltpu.make_async_remote_copy(
            src_ref=late_send.at[p],
            dst_ref=late_kv.at[me],
            send_sem=late_ssem.at[p],
            recv_sem=late_rsem.at[me],
            device_id=(rank, p),
            device_id_type=MESH,
        )

    def fill_late(buf, at, p):
        buf[at, 0] = arrived[0]
        for j in range(per):
            for f in range(n_far):
                buf[at, 1 + j * n_far + f] = arrived[owner[(p * per + j) * n_far + f]]

    for d in far_first:
        p = peer(d)
        fill_late(late_send, p, p)
        late_copy(p).start()
    fill_late(late_kv, me, me)
    for d in range(1, n_head):
        p = peer(d)
        pltpu.make_async_copy(late_kv.at[p], late_kv.at[p], late_rsem.at[p]).wait()

    def red_copy(u, k):
        return pltpu.make_async_remote_copy(
            src_ref=late_part.at[k, u],
            dst_ref=late_land.at[me, u],
            send_sem=red_send.at[u, k],
            recv_sem=red_recv.at[u, me],
            device_id=(rank, k),
            device_id_type=MESH,
        )

    def dq_copy(k, j):
        return pltpu.make_async_copy(
            dq_buf.at[k, j],
            dq_out.at[
                pl.ds(j * BLOCK, BLOCK), pl.ds(pl.multiple_of(k * heads, heads), heads)
            ],
            dq_sem.at[k, j],
        )

    late_row = lax.broadcasted_iota(jnp.int32, (n_late * BLOCK, 1), 0) // BLOCK

    def late_step(k):
        for j in range(per):
            live = jnp.zeros((n_late * BLOCK, 1), jnp.int32)
            for f in range(n_late):
                kind = kind_tab[NEAR - 1 + f, first + me * per + j]
                live = jnp.where(late_row == f, kind, live)
            kv = jnp.concatenate(
                [late_kv[k, 0]] + [late_kv[k, 1 + j * n_far + f] for f in range(n_far)], axis=0
            )
            dq, dk, dv = tile_grads(
                kv[:, :width],
                kv[:, width:],
                q_flat[k, j],
                g_flat[k, j],
                stat_rows[j, pl.ds(k, 1)],
                stat_rows[j, pl.ds(n_head + k, 1)],
                live > 0,
                scale,
            )
            dq_buf[k, j] = ((dq_acc[k, j] + dq) * scale).reshape(BLOCK, heads, width).astype(bf16)
            dq_copy(k, j).start()
            for u, terms in enumerate((dk, dv)):
                if j == 0:
                    late_part[k, u, 0] = terms[:BLOCK]
                else:
                    late_part[k, u, 0] += terms[:BLOCK]
                for f in range(n_far):
                    late_part[k, u, 1 + j * n_far + f] = terms[(1 + f) * BLOCK : (2 + f) * BLOCK]

    def late_remote(t, c):
        k = peer(jnp.where(t < n_head - 2, t + 2, 1))
        late_step(k)
        for u in range(2):
            red_copy(u, k).start()
        return c

    lax.fori_loop(0, n_head - 1, late_remote, 0)
    late_step(me)

    def ret_copy(u, o):
        return pltpu.make_async_remote_copy(
            src_ref=part.at[u, o],
            dst_ref=ret.at[u, rank],
            send_sem=ret_send.at[u, o],
            recv_sem=ret_recv.at[u, rank],
            device_id=(o, me),
            device_id_type=MESH,
        )

    sources = [(peer(d), late_land) for d in range(1, n_head)] + [(me, late_part)]
    for u in range(2):
        for d in range(1, n_head):
            here = late_land.at[peer(d), u]
            pltpu.make_async_copy(here, here, red_recv.at[u, peer(d)]).wait()
        part[u, 0] = sum(buf[p, u, 0] for p, buf in sources)

        @pl.when(rank > 0)
        def _():
            ret_copy(u, 0).start()

        def send_part(o, c):
            terms = jnp.zeros((BLOCK, width), f32)
            for p, buf in sources:
                for j in range(per):
                    for f in range(n_far):
                        mine = owner[(p * per + j) * n_far + f] == o
                        terms += jnp.where(mine, buf[p, u, 1 + j * n_far + f], 0.0)
            part[u, o] = terms
            ret_copy(u, o).start()
            return c

        lax.fori_loop(1, rank - 1, send_part, 0)

    def blk_copy(u, p):
        return pltpu.make_async_remote_copy(
            src_ref=blk_part.at[p, u],
            dst_ref=blk_land.at[me, u],
            send_sem=blk_send.at[u, p],
            recv_sem=blk_recv.at[u, me],
            device_id=(rank, p),
            device_id_type=MESH,
        )

    @pl.when(owes)
    def _():
        for u in range(2):
            blk_part[:, u] = jnp.zeros((n_head, per, BLOCK, width), f32)

            @pl.when(rank == 0)
            def _():
                blk_part[0, u, 0] = part[u, 0]

            def take_part(s, c):
                pltpu.make_async_copy(ret.at[u, s], ret.at[u, s], ret_recv.at[u, s]).wait()
                for i in range(blocks):
                    blk_part[i // per, u, i % per] += jnp.where(want[s] == i, ret[u, s], 0.0)
                return c

            lax.fori_loop(take_lo, n_ctx, take_part, 0)
            for d in far_first:
                blk_copy(u, peer(d)).start()

    @pl.when(has_next)
    def _():
        for k in range(n_head):
            pltpu.make_async_copy(prev_land.at[k], prev_land.at[k], back_recv.at[k]).wait()
            for u in range(2):
                own_acc[u, k, per - 1] += prev_land[k, u]

    @pl.when(owes)
    def _():
        for u in range(2):
            own_acc[u, me] += blk_part[me, u]
            for d in range(1, n_head):
                p = peer(d)
                here = blk_land.at[p, u]
                pltpu.make_async_copy(here, here, blk_recv.at[u, p]).wait()
                own_acc[u, p] += blk_land[p, u]

    for u, out in ((0, dk_out), (1, dv_out)):
        for h in range(n_head):
            terms = own_acc[u, h].reshape(rows, width)
            wide[pl.ds(h, rows, stride=n_head), :] = terms * scale if u == 0 else terms
        out[...] = wide[...].astype(bf16)

    def sent_block(s, c):
        arr_copy(s).wait_send()
        return c

    lax.fori_loop(take_lo, n_ctx, sent_block, 0)

    def sent_part(o, c):
        ret_copy(0, o).wait_send()
        ret_copy(1, o).wait_send()
        return c

    @pl.when(rank > 0)
    def _():
        sent_part(0, 0)

    lax.fori_loop(1, rank - 1, sent_part, 0)
    for d in range(1, n_head):
        p = peer(d)
        kv_copy(p).wait_send()
        late_copy(p).wait_send()
        for u in range(2):
            stat_copy(u, p).wait_send()
            red_copy(u, p).wait_send()

    @pl.when(owes)
    def _():
        for d in range(1, n_head):
            for u in range(2):
                blk_copy(u, peer(d)).wait_send()

    @pl.when(has_next)
    def _():
        prev_copy().wait_send()

    @pl.when(has_prev)
    def _():
        for k in range(n_head):
            back_copy(k).wait_send()

    for k in range(n_head):
        for j in range(per):
            dq_copy(k, j).wait()


def tail(dq_in, dk_in, dv_in, dq_out, dk_out, dv_out, dq_held, dk_held, dv_held, loads, stores):
    pieces = loads.shape[0] - 2
    step = dq_held.shape[0] // pieces
    parts = [pl.ds(k * step, step) for k in range(pieces)]
    routes = [(dq_in.at[at], dq_held.at[at], dq_out.at[at]) for at in parts]
    routes += [(dk_in, dk_held, dk_out), (dv_in, dv_held, dv_out)]
    for k, (source, held, _) in enumerate(routes):
        pltpu.make_async_copy(source, held, loads.at[k]).start()
    for k, (source, held, target) in enumerate(routes):
        pltpu.make_async_copy(source, held, loads.at[k]).wait()
        pltpu.make_async_copy(held, target, stores.at[k]).start()
    for k, (_, held, target) in enumerate(routes):
        pltpu.make_async_copy(held, target, stores.at[k]).wait()


def shards(
    n_ctx,
    n_head,
    queries,
    key_states,
    value_states,
    out_grad,
    log_sums,
    row_deltas,
    block_pairs,
    pair_kinds,
):
    rows, all_heads, width = queries.shape
    heads = all_heads // n_head
    n_slot = block_pairs.shape[1]
    n_far = n_slot - NEAR
    per = rows // BLOCK
    blocks = per * n_head
    lanes = BLOCK * heads
    n_late = 1 + per * n_far
    bf16, f32 = jnp.bfloat16, jnp.float32
    flat = (rows * n_head, width)
    kv = (BLOCK, 2 * width)
    term = (BLOCK, width)
    vmem = pl.BlockSpec(memory_space=pltpu.VMEM)
    smem = pl.BlockSpec(memory_space=pltpu.SMEM)
    anywhere = pl.BlockSpec(memory_space=pl.ANY)
    dma = pltpu.SemaphoreType.DMA
    raw = pltpu.VMEM((n_head, per, BLOCK, heads, width), bf16)
    rolled = pltpu.VMEM((n_head, per, lanes, width), bf16)
    dq, dk, dv = pl.pallas_call(
        partial(kernel, n_ctx, n_head, n_slot),
        out_shape=(
            jax.ShapeDtypeStruct(queries.shape, bf16),
            jax.ShapeDtypeStruct(flat, bf16),
            jax.ShapeDtypeStruct(flat, bf16),
        ),
        in_specs=[smem, smem, anywhere, anywhere, vmem, vmem, vmem, vmem],
        out_specs=(anywhere, vmem, vmem),
        scratch_shapes=[
            pltpu.VMEM(flat, f32),
            pltpu.VMEM((n_head, per) + kv, bf16),
            pltpu.VMEM((blocks,) + kv, bf16),
            pltpu.VMEM((n_head,) + kv, bf16),
            pltpu.VMEM((n_ctx,) + kv, bf16),
            pltpu.VMEM((n_ctx,) + kv, bf16),
            pltpu.VMEM((n_head, n_late) + kv, bf16),
            pltpu.VMEM((n_head, n_late) + kv, bf16),
            raw,
            raw,
            rolled,
            rolled,
            pltpu.VMEM((2, n_head, heads, rows), f32),
            pltpu.VMEM((per, 2 * n_head, lanes), f32),
            pltpu.VMEM((n_head, per, lanes, width), f32),
            raw,
            pltpu.VMEM((2, n_head, per) + term, f32),
            pltpu.VMEM((n_head, 2) + term, f32),
            pltpu.VMEM((n_head, 2) + term, f32),
            pltpu.VMEM((n_head, 2, n_late) + term, f32),
            pltpu.VMEM((n_head, 2, n_late) + term, f32),
            pltpu.VMEM((2, n_ctx) + term, f32),
            pltpu.VMEM((2, n_ctx) + term, f32),
            pltpu.VMEM((n_head, 2, per) + term, f32),
            pltpu.VMEM((n_head, 2, per) + term, f32),
            pltpu.SMEM((n_ctx,), jnp.int32),
            pltpu.SMEM((blocks * n_far,), jnp.int32),
            dma((2, n_head, per)),
            dma((n_head,)),
            dma((n_head,)),
            dma((2, n_head)),
            dma((2, n_head)),
            dma((1,)),
            dma((1,)),
            dma((n_ctx,)),
            dma((n_ctx,)),
            dma((n_head,)),
            dma((n_head,)),
            dma((n_head, per)),
            dma((n_head,)),
            dma((n_head,)),
            dma((2, n_head)),
            dma((2, n_head)),
            dma((2, n_ctx)),
            dma((2, n_ctx)),
            dma((2, n_head)),
            dma((2, n_head)),
        ],
        compiler_params=pltpu.CompilerParams(
            collective_id=0, has_side_effects=True, vmem_limit_bytes=60 * 1024 * 1024
        ),
    )(
        block_pairs.T,
        pair_kinds.T,
        queries,
        out_grad,
        key_states.reshape(flat),
        value_states.reshape(flat),
        log_sums,
        row_deltas,
    )
    dq, dk, dv = pl.pallas_call(
        tail,
        out_shape=(
            jax.ShapeDtypeStruct(queries.shape, bf16),
            jax.ShapeDtypeStruct(flat, bf16),
            jax.ShapeDtypeStruct(flat, bf16),
        ),
        in_specs=[anywhere] * 3,
        out_specs=(anywhere,) * 3,
        scratch_shapes=[
            pltpu.VMEM(queries.shape, bf16),
            pltpu.VMEM(flat, bf16),
            pltpu.VMEM(flat, bf16),
            dma((6,)),
            dma((6,)),
        ],
    )(dq, dk, dv)
    return dq, dk.reshape(key_states.shape), dv.reshape(value_states.shape)


def solution(mesh):
    tokens = P(("ctx", "head"), None, None)
    stats = P("head", "ctx")
    return jax.shard_map(
        partial(shards, mesh.shape["ctx"], mesh.shape["head"]),
        mesh=mesh,
        in_specs=(tokens, tokens, tokens, tokens, stats, stats, P(), P()),
        out_specs=(tokens, tokens, tokens),
        check_vma=False,
    )
```

```python
from functools import partial

import jax
import jax.numpy as jnp
from jax import lax
from jax.experimental import pallas as pl
from jax.experimental.pallas import tpu as pltpu
from jax.sharding import PartitionSpec as P

BLOCK = 64
NEAR = 3
CUTS = 2
MESH = pl.DeviceIdType.MESH
NT = (((1,), (1,)), ((), ()))
TN = (((0,), (0,)), ((), ()))


def tile_grads(keys, values, q, g, log_row, delta_row, live, scale):
    scores = lax.dot_general(keys, q, NT, preferred_element_type=jnp.float32) * scale
    weights = jnp.where(live, jnp.exp(scores - log_row), 0.0)
    prob_grad = lax.dot_general(values, g, NT, preferred_element_type=jnp.float32)
    dscore = (weights * (prob_grad - delta_row)).astype(jnp.bfloat16)
    dv = jnp.dot(weights.astype(jnp.bfloat16), g, preferred_element_type=jnp.float32)
    dk = jnp.dot(dscore, q, preferred_element_type=jnp.float32)
    dq = lax.dot_general(dscore, keys, TN, preferred_element_type=jnp.float32)
    return dq, dk, dv


def kernel(
    n_ctx,
    n_head,
    n_slot,
    pair_tab,
    kind_tab,
    q_hbm,
    g_hbm,
    k_ref,
    v_ref,
    log_ref,
    delta_ref,
    dq_out,
    dk_out,
    dv_out,
    wide,
    kv_own,
    kv_loc,
    kv_prev,
    outgoing,
    arrived,
    far_send,
    far_kv,
    hub_kv,
    q_raw,
    g_raw,
    q_flat,
    g_flat,
    stat_land,
    stat_rows,
    dq_acc,
    dq_buf,
    own_acc,
    prev_part,
    prev_land,
    far_part,
    far_land,
    hub_part,
    hub_land,
    hub_pair,
    hub_sum,
    hub_tree,
    hub_last,
    part,
    ret,
    blk_part,
    blk_land,
    want,
    owner,
    load_sem,
    kv_sem,
    stat_sem,
    prev_sem,
    arr_send,
    arr_recv,
    far_sem,
    hub_sem,
    dq_sem,
    back_sem,
    hred_sem,
    pair_sem,
    tree_send,
    tree_recv,
    last_sem,
    red_send,
    red_recv,
    ret_send,
    ret_recv,
    blk_send,
    blk_recv,
):
    rank = lax.axis_index("ctx")
    me = lax.axis_index("head")
    rows = q_hbm.shape[0]
    width = q_hbm.shape[2]
    heads = q_hbm.shape[1] // n_head
    per = rows // BLOCK
    blocks = per * n_head
    lanes = BLOCK * heads
    n_far = n_slot - NEAR
    here_far = per * n_far
    stages = tree_recv.shape[0]
    chunks, piece = part.shape[1], part.shape[2]
    cuts = BLOCK // piece
    others = n_head - 1
    scale = width ** (-0.5)
    first = rank * blocks
    bf16, f32 = jnp.bfloat16, jnp.float32

    def peer(d):
        return lax.rem(me // 2 + d // 2, n_head // 2) * 2 + lax.rem(
            lax.rem(me, 2) + lax.rem(d, 2), 2
        )

    def arrive(ref, sem):
        pltpu.make_async_copy(ref, ref, sem).wait()

    def remote(source, target, send, recv, device):
        return pltpu.make_async_remote_copy(
            src_ref=source,
            dst_ref=target,
            send_sem=send,
            recv_sem=recv,
            device_id=device,
            device_id_type=MESH,
        )

    far_first = list(range(2, n_head)) + [1]
    across = far_first[:-1]
    has_prev = (rank > 0) | (me > 0)
    has_next = (rank < n_ctx - 1) | (me < n_head - 1)
    prev_dev = (jnp.where(me > 0, rank, rank - 1), jnp.where(me > 0, me - 1, n_head - 1))
    next_dev = (
        jnp.where(me < n_head - 1, rank, rank + 1),
        jnp.where(me < n_head - 1, me + 1, 0),
    )
    outer_prev = (me == 0) & (rank > 0)
    outer_next = (me == n_head - 1) & (rank < n_ctx - 1)
    lends = (rank > 0) & (rank < n_ctx - 2)

    barrier = pltpu.get_barrier_semaphore()
    for d in range(1, n_head):
        pl.semaphore_signal(barrier, inc=1, device_id=(rank, peer(d)), device_id_type=MESH)

    def greet(k, c):
        pl.semaphore_signal(
            barrier, inc=1, device_id=(lax.rem(rank + k, n_ctx), me), device_id_type=MESH
        )
        return c

    lax.fori_loop(1, n_ctx, greet, 0)

    @pl.when(outer_prev)
    def _():
        pl.semaphore_signal(barrier, inc=1, device_id=prev_dev, device_id_type=MESH)

    @pl.when(outer_next)
    def _():
        pl.semaphore_signal(barrier, inc=1, device_id=next_dev, device_id_type=MESH)

    for u, (source, raw) in enumerate(((q_hbm, q_raw), (g_hbm, g_raw))):
        for k in range(n_head):
            for j in range(per):
                pltpu.make_async_copy(
                    source.at[pl.ds(j * BLOCK, BLOCK), pl.ds(k * heads, heads)],
                    raw.at[k, j],
                    load_sem.at[u],
                ).start()

    def wanted_by(s, c):
        best = jnp.int32(0)
        for i in range(blocks):
            at = s * blocks + i
            for j in range(NEAR, n_slot):
                local = pair_tab[j, at] - first
                named = (kind_tab[j, at] > 0) & (local >= 0) & (local < blocks)
                best = jnp.where(named, jnp.maximum(best, local), best)
        want[s] = best
        return c

    @pl.when(lends)
    def _():
        lax.fori_loop(rank + 2, n_ctx, wanted_by, 0)

    for i in range(blocks):
        for f in range(n_far):
            at = first + i
            owner[i * n_far + f] = jnp.where(
                kind_tab[NEAR + f, at] > 0, lax.div(pair_tab[NEAR + f, at], blocks), rank
            )

    @pl.when(jnp.logical_not(has_prev))
    def _():
        kv_prev[...] = jnp.zeros_like(kv_prev)

    for at, source in ((0, k_ref), (width, v_ref)):
        wide[...] = source[...].astype(f32)
        for h in range(n_head):
            head_rows = wide[pl.ds(h, rows, stride=n_head), :]
            kv_own[h, :, :, at : at + width] = head_rows.reshape(per, BLOCK, width).astype(bf16)

    extra = outer_prev.astype(jnp.int32) + outer_next.astype(jnp.int32)
    pl.semaphore_wait(barrier, n_ctx + n_head - 2 + extra)

    def kv_copy(p):
        return remote(
            kv_own.at[p],
            kv_loc.at[pl.ds(me * per, per)],
            kv_sem.at[0],
            kv_sem.at[1],
            (rank, p),
        )

    def first_copy(p):
        return remote(kv_own.at[p, 0], kv_loc.at[0], kv_sem.at[0], kv_sem.at[1], (rank, p))

    def stat_copy(u, p):
        return remote(
            (log_ref, delta_ref)[u].at[:, pl.ds(pl.multiple_of(p * rows, rows), rows)],
            stat_land.at[u, me],
            stat_sem.at[0],
            stat_sem.at[1],
            (rank, p),
        )

    def prev_copy():
        return remote(
            kv_own.at[:, per - 1], kv_prev, prev_sem.at[0], prev_sem.at[1], next_dev
        )

    @pl.when((rank == 0) & (me == 0))
    def _():
        for d in far_first:
            first_copy(peer(d)).start()
        kv_loc[0] = kv_own[0, 0]

    for u in range(2):
        for d in far_first:
            stat_copy(u, peer(d)).start()

    @pl.when(lends)
    def _():
        for d in far_first:
            kv_copy(peer(d)).start()
        kv_loc[pl.ds(me * per, per)] = kv_own[me]

    @pl.when(jnp.logical_not(lends) & has_next)
    def _():
        prev_copy().start()

    for u, source in enumerate((log_ref, delta_ref)):
        stat_land[u, me] = source[:, pl.ds(pl.multiple_of(me * rows, rows), rows)]

    arrive(q_raw, load_sem.at[0])
    arrive(g_raw, load_sem.at[1])

    def flatten(t, c):
        k, j = t // per, lax.rem(t, per)
        for raw, flat in ((q_raw, q_flat), (g_raw, g_flat)):
            flat[k, j] = raw[k, j].astype(f32).reshape(lanes, width).astype(bf16)
        return c

    lax.fori_loop(0, n_head * per, flatten, 0)

    def arr_copy(s):
        return remote(
            outgoing.at[s], arrived.at[rank], arr_send.at[s], arr_recv.at[rank], (s, me)
        )

    @pl.when(rank == 0)
    def _():
        @pl.when(me > 0)
        def _():
            arrive(kv_loc.at[0], kv_sem.at[1])

        def send_first(i, c):
            s = n_ctx - 1 - i
            outgoing[s] = kv_loc[0]
            arr_copy(s).start()
            return c

        lax.fori_loop(0, n_ctx - 1, send_first, 0)
        arrived[0] = kv_loc[0]

    arrive(stat_land.at[:, pl.ds(0, others)], stat_sem.at[1])
    spread = (
        lax.broadcasted_iota(jnp.int32, (BLOCK, lanes), 1) // heads
        == lax.broadcasted_iota(jnp.int32, (BLOCK, lanes), 0)
    ).astype(bf16)
    own_row = lax.broadcasted_iota(jnp.int32, (heads, lanes), 1) % heads == lax.broadcasted_iota(
        jnp.int32, (heads, lanes), 0
    )
    stats = stat_land[...].reshape(2 * n_head * heads, rows)
    high = stats.astype(bf16)
    rest = stats - high.astype(f32)
    mid = rest.astype(bf16)
    low = (rest - mid.astype(f32)).astype(bf16)
    for j in range(per):
        at = slice(j * BLOCK, (j + 1) * BLOCK)
        by_lane = sum(
            jnp.dot(part_of[:, at], spread, preferred_element_type=f32)
            for part_of in (high, mid, low)
        ).reshape(2 * n_head, heads, lanes)
        stat_rows[j] = jnp.sum(jnp.where(own_row[None], by_lane, 0.0), axis=1)

    key_row = lax.broadcasted_iota(jnp.int32, (2 * BLOCK, lanes), 0)
    causal = (key_row >= BLOCK) | (
        key_row <= lax.broadcasted_iota(jnp.int32, (2 * BLOCK, lanes), 1) // heads
    )
    pair_row = lax.broadcasted_iota(jnp.int32, (2 * BLOCK, 1), 0)

    def grads(k, j, kv, live):
        return tile_grads(
            kv[:, :width],
            kv[:, width:],
            q_flat[k, j],
            g_flat[k, j],
            stat_rows[j, pl.ds(k, 1)],
            stat_rows[j, pl.ds(n_head + k, 1)],
            live,
            scale,
        )

    def dq_copy(k, j):
        return pltpu.make_async_copy(
            dq_buf.at[k, j],
            dq_out.at[
                pl.ds(j * BLOCK, BLOCK), pl.ds(pl.multiple_of(k * heads, heads), heads)
            ],
            dq_sem.at[0],
        )

    def finish(k, j, total):
        dq_buf[k, j] = (total * scale).reshape(BLOCK, heads, width).astype(bf16)
        dq_copy(k, j).start()

    own_acc[...] = jnp.zeros_like(own_acc)

    def near(j):
        prev_kind = kind_tab[1, first + me * per + j]
        near_live = causal & (jnp.where(pair_row < BLOCK, 1, prev_kind) > 0)

        def near_step(k, c):
            before = kv_prev[k] if j == 0 else kv_own[k, j - 1]
            kv = jnp.concatenate([kv_own[k, j], before], axis=0)
            dq, dk, dv = grads(k, j, kv, near_live)
            if j == 0:
                finish(k, j, dq_acc[k, j] + dq)
            else:
                dq_acc[k, j] = dq
            for u, terms in enumerate((dk, dv)):
                own_acc[u, k, j] += terms[:BLOCK]
                if j == 0:
                    prev_part[k, u] = terms[BLOCK:]
                else:
                    own_acc[u, k, j - 1] += terms[BLOCK:]
            return c

        lax.fori_loop(0, n_head, near_step, 0, unroll=2)

    def send_block(i, c):
        s = n_ctx - 1 - i
        outgoing[s] = kv_loc[want[s]]
        arr_copy(s).start()
        return c

    @pl.when(lends)
    def _():
        arrive(kv_loc.at[pl.ds(0, others * per)], kv_sem.at[1])
        lax.fori_loop(0, n_ctx - 2 - rank, send_block, 0)
        arrived[rank] = kv_loc[0]

        @pl.when(has_next)
        def _():
            prev_copy().start()

    @pl.when(rank >= n_ctx - 2)
    def _():
        arrived[rank] = kv_own[0, 0]

    for j in range(1, per):
        near(j)

    def arr_wait(o, c):
        arrive(arrived.at[o], arr_recv.at[o])
        return c

    @pl.when(rank > 0)
    def _():
        arr_wait(0, 0)

    def hub_copy(p):
        return remote(arrived.at[0], hub_kv.at[me], hub_sem.at[0], hub_sem.at[1], (rank, p))

    for d in far_first:
        hub_copy(peer(d)).start()
    hub_kv[me] = arrived[0]

    lax.fori_loop(1, rank - 1, arr_wait, 0)

    def far_copy(p):
        return remote(far_send.at[p], far_kv.at[me], far_sem.at[0], far_sem.at[1], (rank, p))

    def fill_far(buf, at, p):
        for i in range(here_far):
            buf[at, i] = arrived[owner[p * here_far + i]]

    for d in far_first:
        p = peer(d)
        fill_far(far_send, p, p)
        far_copy(p).start()
    fill_far(far_kv, me, me)

    arrive(hub_kv.at[pl.ds(0, others)], hub_sem.at[1])

    pairs = n_head // 2
    tens = [2 * i for i in range(1, pairs)]

    def hred_copy(d):
        slot = 0 if d == 1 else d // 2
        return remote(
            hub_part.at[peer(d)], hub_land.at[slot], hred_sem.at[0], hred_sem.at[1], (rank, peer(d))
        )

    def pair_copy(d):
        return remote(
            hub_part.at[peer(d + 1)],
            hub_pair.at[d // 2],
            pair_sem.at[0],
            pair_sem.at[1],
            (rank, peer(1)),
        )

    def hub_step(k):
        for j in range(per):
            kind = kind_tab[NEAR - 1, first + me * per + j]
            dq, dk, dv = grads(k, j, hub_kv[k], kind > 0)
            dq_acc[k, j] = dq if j == 0 else dq_acc[k, j] + dq
            for u, terms in enumerate((dk, dv)):
                if j == 0:
                    hub_part[k, u] = terms
                else:
                    hub_part[k, u] += terms

    for d in tens:
        hub_step(peer(d + 1))
        pair_copy(d).start()
    for d in tens + [1]:
        hub_step(peer(d))
    hred_copy(1).start()
    arrive(hub_pair.at[pl.ds(1, pairs - 1)], pair_sem.at[1])
    for d in tens:
        hub_part[peer(d)] += hub_pair[d // 2]
        hred_copy(d).start()
    hub_step(me)

    arrive(far_kv.at[pl.ds(0, others)], far_sem.at[1])

    def red_copy(c, k):
        return remote(
            far_part.at[k, c], far_land.at[me, c], red_send.at[0], red_recv.at[c], (rank, k)
        )

    def far_step(k):
        for j in range(per):
            total = dq_acc[k, j]
            for f in range(n_far):
                i = j * n_far + f
                kind = kind_tab[NEAR + f, first + me * per + j]
                dq, dk, dv = grads(k, j, far_kv[k, i], kind > 0)
                total += dq
                for u, terms in enumerate((dk, dv)):
                    for b in range(cuts):
                        far_part[k, u * cuts + b, i] = terms[b * piece : (b + 1) * piece]
            if j == 0:
                dq_acc[k, j] = total
            else:
                finish(k, j, total)

    for d in across:
        far_step(peer(d))
        red_copy(0, peer(d)).start()
    for c in range(1, chunks):
        for d in across:
            red_copy(c, peer(d)).start()
    far_step(peer(1))
    for c in range(chunks):
        red_copy(c, peer(1)).start()
    far_step(me)

    @pl.when(has_prev)
    def _():
        arrive(kv_prev, prev_sem.at[1])

    near(0)

    def back_copy():
        return remote(prev_part, prev_land, back_sem.at[0], back_sem.at[1], prev_dev)

    arrive(hub_land, hred_sem.at[1])
    hub_sum[...] = sum((hub_land[i] for i in range(pairs)), hub_part[me])

    def tree_copy(i):
        return remote(
            hub_sum, hub_tree.at[i], tree_send.at[0], tree_recv.at[i], (rank - 2**i, me)
        )

    def tree_up(i):
        @pl.when(lax.rem(rank, 2 ** (i + 1)) == 2**i)
        def _():
            tree_copy(i).start()

    def tree_take(i):
        @pl.when((lax.rem(rank, 2 ** (i + 1)) == 0) & (rank + 2**i < n_ctx))
        def _():
            arrive(hub_tree.at[i], tree_recv.at[i])
            hub_sum[...] += hub_tree[i]

    tree_up(0)

    def ret_copy(c, o):
        return remote(part.at[o, c], ret.at[c, rank], ret_send.at[o], ret_recv.at[c, rank], (o, me))

    sources = [(peer(d), far_land) for d in range(1, n_head)] + [(me, far_part)]
    for c in range(chunks):
        arrive(far_land.at[pl.ds(0, others), c], red_recv.at[c])

        def send_part(o, carry):
            terms = jnp.zeros((piece, width), f32)
            for p, buf in sources:
                for i in range(here_far):
                    mine = owner[p * here_far + i] == o
                    terms += jnp.where(mine, buf[p, c, i], 0.0)
            part[o, c] = terms
            ret_copy(c, o).start()
            return carry

        lax.fori_loop(1, rank - 1, send_part, 0)
        if c == cuts - 1:
            tree_take(0)
            if stages > 1:
                tree_up(1)

    @pl.when(has_prev)
    def _():
        back_copy().start()

    for i in range(1, stages):
        tree_take(i)
        if i + 1 < stages:
            tree_up(i + 1)

    def last_copy():
        return remote(hub_sum, hub_last.at[me], last_sem.at[0], last_sem.at[1], (rank, 0))

    @pl.when((rank == 0) & (me > 0))
    def _():
        last_copy().start()

    def blk_copy(c, p):
        return remote(
            blk_part.at[p, c], blk_land.at[me, c], blk_send.at[0], blk_recv.at[c], (rank, p)
        )

    @pl.when(lends)
    def _():
        blk_part[...] = jnp.zeros_like(blk_part)
        for c in range(chunks):

            def take_part(s, carry):
                arrive(ret.at[c, s], ret_recv.at[c, s])
                for i in range(blocks):
                    blk_part[i // per, c, i % per] += jnp.where(want[s] == i, ret[c, s], 0.0)
                return carry

            lax.fori_loop(rank + 2, n_ctx, take_part, 0)
            for d in far_first:
                blk_copy(c, peer(d)).start()

    @pl.when(has_next)
    def _():
        arrive(prev_land, back_sem.at[1])
        for k in range(n_head):
            for u in range(2):
                own_acc[u, k, per - 1] += prev_land[k, u]

    @pl.when((rank == 0) & (me == 0))
    def _():
        for u in range(2):
            own_acc[u, 0, 0] += hub_sum[u]
        arrive(hub_last.at[pl.ds(0, others)], last_sem.at[1])
        for k in range(1, n_head):
            for u in range(2):
                own_acc[u, k, 0] += hub_last[k, u]

    @pl.when(lends)
    def _():
        for c in range(chunks):
            u, at = c // cuts, pl.ds(c % cuts * piece, piece)
            own_acc[u, me, :, at] += blk_part[me, c]
            arrive(blk_land.at[pl.ds(0, others), c], blk_recv.at[c])
            for d in range(1, n_head):
                own_acc[u, peer(d), :, at] += blk_land[peer(d), c]

    for u, out in ((0, dk_out), (1, dv_out)):
        for h in range(n_head):
            terms = own_acc[u, h].reshape(rows, width)
            wide[pl.ds(h, rows, stride=n_head), :] = terms * scale if u == 0 else terms
        out[...] = wide[...].astype(bf16)

    def sent_block(s, c):
        arr_copy(s).wait_send()
        return c

    lax.fori_loop(jnp.where(rank == 0, 1, rank + 2), n_ctx, sent_block, 0)

    def sent_part(o, c):
        arrive(part.at[o], ret_send.at[o])
        return c

    lax.fori_loop(1, rank - 1, sent_part, 0)
    arrive(stat_land.at[:, pl.ds(0, others)], stat_sem.at[0])
    arrive(hub_kv.at[pl.ds(0, others)], hub_sem.at[0])
    arrive(far_kv.at[pl.ds(0, others)], far_sem.at[0])
    arrive(hub_land, hred_sem.at[0])
    arrive(hub_pair.at[pl.ds(1, pairs - 1)], pair_sem.at[0])
    arrive(far_land.at[pl.ds(0, others)], red_send.at[0])

    @pl.when((rank == 0) & (me == 0))
    def _():
        arrive(kv_loc.at[pl.ds(0, others)], kv_sem.at[0])

    @pl.when(lends)
    def _():
        arrive(kv_loc.at[pl.ds(0, others * per)], kv_sem.at[0])
        arrive(blk_land.at[pl.ds(0, others)], blk_send.at[0])

    @pl.when(rank > 0)
    def _():
        arrive(hub_sum, tree_send.at[0])

    @pl.when((rank == 0) & (me > 0))
    def _():
        arrive(hub_sum, last_sem.at[0])

    @pl.when(has_next)
    def _():
        prev_copy().wait_send()

    @pl.when(has_prev)
    def _():
        back_copy().wait_send()

    arrive(dq_buf, dq_sem.at[0])


def tail(dq_in, dk_in, dv_in, dq_out, dk_out, dv_out, dq_held, dk_held, dv_held, loads, stores):
    pieces = loads.shape[0] - 2
    step = dq_held.shape[0] // pieces
    parts = [pl.ds(k * step, step) for k in range(pieces)]
    routes = [(dq_in.at[at], dq_held.at[at], dq_out.at[at]) for at in parts]
    routes += [(dk_in, dk_held, dk_out), (dv_in, dv_held, dv_out)]
    for k, (source, held, _) in enumerate(routes):
        pltpu.make_async_copy(source, held, loads.at[k]).start()
    for k, (source, held, target) in enumerate(routes):
        pltpu.make_async_copy(source, held, loads.at[k]).wait()
        pltpu.make_async_copy(held, target, stores.at[k]).start()
    for k, (_, held, target) in enumerate(routes):
        pltpu.make_async_copy(held, target, stores.at[k]).wait()


def shards(
    n_ctx,
    n_head,
    queries,
    key_states,
    value_states,
    out_grad,
    log_sums,
    row_deltas,
    block_pairs,
    pair_kinds,
):
    rows, all_heads, width = queries.shape
    heads = all_heads // n_head
    n_slot = block_pairs.shape[1]
    n_far = n_slot - NEAR
    per = rows // BLOCK
    blocks = per * n_head
    lanes = BLOCK * heads
    n_far_here = per * n_far
    stages = (n_ctx - 1).bit_length()
    bf16, f32 = jnp.bfloat16, jnp.float32
    flat = (rows * n_head, width)
    kv = (BLOCK, 2 * width)
    term = (BLOCK, width)
    piece = (BLOCK // CUTS, width)
    chunks = 2 * CUTS
    vmem = pl.BlockSpec(memory_space=pltpu.VMEM)
    smem = pl.BlockSpec(memory_space=pltpu.SMEM)
    anywhere = pl.BlockSpec(memory_space=pl.ANY)
    dma = pltpu.SemaphoreType.DMA
    raw = pltpu.VMEM((n_head, per, BLOCK, heads, width), bf16)
    rolled = pltpu.VMEM((n_head, per, lanes, width), bf16)
    dq, dk, dv = pl.pallas_call(
        partial(kernel, n_ctx, n_head, n_slot),
        out_shape=(
            jax.ShapeDtypeStruct(queries.shape, bf16),
            jax.ShapeDtypeStruct(flat, bf16),
            jax.ShapeDtypeStruct(flat, bf16),
        ),
        in_specs=[smem, smem, anywhere, anywhere, vmem, vmem, vmem, vmem],
        out_specs=(anywhere, vmem, vmem),
        scratch_shapes=[
            pltpu.VMEM(flat, f32),
            pltpu.VMEM((n_head, per) + kv, bf16),
            pltpu.VMEM((blocks,) + kv, bf16),
            pltpu.VMEM((n_head,) + kv, bf16),
            pltpu.VMEM((n_ctx,) + kv, bf16),
            pltpu.VMEM((n_ctx,) + kv, bf16),
            pltpu.VMEM((n_head, n_far_here) + kv, bf16),
            pltpu.VMEM((n_head, n_far_here) + kv, bf16),
            pltpu.VMEM((n_head,) + kv, bf16),
            raw,
            raw,
            rolled,
            rolled,
            pltpu.VMEM((2, n_head, heads, rows), f32),
            pltpu.VMEM((per, 2 * n_head, lanes), f32),
            pltpu.VMEM((n_head, per, lanes, width), f32),
            raw,
            pltpu.VMEM((2, n_head, per) + term, f32),
            pltpu.VMEM((n_head, 2) + term, f32),
            pltpu.VMEM((n_head, 2) + term, f32),
            pltpu.VMEM((n_head, chunks, n_far_here) + piece, f32),
            pltpu.VMEM((n_head, chunks, n_far_here) + piece, f32),
            pltpu.VMEM((n_head, 2) + term, f32),
            pltpu.VMEM((n_head // 2, 2) + term, f32),
            pltpu.VMEM((n_head // 2, 2) + term, f32),
            pltpu.VMEM((2,) + term, f32),
            pltpu.VMEM((stages, 2) + term, f32),
            pltpu.VMEM((n_head, 2) + term, f32),
            pltpu.VMEM((n_ctx, chunks) + piece, f32),
            pltpu.VMEM((chunks, n_ctx) + piece, f32),
            pltpu.VMEM((n_head, chunks, per) + piece, f32),
            pltpu.VMEM((n_head, chunks, per) + piece, f32),
            pltpu.SMEM((n_ctx,), jnp.int32),
            pltpu.SMEM((blocks * n_far,), jnp.int32),
            dma((2,)),
            dma((2,)),
            dma((2,)),
            dma((2,)),
            dma((n_ctx,)),
            dma((n_ctx,)),
            dma((2,)),
            dma((2,)),
            dma((1,)),
            dma((2,)),
            dma((2,)),
            dma((2,)),
            dma((1,)),
            dma((stages,)),
            dma((2,)),
            dma((1,)),
            dma((chunks,)),
            dma((n_ctx,)),
            dma((chunks, n_ctx)),
            dma((1,)),
            dma((chunks,)),
        ],
        compiler_params=pltpu.CompilerParams(
            collective_id=0, has_side_effects=True, vmem_limit_bytes=60 * 1024 * 1024
        ),
    )(
        block_pairs.T,
        pair_kinds.T,
        queries,
        out_grad,
        key_states.reshape(flat),
        value_states.reshape(flat),
        log_sums,
        row_deltas,
    )
    dq, dk, dv = pl.pallas_call(
        tail,
        out_shape=(
            jax.ShapeDtypeStruct(queries.shape, bf16),
            jax.ShapeDtypeStruct(flat, bf16),
            jax.ShapeDtypeStruct(flat, bf16),
        ),
        in_specs=[anywhere] * 3,
        out_specs=(anywhere,) * 3,
        scratch_shapes=[
            pltpu.VMEM(queries.shape, bf16),
            pltpu.VMEM(flat, bf16),
            pltpu.VMEM(flat, bf16),
            dma((6,)),
            dma((6,)),
        ],
    )(dq, dk, dv)
    return dq, dk.reshape(key_states.shape), dv.reshape(value_states.shape)


def solution(mesh):
    tokens = P(("ctx", "head"), None, None)
    stats = P("head", "ctx")
    return jax.shard_map(
        partial(shards, mesh.shape["ctx"], mesh.shape["head"]),
        mesh=mesh,
        in_specs=(tokens, tokens, tokens, tokens, stats, stats, P(), P()),
        out_specs=(tokens, tokens, tokens),
        check_vma=False,
    )
```

```python
from functools import partial

import jax
import jax.numpy as jnp
from jax import lax
from jax.experimental import pallas as pl
from jax.experimental.pallas import tpu as pltpu
from jax.sharding import PartitionSpec as P

BLOCK = 64
NEAR = 3
CUTS = 2
MESH = pl.DeviceIdType.MESH
NT = (((1,), (1,)), ((), ()))
TN = (((0,), (0,)), ((), ()))


def tile_grads(keys, values, q, g, log_row, delta_row, live, scale):
    scores = lax.dot_general(keys, q, NT, preferred_element_type=jnp.float32) * scale
    weights = jnp.where(live, jnp.exp(scores - log_row), 0.0)
    prob_grad = lax.dot_general(values, g, NT, preferred_element_type=jnp.float32)
    dscore = (weights * (prob_grad - delta_row)).astype(jnp.bfloat16)
    dv = jnp.dot(weights.astype(jnp.bfloat16), g, preferred_element_type=jnp.float32)
    dk = jnp.dot(dscore, q, preferred_element_type=jnp.float32)
    dq = lax.dot_general(dscore, keys, TN, preferred_element_type=jnp.float32)
    return dq, dk, dv


def kernel(
    n_ctx,
    n_head,
    n_slot,
    pair_tab,
    kind_tab,
    q_hbm,
    g_hbm,
    k_ref,
    v_ref,
    log_ref,
    delta_ref,
    dq_out,
    dk_out,
    dv_out,
    wide,
    kv_own,
    k_loc,
    v_loc,
    kv_prev,
    outgoing,
    k_arrived,
    v_arrived,
    far_send,
    far_kv,
    hub_kv,
    q_raw,
    g_raw,
    q_flat,
    g_flat,
    stat_land,
    stat_rows,
    dq_acc,
    dq_buf,
    own_acc,
    prev_part,
    prev_land,
    far_part,
    far_land,
    hub_part,
    hub_land,
    hub_pair,
    hub_sum,
    hub_tree,
    hub_last,
    part,
    ret,
    blk_part,
    blk_land,
    want,
    owner,
    load_sem,
    kv_sem,
    stat_sem,
    prev_sem,
    arr_send,
    arr_recv,
    far_sem,
    hub_sem,
    dq_sem,
    back_sem,
    hred_sem,
    pair_sem,
    tree_send,
    tree_recv,
    last_sem,
    red_send,
    red_recv,
    ret_send,
    ret_recv,
    blk_send,
    blk_recv,
    ready,
):
    kv_loc, arrived = (k_loc, v_loc), (k_arrived, v_arrived)
    rank = lax.axis_index("ctx")
    me = lax.axis_index("head")
    rows = q_hbm.shape[0]
    width = q_hbm.shape[2]
    heads = q_hbm.shape[1] // n_head
    per = rows // BLOCK
    blocks = per * n_head
    lanes = BLOCK * heads
    n_far = n_slot - NEAR
    here_far = per * n_far
    chunks, piece = part.shape[1], part.shape[2]
    cuts = BLOCK // piece
    others = n_head - 1
    scale = width ** (-0.5)
    first = rank * blocks
    bf16, f32 = jnp.bfloat16, jnp.float32

    def peer(d):
        return lax.rem(me // 2 + d // 2, n_head // 2) * 2 + lax.rem(
            lax.rem(me, 2) + lax.rem(d, 2), 2
        )

    def arrive(ref, sem):
        pltpu.make_async_copy(ref, ref, sem).wait()

    def remote(source, target, send, recv, device):
        return pltpu.make_async_remote_copy(
            src_ref=source,
            dst_ref=target,
            send_sem=send,
            recv_sem=recv,
            device_id=device,
            device_id_type=MESH,
        )

    far_first = list(range(2, n_head)) + [1]
    across = far_first[:-1]
    has_prev = (rank > 0) | (me > 0)
    has_next = (rank < n_ctx - 1) | (me < n_head - 1)
    prev_dev = (jnp.where(me > 0, rank, rank - 1), jnp.where(me > 0, me - 1, n_head - 1))
    next_dev = (
        jnp.where(me < n_head - 1, rank, rank + 1),
        jnp.where(me < n_head - 1, me + 1, 0),
    )
    outer_prev = (me == 0) & (rank > 0)
    outer_next = (me == n_head - 1) & (rank < n_ctx - 1)
    lends = (rank > 0) & (rank < n_ctx - 2)

    barrier = pltpu.get_barrier_semaphore()
    for d in range(1, n_head):
        pl.semaphore_signal(barrier, inc=1, device_id=(rank, peer(d)), device_id_type=MESH)

    def greet(s, c):
        pl.semaphore_signal(barrier, inc=1, device_id=(s, me), device_id_type=MESH)
        return c

    lax.fori_loop(rank + 1, n_ctx, greet, 0)

    @pl.when(outer_next)
    def _():
        pl.semaphore_signal(barrier, inc=1, device_id=next_dev, device_id_type=MESH)

    for u, (source, raw) in enumerate(((q_hbm, q_raw), (g_hbm, g_raw))):
        for k in range(n_head):
            for j in range(per):
                pltpu.make_async_copy(
                    source.at[pl.ds(j * BLOCK, BLOCK), pl.ds(k * heads, heads)],
                    raw.at[k, j],
                    load_sem.at[u],
                ).start()

    def wanted_by(s, c):
        best = jnp.int32(0)
        for i in range(blocks):
            at = s * blocks + i
            for j in range(NEAR, n_slot):
                local = pair_tab[j, at] - first
                named = (kind_tab[j, at] > 0) & (local >= 0) & (local < blocks)
                best = jnp.where(named, jnp.maximum(best, local), best)
        want[s] = best
        return c

    @pl.when(lends)
    def _():
        lax.fori_loop(rank + 2, n_ctx, wanted_by, 0)

    for i in range(blocks):
        for f in range(n_far):
            at = first + i
            owner[i * n_far + f] = jnp.where(
                kind_tab[NEAR + f, at] > 0, lax.div(pair_tab[NEAR + f, at], blocks), rank
            )

    @pl.when(jnp.logical_not(has_prev))
    def _():
        kv_prev[...] = jnp.zeros_like(kv_prev)

    for at, source in enumerate((k_ref, v_ref)):
        wide[...] = source[...].astype(f32)
        for h in range(n_head):
            head_rows = wide[pl.ds(h, rows, stride=n_head), :]
            kv_own[at, h] = head_rows.reshape(per, BLOCK, width).astype(bf16)

    pl.semaphore_wait(barrier, others + rank + outer_prev.astype(jnp.int32))

    def answer(o, c):
        pl.semaphore_signal(ready, inc=1, device_id=(o, me), device_id_type=MESH)
        return c

    lax.fori_loop(0, rank, answer, 0)

    @pl.when(outer_prev)
    def _():
        pl.semaphore_signal(ready, inc=1, device_id=prev_dev, device_id_type=MESH)

    def await_ready():
        @pl.when(rank < n_ctx - 1)
        def _():
            pl.semaphore_wait(ready, n_ctx - 1 - rank + outer_next.astype(jnp.int32))

    def kv_copy(a, p):
        return remote(
            kv_own.at[a, p],
            kv_loc[a].at[pl.ds(me * per, per)],
            kv_sem.at[0],
            kv_sem.at[1 + a],
            (rank, p),
        )

    def first_copy(a, p):
        return remote(
            kv_own.at[a, p, 0], kv_loc[a].at[0], kv_sem.at[0], kv_sem.at[1 + a], (rank, p)
        )

    def stat_copy(u, p):
        return remote(
            (log_ref, delta_ref)[u].at[:, pl.ds(pl.multiple_of(p * rows, rows), rows)],
            stat_land.at[u, me],
            stat_sem.at[0],
            stat_sem.at[1],
            (rank, p),
        )

    def prev_copy():
        return remote(
            kv_own.at[:, :, per - 1], kv_prev, prev_sem.at[0], prev_sem.at[1], next_dev
        )

    @pl.when((rank == 0) & (me == 0))
    def _():
        for a in range(2):
            for d in far_first:
                first_copy(a, peer(d)).start()
            kv_loc[a][0] = kv_own[a, 0, 0]

    for u in range(2):
        for d in far_first:
            stat_copy(u, peer(d)).start()

    @pl.when(lends)
    def _():
        for a in range(2):
            for d in far_first:
                kv_copy(a, peer(d)).start()
        for a in range(2):
            kv_loc[a][pl.ds(me * per, per)] = kv_own[a, me]

    for u, source in enumerate((log_ref, delta_ref)):
        stat_land[u, me] = source[:, pl.ds(pl.multiple_of(me * rows, rows), rows)]

    def arr_copy(a, s):
        return remote(
            outgoing.at[a, s], arrived[a].at[rank], arr_send.at[s], arr_recv.at[a, rank], (s, me)
        )

    @pl.when(rank == 0)
    def _():
        @pl.when(me > 0)
        def _():
            for a in range(2):
                arrive(kv_loc[a].at[0], kv_sem.at[1 + a])

        await_ready()

        def send_first(i, c):
            s = n_ctx - 1 - i
            for a in range(2):
                outgoing[a, s] = kv_loc[a][0]
                arr_copy(a, s).start()
            return c

        lax.fori_loop(0, n_ctx - 1, send_first, 0)
        for a in range(2):
            arrived[a][0] = kv_loc[a][0]
        prev_copy().start()

    arrive(stat_land.at[:, pl.ds(0, others)], stat_sem.at[1])
    spread = (
        lax.broadcasted_iota(jnp.int32, (BLOCK, lanes), 1) // heads
        == lax.broadcasted_iota(jnp.int32, (BLOCK, lanes), 0)
    ).astype(bf16)
    own_row = lax.broadcasted_iota(jnp.int32, (heads, lanes), 1) % heads == lax.broadcasted_iota(
        jnp.int32, (heads, lanes), 0
    )
    stats = stat_land[...].reshape(2 * n_head * heads, rows)
    high = stats.astype(bf16)
    rest = stats - high.astype(f32)
    mid = rest.astype(bf16)
    low = (rest - mid.astype(f32)).astype(bf16)
    for j in range(per):
        at = slice(j * BLOCK, (j + 1) * BLOCK)
        by_lane = sum(
            jnp.dot(part_of[:, at], spread, preferred_element_type=f32)
            for part_of in (high, mid, low)
        ).reshape(2 * n_head, heads, lanes)
        stat_rows[j] = jnp.sum(jnp.where(own_row[None], by_lane, 0.0), axis=1)

    key_row = lax.broadcasted_iota(jnp.int32, (2 * BLOCK, lanes), 0)
    causal = (key_row >= BLOCK) | (
        key_row <= lax.broadcasted_iota(jnp.int32, (2 * BLOCK, lanes), 1) // heads
    )
    pair_row = lax.broadcasted_iota(jnp.int32, (2 * BLOCK, 1), 0)

    def grads(k, j, keys, values, live):
        return tile_grads(
            keys,
            values,
            q_flat[k, j],
            g_flat[k, j],
            stat_rows[j, pl.ds(k, 1)],
            stat_rows[j, pl.ds(n_head + k, 1)],
            live,
            scale,
        )

    def dq_copy(k, j):
        return pltpu.make_async_copy(
            dq_buf.at[k, j],
            dq_out.at[
                pl.ds(j * BLOCK, BLOCK), pl.ds(pl.multiple_of(k * heads, heads), heads)
            ],
            dq_sem.at[0],
        )

    def finish(k, j, total):
        dq_buf[k, j] = (total * scale).reshape(BLOCK, heads, width).astype(bf16)
        dq_copy(k, j).start()

    arrive(q_raw, load_sem.at[0])
    arrive(g_raw, load_sem.at[1])

    def flatten(t, c):
        k, j = t // per, lax.rem(t, per)
        for raw, flat in ((q_raw, q_flat), (g_raw, g_flat)):
            flat[k, j] = raw[k, j].astype(f32).reshape(lanes, width).astype(bf16)
        return c

    lax.fori_loop(0, n_head * per, flatten, 0)

    own_acc[...] = jnp.zeros_like(own_acc)
    dq_acc[:, 0] = jnp.zeros((n_head, lanes, width), f32)

    def near(j, lo, hi):
        prev_kind = kind_tab[1, first + me * per + j]
        near_live = causal & (jnp.where(pair_row < BLOCK, 1, prev_kind) > 0)

        def near_step(k, c):
            keys, values = (
                jnp.concatenate(
                    [kv_own[a, k, j], kv_prev[a, k] if j == 0 else kv_own[a, k, j - 1]], axis=0
                )
                for a in range(2)
            )
            dq, dk, dv = grads(k, j, keys, values, near_live)
            if j == 0:
                finish(k, 0, dq_acc[k, 0] + dq)
                for other in range(1, per):
                    finish(k, other, dq_acc[k, other])
            else:
                dq_acc[k, j] = dq
            for u, terms in enumerate((dk, dv)):
                own_acc[u, k, j] += terms[:BLOCK]
                if j == 0:
                    prev_part[k, u] = terms[BLOCK:]
                else:
                    own_acc[u, k, j - 1] += terms[BLOCK:]
            return c

        lax.fori_loop(lo, hi, near_step, 0, unroll=2)

    half = n_head // 2

    def send_block(a):
        def send(i, c):
            s = n_ctx - 1 - i
            outgoing[a, s] = kv_loc[a][want[s]]
            arr_copy(a, s).start()
            return c

        lax.fori_loop(0, n_ctx - 2 - rank, send, 0)

    def lend(a):
        @pl.when(lends)
        def _():
            arrive(kv_loc[a].at[pl.ds(0, others * per)], kv_sem.at[1 + a])
            if a == 0:
                await_ready()
            send_block(a)
            arrived[a][rank] = kv_loc[a][0]
            if a == 1:
                prev_copy().start()

    lend(0)

    @pl.when(rank >= n_ctx - 2)
    def _():
        await_ready()
        for a in range(2):
            arrived[a][rank] = kv_own[a, 0, 0]

        @pl.when(has_next)
        def _():
            prev_copy().start()

    for j in range(1, per):
        near(j, 0, half)
    lend(1)
    for j in range(1, per):
        near(j, half, n_head)

    @pl.when(rank > 0)
    def _():
        for a in range(2):
            arrive(arrived[a].at[0], arr_recv.at[a, 0])

    for a in range(2):
        for d in far_first:
            remote(
                arrived[a].at[0], hub_kv.at[a, me], hub_sem.at[0], hub_sem.at[1], (rank, peer(d))
            ).start()
        hub_kv[a, me] = arrived[a][0]

    def far_copy(a, d):
        return remote(
            far_send.at[a, peer(d)],
            far_kv.at[a, me],
            far_sem.at[0],
            far_sem.at[1 if d == 1 else 2 + a],
            (rank, peer(d)),
        )

    def fill_far(buf, a, p):
        for i in range(here_far):
            buf[a, p, i] = arrived[a][owner[p * here_far + i]]

    for a in range(2):

        def arr_wait(o, c):
            arrive(arrived[a].at[o], arr_recv.at[a, o])
            return c

        lax.fori_loop(1, rank - 1, arr_wait, 0)
        for d in far_first:
            fill_far(far_send, a, peer(d))
            far_copy(a, d).start()
        fill_far(far_kv, a, me)

    def red_copy(c, k):
        return remote(
            far_part.at[k, c], far_land.at[me, c], red_send.at[0], red_recv.at[c], (rank, k)
        )

    def far_step(k):
        for j in range(per):
            total = dq_acc[k, j]
            for f in range(n_far):
                i = j * n_far + f
                kind = kind_tab[NEAR + f, first + me * per + j]
                dq, dk, dv = grads(k, j, far_kv[0, k, i], far_kv[1, k, i], kind > 0)
                total += dq
                for u, terms in enumerate((dk, dv)):
                    for b in range(cuts):
                        far_part[k, u * cuts + b, i] = terms[b * piece : (b + 1) * piece]
            dq_acc[k, j] = total

    far_step(me)
    arrive(far_kv.at[:, 0], far_sem.at[1])
    far_step(peer(1))
    for c in range(chunks):
        red_copy(c, peer(1)).start()

    arrive(hub_kv.at[:, pl.ds(0, others)], hub_sem.at[1])

    pairs = n_head // 2
    tens = [2 * i for i in range(1, pairs)]

    def hred_copy(d):
        slot = 0 if d == 1 else d // 2
        return remote(
            hub_part.at[peer(d)], hub_land.at[slot], hred_sem.at[0], hred_sem.at[1], (rank, peer(d))
        )

    def pair_copy(d):
        return remote(
            hub_part.at[peer(d + 1)],
            hub_pair.at[d // 2],
            pair_sem.at[0],
            pair_sem.at[1],
            (rank, peer(1)),
        )

    def hub_step(k):
        for j in range(per):
            kind = kind_tab[NEAR - 1, first + me * per + j]
            dq, dk, dv = grads(k, j, hub_kv[0, k], hub_kv[1, k], kind > 0)
            dq_acc[k, j] += dq
            for u, terms in enumerate((dk, dv)):
                if j == 0:
                    hub_part[k, u] = terms
                else:
                    hub_part[k, u] += terms

    for d in tens:
        hub_step(peer(d + 1))
        pair_copy(d).start()
    for d in tens:
        hub_step(peer(d))
    arrive(hub_pair.at[pl.ds(1, pairs - 1)], pair_sem.at[1])
    for d in tens:
        hub_part[peer(d)] += hub_pair[d // 2]
        hred_copy(d).start()

    for a in range(2):
        arrive(far_kv.at[a, pl.ds(0, others - 1)], far_sem.at[2 + a])

    for d in across:
        far_step(peer(d))
        red_copy(0, peer(d)).start()
    for c in range(1, chunks):
        for d in across:
            red_copy(c, peer(d)).start()

    hub_step(peer(1))
    hred_copy(1).start()
    hub_step(me)

    def tree_copy():
        odd = lax.rem(rank, 2)
        slot = jnp.where(odd == 1, 0, rank // 2)
        return remote(
            hub_sum,
            hub_tree.at[slot],
            tree_send.at[0],
            tree_recv.at[slot],
            (jnp.where(odd == 1, rank - 1, 0), me),
        )

    def tree_take(i, c):
        arrive(hub_tree.at[i], tree_recv.at[i])
        hub_sum[...] += hub_tree[i]
        return c

    def ret_copy(c, o):
        return remote(part.at[o, c], ret.at[c, rank], ret_send.at[o], ret_recv.at[c, rank], (o, me))

    sources = [(peer(d), far_land) for d in range(1, n_head)] + [(me, far_part)]

    def reduce(c):
        arrive(far_land.at[pl.ds(0, others), c], red_recv.at[c])

        def send_part(o, carry):
            terms = jnp.zeros((piece, width), f32)
            for p, buf in sources:
                for i in range(here_far):
                    mine = owner[p * here_far + i] == o
                    terms += jnp.where(mine, buf[p, c, i], 0.0)
            part[o, c] = terms
            ret_copy(c, o).start()
            return carry

        lax.fori_loop(1, rank - 1, send_part, 0)

    def back_copy():
        return remote(prev_part, prev_land, back_sem.at[0], back_sem.at[1], prev_dev)

    @pl.when(has_prev)
    def _():
        arrive(kv_prev, prev_sem.at[1])

    reduce(0)
    arrive(hub_land, hred_sem.at[1])
    hub_sum[...] = sum((hub_land[i] for i in range(pairs)), hub_part[me])

    @pl.when(lax.rem(rank, 2) == 1)
    def _():
        tree_copy().start()

    near(0, 0, half)
    reduce(1)
    near(0, half, n_head)
    for c in range(2, min(3, chunks)):
        reduce(c)
    @pl.when((lax.rem(rank, 2) == 0) & (rank + 1 < n_ctx))
    def _():
        tree_take(0, 0)

        @pl.when(rank > 0)
        def _():
            tree_copy().start()

    for c in range(3, chunks):
        reduce(c)

    @pl.when(has_prev)
    def _():
        back_copy().start()

    @pl.when(rank == 0)
    def _():
        lax.fori_loop(1, (n_ctx + 1) // 2, tree_take, 0)

    def last_copy():
        return remote(hub_sum, hub_last.at[me], last_sem.at[0], last_sem.at[1], (rank, 0))

    @pl.when((rank == 0) & (me > 0))
    def _():
        last_copy().start()

    def blk_copy(c, p):
        return remote(
            blk_part.at[p, c], blk_land.at[me, c], blk_send.at[0], blk_recv.at[c], (rank, p)
        )

    @pl.when(lends)
    def _():
        blk_part[...] = jnp.zeros_like(blk_part)
        for c in range(chunks):

            def take_part(s, carry):
                arrive(ret.at[c, s], ret_recv.at[c, s])
                for i in range(blocks):
                    blk_part[i // per, c, i % per] += jnp.where(want[s] == i, ret[c, s], 0.0)
                return carry

            lax.fori_loop(rank + 2, n_ctx, take_part, 0)
            for d in far_first:
                blk_copy(c, peer(d)).start()

    @pl.when(has_next)
    def _():
        arrive(prev_land, back_sem.at[1])
        for k in range(n_head):
            for u in range(2):
                own_acc[u, k, per - 1] += prev_land[k, u]

    @pl.when((rank == 0) & (me == 0))
    def _():
        for u in range(2):
            own_acc[u, 0, 0] += hub_sum[u]
        arrive(hub_last.at[pl.ds(0, others)], last_sem.at[1])
        for k in range(1, n_head):
            for u in range(2):
                own_acc[u, k, 0] += hub_last[k, u]

    @pl.when(lends)
    def _():
        for c in range(chunks):
            u, at = c // cuts, pl.ds(c % cuts * piece, piece)
            own_acc[u, me, :, at] += blk_part[me, c]
            arrive(blk_land.at[pl.ds(0, others), c], blk_recv.at[c])
            for d in range(1, n_head):
                own_acc[u, peer(d), :, at] += blk_land[peer(d), c]

    for u, out in ((0, dk_out), (1, dv_out)):
        for h in range(n_head):
            terms = own_acc[u, h].reshape(rows, width)
            wide[pl.ds(h, rows, stride=n_head), :] = terms * scale if u == 0 else terms
        out[...] = wide[...].astype(bf16)

    def sent_block(s, c):
        arrive(outgoing.at[:, s], arr_send.at[s])
        return c

    lax.fori_loop(jnp.where(rank == 0, 1, rank + 2), n_ctx, sent_block, 0)

    def sent_part(o, c):
        arrive(part.at[o], ret_send.at[o])
        return c

    lax.fori_loop(1, rank - 1, sent_part, 0)
    arrive(stat_land.at[:, pl.ds(0, others)], stat_sem.at[0])
    arrive(hub_kv.at[:, pl.ds(0, others)], hub_sem.at[0])
    arrive(far_kv.at[:, pl.ds(0, others)], far_sem.at[0])
    arrive(hub_land, hred_sem.at[0])
    arrive(hub_pair.at[pl.ds(1, pairs - 1)], pair_sem.at[0])
    arrive(far_land.at[pl.ds(0, others)], red_send.at[0])

    @pl.when((rank == 0) & (me == 0))
    def _():
        arrive(hub_kv.at[:, pl.ds(0, others)], kv_sem.at[0])

    @pl.when(lends)
    def _():
        arrive(kv_own.at[:, pl.ds(0, others)], kv_sem.at[0])
        arrive(blk_land.at[pl.ds(0, others)], blk_send.at[0])

    @pl.when(rank > 0)
    def _():
        arrive(hub_sum, tree_send.at[0])

    @pl.when((rank == 0) & (me > 0))
    def _():
        arrive(hub_sum, last_sem.at[0])

    @pl.when(has_next)
    def _():
        prev_copy().wait_send()

    @pl.when(has_prev)
    def _():
        back_copy().wait_send()

    arrive(dq_buf, dq_sem.at[0])


def tail(dq_in, dk_in, dv_in, dq_out, dk_out, dv_out, dq_held, dk_held, dv_held, loads, stores):
    pieces = loads.shape[0] - 2
    step = dq_held.shape[0] // pieces
    parts = [pl.ds(k * step, step) for k in range(pieces)]
    routes = [(dq_in.at[at], dq_held.at[at], dq_out.at[at]) for at in parts]
    routes += [(dk_in, dk_held, dk_out), (dv_in, dv_held, dv_out)]
    for k, (source, held, _) in enumerate(routes):
        pltpu.make_async_copy(source, held, loads.at[k]).start()
    for k, (source, held, target) in enumerate(routes):
        pltpu.make_async_copy(source, held, loads.at[k]).wait()
        pltpu.make_async_copy(held, target, stores.at[k]).start()
    for k, (_, held, target) in enumerate(routes):
        pltpu.make_async_copy(held, target, stores.at[k]).wait()


def shards(
    n_ctx,
    n_head,
    queries,
    key_states,
    value_states,
    out_grad,
    log_sums,
    row_deltas,
    block_pairs,
    pair_kinds,
):
    rows, all_heads, width = queries.shape
    heads = all_heads // n_head
    n_slot = block_pairs.shape[1]
    n_far = n_slot - NEAR
    per = rows // BLOCK
    blocks = per * n_head
    lanes = BLOCK * heads
    n_far_here = per * n_far
    bf16, f32 = jnp.bfloat16, jnp.float32
    flat = (rows * n_head, width)
    term = (BLOCK, width)
    piece = (BLOCK // CUTS, width)
    chunks = 2 * CUTS
    vmem = pl.BlockSpec(memory_space=pltpu.VMEM)
    smem = pl.BlockSpec(memory_space=pltpu.SMEM)
    anywhere = pl.BlockSpec(memory_space=pl.ANY)
    dma = pltpu.SemaphoreType.DMA
    raw = pltpu.VMEM((n_head, per, BLOCK, heads, width), bf16)
    rolled = pltpu.VMEM((n_head, per, lanes, width), bf16)
    dq, dk, dv = pl.pallas_call(
        partial(kernel, n_ctx, n_head, n_slot),
        out_shape=(
            jax.ShapeDtypeStruct(queries.shape, bf16),
            jax.ShapeDtypeStruct(flat, bf16),
            jax.ShapeDtypeStruct(flat, bf16),
        ),
        in_specs=[smem, smem, anywhere, anywhere, vmem, vmem, vmem, vmem],
        out_specs=(anywhere, vmem, vmem),
        scratch_shapes=[
            pltpu.VMEM(flat, f32),
            pltpu.VMEM((2, n_head, per) + term, bf16),
            pltpu.VMEM((blocks,) + term, bf16),
            pltpu.VMEM((blocks,) + term, bf16),
            pltpu.VMEM((2, n_head) + term, bf16),
            pltpu.VMEM((2, n_ctx) + term, bf16),
            pltpu.VMEM((n_ctx,) + term, bf16),
            pltpu.VMEM((n_ctx,) + term, bf16),
            pltpu.VMEM((2, n_head, n_far_here) + term, bf16),
            pltpu.VMEM((2, n_head, n_far_here) + term, bf16),
            pltpu.VMEM((2, n_head) + term, bf16),
            raw,
            raw,
            rolled,
            rolled,
            pltpu.VMEM((2, n_head, heads, rows), f32),
            pltpu.VMEM((per, 2 * n_head, lanes), f32),
            pltpu.VMEM((n_head, per, lanes, width), f32),
            raw,
            pltpu.VMEM((2, n_head, per) + term, f32),
            pltpu.VMEM((n_head, 2) + term, f32),
            pltpu.VMEM((n_head, 2) + term, f32),
            pltpu.VMEM((n_head, chunks, n_far_here) + piece, f32),
            pltpu.VMEM((n_head, chunks, n_far_here) + piece, f32),
            pltpu.VMEM((n_head, 2) + term, f32),
            pltpu.VMEM((n_head // 2, 2) + term, f32),
            pltpu.VMEM((n_head // 2, 2) + term, f32),
            pltpu.VMEM((2,) + term, f32),
            pltpu.VMEM(((n_ctx + 1) // 2, 2) + term, f32),
            pltpu.VMEM((n_head, 2) + term, f32),
            pltpu.VMEM((n_ctx, chunks) + piece, f32),
            pltpu.VMEM((chunks, n_ctx) + piece, f32),
            pltpu.VMEM((n_head, chunks, per) + piece, f32),
            pltpu.VMEM((n_head, chunks, per) + piece, f32),
            pltpu.SMEM((n_ctx,), jnp.int32),
            pltpu.SMEM((blocks * n_far,), jnp.int32),
            dma((2,)),
            dma((3,)),
            dma((2,)),
            dma((2,)),
            dma((n_ctx,)),
            dma((2, n_ctx)),
            dma((4,)),
            dma((2,)),
            dma((1,)),
            dma((2,)),
            dma((2,)),
            dma((2,)),
            dma((1,)),
            dma(((n_ctx + 1) // 2,)),
            dma((2,)),
            dma((1,)),
            dma((chunks,)),
            dma((n_ctx,)),
            dma((chunks, n_ctx)),
            dma((1,)),
            dma((chunks,)),
            pltpu.SemaphoreType.REGULAR,
        ],
        compiler_params=pltpu.CompilerParams(
            collective_id=0, has_side_effects=True, vmem_limit_bytes=60 * 1024 * 1024
        ),
    )(
        block_pairs.T,
        pair_kinds.T,
        queries,
        out_grad,
        key_states.reshape(flat),
        value_states.reshape(flat),
        log_sums,
        row_deltas,
    )
    dq, dk, dv = pl.pallas_call(
        tail,
        out_shape=(
            jax.ShapeDtypeStruct(queries.shape, bf16),
            jax.ShapeDtypeStruct(flat, bf16),
            jax.ShapeDtypeStruct(flat, bf16),
        ),
        in_specs=[anywhere] * 3,
        out_specs=(anywhere,) * 3,
        scratch_shapes=[
            pltpu.VMEM(queries.shape, bf16),
            pltpu.VMEM(flat, bf16),
            pltpu.VMEM(flat, bf16),
            dma((6,)),
            dma((6,)),
        ],
    )(dq, dk, dv)
    return dq, dk.reshape(key_states.shape), dv.reshape(value_states.shape)


def solution(mesh):
    tokens = P(("ctx", "head"), None, None)
    stats = P("head", "ctx")
    return jax.shard_map(
        partial(shards, mesh.shape["ctx"], mesh.shape["head"]),
        mesh=mesh,
        in_specs=(tokens, tokens, tokens, tokens, stats, stats, P(), P()),
        out_specs=(tokens, tokens, tokens),
        check_vma=False,
    )
```

```python
from functools import partial

import jax
import jax.numpy as jnp
from jax import lax
from jax.experimental import pallas as pl
from jax.experimental.pallas import tpu as pltpu
from jax.sharding import PartitionSpec as P

BLOCK = 64
NEAR = 3
CUTS = 2
MESH = pl.DeviceIdType.MESH
NT = (((1,), (1,)), ((), ()))
TN = (((0,), (0,)), ((), ()))


def tile_grads(keys, values, q, g, log_row, delta_row, live, scale):
    scores = lax.dot_general(keys, q, NT, preferred_element_type=jnp.float32) * scale
    weights = jnp.where(live, jnp.exp(scores - log_row), 0.0)
    prob_grad = lax.dot_general(values, g, NT, preferred_element_type=jnp.float32)
    dscore = (weights * (prob_grad - delta_row)).astype(jnp.bfloat16)
    dv = jnp.dot(weights.astype(jnp.bfloat16), g, preferred_element_type=jnp.float32)
    dk = jnp.dot(dscore, q, preferred_element_type=jnp.float32)
    dq = lax.dot_general(dscore, keys, TN, preferred_element_type=jnp.float32)
    return dq, dk, dv


def kernel(
    n_ctx,
    n_head,
    n_slot,
    pair_tab,
    kind_tab,
    q_hbm,
    g_hbm,
    k_ref,
    v_ref,
    log_ref,
    delta_ref,
    dq_buf,
    dk_out,
    dv_out,
    wide,
    kv_own,
    k_loc,
    v_loc,
    kv_prev,
    outgoing,
    k_arrived,
    v_arrived,
    far_send,
    far_kv,
    hub_kv,
    q_raw,
    g_raw,
    q_flat,
    g_flat,
    stat_land,
    stat_rows,
    dq_acc,
    own_acc,
    prev_part,
    prev_land,
    far_part,
    far_land,
    hub_part,
    hub_land,
    hub_pair,
    hub_sum,
    hub_tree,
    hub_last,
    part,
    ret,
    blk_part,
    blk_land,
    want,
    owner,
    load_sem,
    kv_sem,
    stat_sem,
    prev_sem,
    arr_send,
    arr_recv,
    far_sem,
    hub_sem,
    back_sem,
    hred_sem,
    pair_sem,
    tree_send,
    tree_recv,
    last_sem,
    red_send,
    red_recv,
    ret_send,
    ret_recv,
    blk_send,
    blk_recv,
    ready,
):
    kv_loc, arrived = (k_loc, v_loc), (k_arrived, v_arrived)
    rank = lax.axis_index("ctx")
    me = lax.axis_index("head")
    rows = q_hbm.shape[0]
    width = q_hbm.shape[2]
    heads = q_hbm.shape[1] // n_head
    per = rows // BLOCK
    blocks = per * n_head
    lanes = BLOCK * heads
    n_far = n_slot - NEAR
    here_far = per * n_far
    chunks, piece = part.shape[1], part.shape[2]
    cuts = BLOCK // piece
    others = n_head - 1
    scale = width ** (-0.5)
    first = rank * blocks
    bf16, f32 = jnp.bfloat16, jnp.float32

    def peer(d):
        return lax.rem(me // 2 + d // 2, n_head // 2) * 2 + lax.rem(
            lax.rem(me, 2) + lax.rem(d, 2), 2
        )

    def arrive(ref, sem):
        pltpu.make_async_copy(ref, ref, sem).wait()

    def remote(source, target, send, recv, device):
        return pltpu.make_async_remote_copy(
            src_ref=source,
            dst_ref=target,
            send_sem=send,
            recv_sem=recv,
            device_id=device,
            device_id_type=MESH,
        )

    far_first = list(range(2, n_head)) + [1]
    across = far_first[:-1]
    has_prev = (rank > 0) | (me > 0)
    has_next = (rank < n_ctx - 1) | (me < n_head - 1)
    prev_dev = (jnp.where(me > 0, rank, rank - 1), jnp.where(me > 0, me - 1, n_head - 1))
    next_dev = (
        jnp.where(me < n_head - 1, rank, rank + 1),
        jnp.where(me < n_head - 1, me + 1, 0),
    )
    outer_prev = (me == 0) & (rank > 0)
    outer_next = (me == n_head - 1) & (rank < n_ctx - 1)
    lends = (rank > 0) & (rank < n_ctx - 2)
    has_far = rank > 2

    barrier = pltpu.get_barrier_semaphore()
    for d in range(1, n_head):
        pl.semaphore_signal(barrier, inc=1, device_id=(rank, peer(d)), device_id_type=MESH)

    def greet(s, c):
        pl.semaphore_signal(barrier, inc=1, device_id=(s, me), device_id_type=MESH)
        return c

    lax.fori_loop(rank + 1, n_ctx, greet, 0)

    @pl.when(outer_next)
    def _():
        pl.semaphore_signal(barrier, inc=1, device_id=next_dev, device_id_type=MESH)

    for u, (source, raw) in enumerate(((q_hbm, q_raw), (g_hbm, g_raw))):
        for k in range(n_head):
            for j in range(per):
                pltpu.make_async_copy(
                    source.at[pl.ds(j * BLOCK, BLOCK), pl.ds(k * heads, heads)],
                    raw.at[k, j],
                    load_sem.at[u],
                ).start()

    def wanted_by(s, c):
        best = jnp.int32(0)
        for i in range(blocks):
            at = s * blocks + i
            for j in range(NEAR, n_slot):
                local = pair_tab[j, at] - first
                named = (kind_tab[j, at] > 0) & (local >= 0) & (local < blocks)
                best = jnp.where(named, jnp.maximum(best, local), best)
        want[s] = best
        return c

    @pl.when(lends)
    def _():
        lax.fori_loop(rank + 2, n_ctx, wanted_by, 0)

    for i in range(blocks):
        for f in range(n_far):
            at = first + i
            owner[i * n_far + f] = jnp.where(
                kind_tab[NEAR + f, at] > 0, lax.div(pair_tab[NEAR + f, at], blocks), rank
            )

    @pl.when(jnp.logical_not(has_prev))
    def _():
        kv_prev[...] = jnp.zeros_like(kv_prev)

    for at, source in enumerate((k_ref, v_ref)):
        wide[...] = source[...].astype(f32)
        for h in range(n_head):
            head_rows = wide[pl.ds(h, rows, stride=n_head), :]
            kv_own[at, h] = head_rows.reshape(per, BLOCK, width).astype(bf16)

    pl.semaphore_wait(barrier, others + rank + outer_prev.astype(jnp.int32))

    def answer(o, c):
        pl.semaphore_signal(ready, inc=1, device_id=(o, me), device_id_type=MESH)
        return c

    lax.fori_loop(0, rank, answer, 0)

    @pl.when(outer_prev)
    def _():
        pl.semaphore_signal(ready, inc=1, device_id=prev_dev, device_id_type=MESH)

    def await_ready():
        @pl.when(rank < n_ctx - 1)
        def _():
            pl.semaphore_wait(ready, n_ctx - 1 - rank + outer_next.astype(jnp.int32))

    def kv_copy(a, p):
        return remote(
            kv_own.at[a, p],
            kv_loc[a].at[pl.ds(me * per, per)],
            kv_sem.at[0],
            kv_sem.at[1 + a],
            (rank, p),
        )

    def first_copy(a, p):
        return remote(
            kv_own.at[a, p, 0], kv_loc[a].at[0], kv_sem.at[0], kv_sem.at[1 + a], (rank, p)
        )

    def stat_copy(u, p):
        return remote(
            (log_ref, delta_ref)[u].at[:, pl.ds(pl.multiple_of(p * rows, rows), rows)],
            stat_land.at[u, me],
            stat_sem.at[0],
            stat_sem.at[1],
            (rank, p),
        )

    def prev_copy():
        return remote(
            kv_own.at[:, :, per - 1], kv_prev, prev_sem.at[0], prev_sem.at[1], next_dev
        )

    @pl.when((rank == 0) & (me == 0))
    def _():
        for a in range(2):
            for d in far_first:
                first_copy(a, peer(d)).start()
            kv_loc[a][0] = kv_own[a, 0, 0]

    for u in range(2):
        for d in far_first:
            stat_copy(u, peer(d)).start()

    @pl.when(lends)
    def _():
        for a in range(2):
            for d in far_first:
                kv_copy(a, peer(d)).start()
        for a in range(2):
            kv_loc[a][pl.ds(me * per, per)] = kv_own[a, me]

    for u, source in enumerate((log_ref, delta_ref)):
        stat_land[u, me] = source[:, pl.ds(pl.multiple_of(me * rows, rows), rows)]

    def arr_copy(a, s):
        return remote(
            outgoing.at[a, s], arrived[a].at[rank], arr_send.at[s], arr_recv.at[a, rank], (s, me)
        )

    @pl.when(rank == 0)
    def _():
        @pl.when(me > 0)
        def _():
            for a in range(2):
                arrive(kv_loc[a].at[0], kv_sem.at[1 + a])

        await_ready()

        def send_first(i, c):
            s = n_ctx - 1 - i
            for a in range(2):
                outgoing[a, s] = kv_loc[a][0]
                arr_copy(a, s).start()
            return c

        lax.fori_loop(0, n_ctx - 1, send_first, 0)
        for a in range(2):
            arrived[a][0] = kv_loc[a][0]
        prev_copy().start()

    arrive(stat_land.at[:, pl.ds(0, others)], stat_sem.at[1])
    spread = (
        lax.broadcasted_iota(jnp.int32, (BLOCK, lanes), 1) // heads
        == lax.broadcasted_iota(jnp.int32, (BLOCK, lanes), 0)
    ).astype(bf16)
    own_row = lax.broadcasted_iota(jnp.int32, (heads, lanes), 1) % heads == lax.broadcasted_iota(
        jnp.int32, (heads, lanes), 0
    )
    stats = stat_land[...].reshape(2 * n_head * heads, rows)
    high = stats.astype(bf16)
    rest = stats - high.astype(f32)
    mid = rest.astype(bf16)
    low = (rest - mid.astype(f32)).astype(bf16)
    for j in range(per):
        at = slice(j * BLOCK, (j + 1) * BLOCK)
        by_lane = sum(
            jnp.dot(part_of[:, at], spread, preferred_element_type=f32)
            for part_of in (high, mid, low)
        ).reshape(2 * n_head, heads, lanes)
        stat_rows[j] = jnp.sum(jnp.where(own_row[None], by_lane, 0.0), axis=1)

    key_row = lax.broadcasted_iota(jnp.int32, (2 * BLOCK, lanes), 0)
    causal = (key_row >= BLOCK) | (
        key_row <= lax.broadcasted_iota(jnp.int32, (2 * BLOCK, lanes), 1) // heads
    )
    pair_row = lax.broadcasted_iota(jnp.int32, (2 * BLOCK, 1), 0)

    def grads(k, j, keys, values, live):
        return tile_grads(
            keys,
            values,
            q_flat[k, j],
            g_flat[k, j],
            stat_rows[j, pl.ds(k, 1)],
            stat_rows[j, pl.ds(n_head + k, 1)],
            live,
            scale,
        )

    def finish(lo, hi):
        def each(k, c):
            for j in range(per):
                total = dq_acc[k, j] * scale
                dq_buf[k, j] = total.reshape(BLOCK, heads, width).astype(bf16)
            return c

        lax.fori_loop(lo, hi, each, 0)

    arrive(q_raw, load_sem.at[0])
    arrive(g_raw, load_sem.at[1])

    def flatten(t, c):
        k, j = t // per, lax.rem(t, per)
        for raw, flat in ((q_raw, q_flat), (g_raw, g_flat)):
            flat[k, j] = raw[k, j].astype(f32).reshape(lanes, width).astype(bf16)
        return c

    lax.fori_loop(0, n_head * per, flatten, 0)

    own_acc[...] = jnp.zeros_like(own_acc)
    dq_acc[:, 0] = jnp.zeros((n_head, lanes, width), f32)

    def near(j, lo, hi):
        prev_kind = kind_tab[1, first + me * per + j]
        near_live = causal & (jnp.where(pair_row < BLOCK, 1, prev_kind) > 0)

        def near_step(k, c):
            keys, values = (
                jnp.concatenate(
                    [kv_own[a, k, j], kv_prev[a, k] if j == 0 else kv_own[a, k, j - 1]], axis=0
                )
                for a in range(2)
            )
            dq, dk, dv = grads(k, j, keys, values, near_live)
            dq_acc[k, j] = dq if j else dq_acc[k, j] + dq
            for u, terms in enumerate((dk, dv)):
                own_acc[u, k, j] += terms[:BLOCK]
                if j == 0:
                    prev_part[k, u] = terms[BLOCK:]
                else:
                    own_acc[u, k, j - 1] += terms[BLOCK:]
            return c

        lax.fori_loop(lo, hi, near_step, 0, unroll=2)

    half = n_head // 2

    def send_block(a):
        def send(i, c):
            s = n_ctx - 1 - i
            outgoing[a, s] = kv_loc[a][want[s]]
            arr_copy(a, s).start()
            return c

        lax.fori_loop(0, n_ctx - 2 - rank, send, 0)

    def lend(a):
        @pl.when(lends)
        def _():
            arrive(kv_loc[a].at[pl.ds(0, others * per)], kv_sem.at[1 + a])
            if a == 0:
                await_ready()
            send_block(a)
            arrived[a][rank] = kv_loc[a][0]
            if a == 1:
                prev_copy().start()

    lend(0)

    @pl.when(rank >= n_ctx - 2)
    def _():
        await_ready()
        for a in range(2):
            arrived[a][rank] = kv_own[a, 0, 0]

        @pl.when(has_next)
        def _():
            prev_copy().start()

    for j in range(1, per):
        near(j, 0, half)
    lend(1)
    for j in range(1, per):
        near(j, half, n_head)

    @pl.when(rank > 0)
    def _():
        for a in range(2):
            arrive(arrived[a].at[0], arr_recv.at[a, 0])

    for a in range(2):
        for d in far_first:
            remote(
                arrived[a].at[0], hub_kv.at[a, me], hub_sem.at[0], hub_sem.at[1], (rank, peer(d))
            ).start()
        hub_kv[a, me] = arrived[a][0]

    def back_copy():
        return remote(prev_part, prev_land, back_sem.at[0], back_sem.at[1], prev_dev)

    late0 = outer_prev & (lax.rem(rank, 2) == 0)
    early_back = (
        has_prev & jnp.logical_not(late0) & jnp.logical_not(has_far)
    )
    yields = late0 & lends & has_far

    def near_first():
        @pl.when(has_prev)
        def _():
            arrive(kv_prev, prev_sem.at[1])

        near(0, 0, n_head)

    @pl.when(jnp.logical_not(late0))
    def _():
        near_first()

    @pl.when(early_back)
    def _():
        back_copy().start()

    def far_copy(a, d):
        return remote(
            far_send.at[a, peer(d)],
            far_kv.at[a, me],
            far_sem.at[0],
            far_sem.at[1 if d == 1 else 2 + a],
            (rank, peer(d)),
        )

    def fill_far(buf, a, p):
        for i in range(here_far):
            buf[a, p, i] = arrived[a][owner[p * here_far + i]]

    @pl.when(has_far)
    def _():
        for a in range(2):

            def arr_wait(o, c):
                arrive(arrived[a].at[o], arr_recv.at[a, o])
                return c

            lax.fori_loop(1, rank - 1, arr_wait, 0)
            for d in far_first:
                fill_far(far_send, a, peer(d))
                far_copy(a, d).start()
            fill_far(far_kv, a, me)

    def red_copy(c, k):
        return remote(
            far_part.at[k, c], far_land.at[me, c], red_send.at[0], red_recv.at[c], (rank, k)
        )

    def far_step(k):
        for j in range(per):
            total = dq_acc[k, j]
            for f in range(n_far):
                i = j * n_far + f
                kind = kind_tab[NEAR + f, first + me * per + j]
                dq, dk, dv = grads(k, j, far_kv[0, k, i], far_kv[1, k, i], kind > 0)
                total += dq
                for u, terms in enumerate((dk, dv)):
                    for b in range(cuts):
                        far_part[k, u * cuts + b, i] = terms[b * piece : (b + 1) * piece]
            dq_acc[k, j] = total

    @pl.when(has_far)
    def _():
        far_step(me)

    arrive(hub_kv.at[:, pl.ds(0, others)], hub_sem.at[1])

    pairs = n_head // 2
    tens = [2 * i for i in range(1, pairs)]

    def hred_copy(d):
        slot = 0 if d == 1 else d // 2
        return remote(
            hub_part.at[peer(d)], hub_land.at[slot], hred_sem.at[0], hred_sem.at[1], (rank, peer(d))
        )

    def pair_copy(d):
        return remote(
            hub_part.at[peer(d + 1)],
            hub_pair.at[d // 2],
            pair_sem.at[0],
            pair_sem.at[1],
            (rank, peer(1)),
        )

    def hub_step(k):
        for j in range(per):
            kind = kind_tab[NEAR - 1, first + me * per + j]
            dq, dk, dv = grads(k, j, hub_kv[0, k], hub_kv[1, k], kind > 0)
            dq_acc[k, j] += dq
            for u, terms in enumerate((dk, dv)):
                if j == 0:
                    hub_part[k, u] = terms
                else:
                    hub_part[k, u] += terms

    for d in tens:
        hub_step(peer(d + 1))
        pair_copy(d).start()
    for d in tens:
        hub_step(peer(d))
    arrive(hub_pair.at[pl.ds(1, pairs - 1)], pair_sem.at[1])
    for d in tens:
        hub_part[peer(d)] += hub_pair[d // 2]
        hred_copy(d).start()

    hub_step(peer(1))
    hred_copy(1).start()
    hub_step(me)

    @pl.when(has_far)
    def _():
        for a in range(2):
            arrive(far_kv.at[a, pl.ds(0, others - 1)], far_sem.at[2 + a])

        for d in across:
            far_step(peer(d))
            red_copy(0, peer(d)).start()
        for c in range(1, chunks):
            for d in across:
                red_copy(c, peer(d)).start()
        arrive(far_kv.at[:, 0], far_sem.at[1])
        far_step(peer(1))
        for c in range(chunks):
            red_copy(c, peer(1)).start()


    stages = tree_recv.shape[0]

    def tree_copy(i):
        return remote(
            hub_sum, hub_tree.at[i], tree_send.at[0], tree_recv.at[i], (rank - 2**i, me)
        )

    def tree_up(i):
        if i < stages:

            @pl.when(lax.rem(rank, 2 ** (i + 1)) == 2**i)
            def _():
                tree_copy(i).start()

    def tree_take(i):
        if i < stages:

            @pl.when((lax.rem(rank, 2 ** (i + 1)) == 0) & (rank + 2**i < n_ctx))
            def _():
                arrive(hub_tree.at[i], tree_recv.at[i])
                hub_sum[...] += hub_tree[i]

    def ret_copy(c, o):
        return remote(part.at[o, c], ret.at[c, rank], ret_send.at[o], ret_recv.at[c, rank], (o, me))

    sources = [(peer(d), far_land) for d in range(1, n_head)] + [(me, far_part)]

    def reduce(c):
        @pl.when(has_far)
        def _():
            reduce_live(c)

    def reduce_live(c):
        arrive(far_land.at[pl.ds(0, others), c], red_recv.at[c])

        def send_part(o, carry):
            terms = jnp.zeros((piece, width), f32)
            for p, buf in sources:
                for i in range(here_far):
                    mine = owner[p * here_far + i] == o
                    terms += jnp.where(mine, buf[p, c, i], 0.0)
            part[o, c] = terms
            ret_copy(c, o).start()
            return carry

        lax.fori_loop(1, rank - 1, send_part, 0)

    arrive(hub_land, hred_sem.at[1])
    hub_sum[...] = sum((hub_land[i] for i in range(pairs)), hub_part[me])
    tree_up(0)
    reduce(0)
    @pl.when(late0)
    def _():
        near_first()

    finish(0, half)
    reduce(1)
    tree_take(0)
    tree_up(1)
    finish(half, n_head)
    for c in range(2, chunks):
        reduce(c)

    @pl.when(has_prev & jnp.logical_not(yields | early_back))
    def _():
        back_copy().start()

    for i in range(1, stages):
        tree_take(i)
        tree_up(i + 1)

    def last_copy():
        return remote(hub_sum, hub_last.at[me], last_sem.at[0], last_sem.at[1], (rank, 0))

    @pl.when((rank == 0) & (me > 0))
    def _():
        last_copy().start()

    def blk_copy(c, p):
        return remote(
            blk_part.at[p, c], blk_land.at[me, c], blk_send.at[0], blk_recv.at[c], (rank, p)
        )

    @pl.when(lends)
    def _():
        blk_part[...] = jnp.zeros_like(blk_part)
        for c in range(chunks):

            def take_part(s, carry):
                arrive(ret.at[c, s], ret_recv.at[c, s])
                for i in range(blocks):
                    blk_part[i // per, c, i % per] += jnp.where(want[s] == i, ret[c, s], 0.0)
                return carry

            lax.fori_loop(rank + 2, n_ctx, take_part, 0)
            for d in far_first:
                blk_copy(c, peer(d)).start()

    @pl.when(yields)
    def _():
        back_copy().start()

    @pl.when(has_next)
    def _():
        arrive(prev_land, back_sem.at[1])
        for k in range(n_head):
            for u in range(2):
                own_acc[u, k, per - 1] += prev_land[k, u]

    @pl.when((rank == 0) & (me == 0))
    def _():
        for u in range(2):
            own_acc[u, 0, 0] += hub_sum[u]
        arrive(hub_last.at[pl.ds(0, others)], last_sem.at[1])
        for k in range(1, n_head):
            for u in range(2):
                own_acc[u, k, 0] += hub_last[k, u]

    @pl.when(lends)
    def _():
        for c in range(chunks):
            u, at = c // cuts, pl.ds(c % cuts * piece, piece)
            own_acc[u, me, :, at] += blk_part[me, c]
            arrive(blk_land.at[pl.ds(0, others), c], blk_recv.at[c])
            for d in range(1, n_head):
                own_acc[u, peer(d), :, at] += blk_land[peer(d), c]

    for u, out in ((0, dk_out), (1, dv_out)):
        for h in range(n_head):
            terms = own_acc[u, h].reshape(rows, width)
            wide[pl.ds(h, rows, stride=n_head), :] = terms * scale if u == 0 else terms
        out[...] = wide[...].astype(bf16)

    def sent_block(s, c):
        arrive(outgoing.at[:, s], arr_send.at[s])
        return c

    lax.fori_loop(jnp.where(rank == 0, 1, rank + 2), n_ctx, sent_block, 0)

    def sent_part(o, c):
        arrive(part.at[o], ret_send.at[o])
        return c

    lax.fori_loop(1, rank - 1, sent_part, 0)
    arrive(stat_land.at[:, pl.ds(0, others)], stat_sem.at[0])
    arrive(hub_kv.at[:, pl.ds(0, others)], hub_sem.at[0])
    arrive(hub_land, hred_sem.at[0])
    arrive(hub_pair.at[pl.ds(1, pairs - 1)], pair_sem.at[0])

    @pl.when(has_far)
    def _():
        arrive(far_kv.at[:, pl.ds(0, others)], far_sem.at[0])
        arrive(far_land.at[pl.ds(0, others)], red_send.at[0])

    @pl.when((rank == 0) & (me == 0))
    def _():
        arrive(hub_kv.at[:, pl.ds(0, others)], kv_sem.at[0])

    @pl.when(lends)
    def _():
        arrive(kv_own.at[:, pl.ds(0, others)], kv_sem.at[0])
        arrive(blk_land.at[pl.ds(0, others)], blk_send.at[0])

    @pl.when(rank > 0)
    def _():
        arrive(hub_sum, tree_send.at[0])

    @pl.when((rank == 0) & (me > 0))
    def _():
        arrive(hub_sum, last_sem.at[0])

    @pl.when(has_next)
    def _():
        prev_copy().wait_send()

    @pl.when(has_prev)
    def _():
        back_copy().wait_send()


def tail(dq_in, dk_in, dv_in, dq_out, dk_out, dv_out, stores):
    n_head, per, block, heads, _ = dq_in.shape
    routes = [
        (dq_in.at[k, j], dq_out.at[pl.ds(j * block, block), pl.ds(k * heads, heads)])
        for k in range(n_head)
        for j in range(per)
    ]
    routes += [(dk_in, dk_out), (dv_in, dv_out)]
    copies = [
        pltpu.make_async_copy(source, target, stores.at[i])
        for i, (source, target) in enumerate(routes)
    ]
    for copy in copies:
        copy.start()
    for copy in copies:
        copy.wait()


def shards(
    n_ctx,
    n_head,
    queries,
    key_states,
    value_states,
    out_grad,
    log_sums,
    row_deltas,
    block_pairs,
    pair_kinds,
):
    rows, all_heads, width = queries.shape
    heads = all_heads // n_head
    n_slot = block_pairs.shape[1]
    n_far = n_slot - NEAR
    per = rows // BLOCK
    blocks = per * n_head
    lanes = BLOCK * heads
    n_far_here = per * n_far
    stages = (n_ctx - 1).bit_length()
    bf16, f32 = jnp.bfloat16, jnp.float32
    flat = (rows * n_head, width)
    term = (BLOCK, width)
    piece = (BLOCK // CUTS, width)
    chunks = 2 * CUTS
    vmem = pl.BlockSpec(memory_space=pltpu.VMEM)
    smem = pl.BlockSpec(memory_space=pltpu.SMEM)
    anywhere = pl.BlockSpec(memory_space=pl.ANY)
    dma = pltpu.SemaphoreType.DMA
    raw = pltpu.VMEM((n_head, per, BLOCK, heads, width), bf16)
    rolled = pltpu.VMEM((n_head, per, lanes, width), bf16)
    dq, dk, dv = pl.pallas_call(
        partial(kernel, n_ctx, n_head, n_slot),
        out_shape=(raw, pltpu.VMEM(flat, bf16), pltpu.VMEM(flat, bf16)),
        in_specs=[smem, smem, anywhere, anywhere, vmem, vmem, vmem, vmem],
        out_specs=(vmem, vmem, vmem),
        scratch_shapes=[
            pltpu.VMEM(flat, f32),
            pltpu.VMEM((2, n_head, per) + term, bf16),
            pltpu.VMEM((blocks,) + term, bf16),
            pltpu.VMEM((blocks,) + term, bf16),
            pltpu.VMEM((2, n_head) + term, bf16),
            pltpu.VMEM((2, n_ctx) + term, bf16),
            pltpu.VMEM((n_ctx,) + term, bf16),
            pltpu.VMEM((n_ctx,) + term, bf16),
            pltpu.VMEM((2, n_head, n_far_here) + term, bf16),
            pltpu.VMEM((2, n_head, n_far_here) + term, bf16),
            pltpu.VMEM((2, n_head) + term, bf16),
            raw,
            raw,
            rolled,
            rolled,
            pltpu.VMEM((2, n_head, heads, rows), f32),
            pltpu.VMEM((per, 2 * n_head, lanes), f32),
            pltpu.VMEM((n_head, per, lanes, width), f32),
            pltpu.VMEM((2, n_head, per) + term, f32),
            pltpu.VMEM((n_head, 2) + term, f32),
            pltpu.VMEM((n_head, 2) + term, f32),
            pltpu.VMEM((n_head, chunks, n_far_here) + piece, f32),
            pltpu.VMEM((n_head, chunks, n_far_here) + piece, f32),
            pltpu.VMEM((n_head, 2) + term, f32),
            pltpu.VMEM((n_head // 2, 2) + term, f32),
            pltpu.VMEM((n_head // 2, 2) + term, f32),
            pltpu.VMEM((2,) + term, f32),
            pltpu.VMEM((stages, 2) + term, f32),
            pltpu.VMEM((n_head, 2) + term, f32),
            pltpu.VMEM((n_ctx, chunks) + piece, f32),
            pltpu.VMEM((chunks, n_ctx) + piece, f32),
            pltpu.VMEM((n_head, chunks, per) + piece, f32),
            pltpu.VMEM((n_head, chunks, per) + piece, f32),
            pltpu.SMEM((n_ctx,), jnp.int32),
            pltpu.SMEM((blocks * n_far,), jnp.int32),
            dma((2,)),
            dma((3,)),
            dma((2,)),
            dma((2,)),
            dma((n_ctx,)),
            dma((2, n_ctx)),
            dma((4,)),
            dma((2,)),
            dma((2,)),
            dma((2,)),
            dma((2,)),
            dma((1,)),
            dma((stages,)),
            dma((2,)),
            dma((1,)),
            dma((chunks,)),
            dma((n_ctx,)),
            dma((chunks, n_ctx)),
            dma((1,)),
            dma((chunks,)),
            pltpu.SemaphoreType.REGULAR,
        ],
        compiler_params=pltpu.CompilerParams(
            collective_id=0, has_side_effects=True, vmem_limit_bytes=60 * 1024 * 1024
        ),
    )(
        block_pairs.T,
        pair_kinds.T,
        queries,
        out_grad,
        key_states.reshape(flat),
        value_states.reshape(flat),
        log_sums,
        row_deltas,
    )
    dq, dk, dv = pl.pallas_call(
        tail,
        out_shape=(
            jax.ShapeDtypeStruct(queries.shape, bf16),
            jax.ShapeDtypeStruct(flat, bf16),
            jax.ShapeDtypeStruct(flat, bf16),
        ),
        in_specs=[vmem] * 3,
        out_specs=(anywhere,) * 3,
        scratch_shapes=[dma((n_head * per + 2,))],
    )(*(pltpu.with_memory_space_constraint(x, pltpu.VMEM) for x in (dq, dk, dv)))
    return dq, dk.reshape(key_states.shape), dv.reshape(value_states.shape)


def solution(mesh):
    tokens = P(("ctx", "head"), None, None)
    stats = P("head", "ctx")
    return jax.shard_map(
        partial(shards, mesh.shape["ctx"], mesh.shape["head"]),
        mesh=mesh,
        in_specs=(tokens, tokens, tokens, tokens, stats, stats, P(), P()),
        out_specs=(tokens, tokens, tokens),
        check_vma=False,
    )
```

```python
from functools import partial

import jax
import jax.numpy as jnp
from jax import lax
from jax.experimental import pallas as pl
from jax.experimental.pallas import tpu as pltpu
from jax.sharding import PartitionSpec as P

BLOCK = 64
NEAR = 3
CUTS = 2
MESH = pl.DeviceIdType.MESH
NT = (((1,), (1,)), ((), ()))
TN = (((0,), (0,)), ((), ()))


def tile_grads(keys, values, q, g, log_row, delta_row, live, scale):
    scores = lax.dot_general(keys, q, NT, preferred_element_type=jnp.float32) * scale
    weights = jnp.where(live, jnp.exp(scores - log_row), 0.0)
    prob_grad = lax.dot_general(values, g, NT, preferred_element_type=jnp.float32)
    dscore = (weights * (prob_grad - delta_row)).astype(jnp.bfloat16)
    dv = jnp.dot(weights.astype(jnp.bfloat16), g, preferred_element_type=jnp.float32)
    dk = jnp.dot(dscore, q, preferred_element_type=jnp.float32)
    dq = lax.dot_general(dscore, keys, TN, preferred_element_type=jnp.float32)
    return dq, dk, dv


def kernel(
    n_ctx,
    n_head,
    n_slot,
    pair_tab,
    kind_tab,
    q_hbm,
    g_hbm,
    k_ref,
    v_ref,
    log_ref,
    delta_ref,
    dq_buf,
    dk_out,
    dv_out,
    wide,
    kv_own,
    k_loc,
    v_loc,
    kv_prev,
    outgoing,
    k_arrived,
    v_arrived,
    far_send,
    far_kv,
    hub_kv,
    q_raw,
    g_raw,
    q_flat,
    g_flat,
    stat_land,
    stat_rows,
    dq_acc,
    own_acc,
    prev_part,
    prev_land,
    far_part,
    far_land,
    hub_part,
    hub_land,
    hub_pair,
    hub_sum,
    hub_tree,
    hub_last,
    part,
    ret,
    blk_part,
    blk_land,
    want,
    owner,
    load_sem,
    kv_sem,
    stat_sem,
    prev_sem,
    arr_send,
    arr_recv,
    far_sem,
    hub_sem,
    back_sem,
    hred_sem,
    pair_sem,
    tree_send,
    tree_recv,
    last_sem,
    red_send,
    red_recv,
    ret_send,
    ret_recv,
    blk_send,
    blk_recv,
    ready,
):
    kv_loc, arrived = (k_loc, v_loc), (k_arrived, v_arrived)
    rank = lax.axis_index("ctx")
    me = lax.axis_index("head")
    rows = q_hbm.shape[0]
    width = q_hbm.shape[2]
    heads = q_hbm.shape[1] // n_head
    per = rows // BLOCK
    blocks = per * n_head
    lanes = BLOCK * heads
    n_far = n_slot - NEAR
    here_far = per * n_far
    chunks, piece = part.shape[1], part.shape[2]
    cuts = BLOCK // piece
    others = n_head - 1
    scale = width ** (-0.5)
    first = rank * blocks
    bf16, f32 = jnp.bfloat16, jnp.float32

    def peer(d):
        return lax.rem(me // 2 + d // 2, n_head // 2) * 2 + lax.rem(
            lax.rem(me, 2) + lax.rem(d, 2), 2
        )

    def arrive(ref, sem):
        pltpu.make_async_copy(ref, ref, sem).wait()

    def remote(source, target, send, recv, device):
        return pltpu.make_async_remote_copy(
            src_ref=source,
            dst_ref=target,
            send_sem=send,
            recv_sem=recv,
            device_id=device,
            device_id_type=MESH,
        )

    far_first = list(range(2, n_head)) + [1]
    across = far_first[:-1]
    has_prev = (rank > 0) | (me > 0)
    has_next = (rank < n_ctx - 1) | (me < n_head - 1)
    prev_dev = (jnp.where(me > 0, rank, rank - 1), jnp.where(me > 0, me - 1, n_head - 1))
    next_dev = (
        jnp.where(me < n_head - 1, rank, rank + 1),
        jnp.where(me < n_head - 1, me + 1, 0),
    )
    outer_prev = (me == 0) & (rank > 0)
    outer_next = (me == n_head - 1) & (rank < n_ctx - 1)
    lends = (rank > 0) & (rank < n_ctx - 2)
    has_far = rank > 2

    barrier = pltpu.get_barrier_semaphore()
    for d in range(1, n_head):
        pl.semaphore_signal(barrier, inc=1, device_id=(rank, peer(d)), device_id_type=MESH)

    def greet(s, c):
        pl.semaphore_signal(barrier, inc=1, device_id=(s, me), device_id_type=MESH)
        return c

    lax.fori_loop(rank + 1, n_ctx, greet, 0)

    @pl.when(outer_next)
    def _():
        pl.semaphore_signal(barrier, inc=1, device_id=next_dev, device_id_type=MESH)

    for u, (source, raw) in enumerate(((q_hbm, q_raw), (g_hbm, g_raw))):
        for k in range(n_head):
            for j in range(per):
                pltpu.make_async_copy(
                    source.at[pl.ds(j * BLOCK, BLOCK), pl.ds(k * heads, heads)],
                    raw.at[k, j],
                    load_sem.at[u],
                ).start()

    def wanted_by(s, c):
        best = jnp.int32(0)
        for i in range(blocks):
            at = s * blocks + i
            for j in range(NEAR, n_slot):
                local = pair_tab[j, at] - first
                named = (kind_tab[j, at] > 0) & (local >= 0) & (local < blocks)
                best = jnp.where(named, jnp.maximum(best, local), best)
        want[s] = best
        return c

    @pl.when(lends)
    def _():
        lax.fori_loop(rank + 2, n_ctx, wanted_by, 0)

    for i in range(blocks):
        for f in range(n_far):
            at = first + i
            owner[i * n_far + f] = jnp.where(
                kind_tab[NEAR + f, at] > 0, lax.div(pair_tab[NEAR + f, at], blocks), rank
            )

    @pl.when(jnp.logical_not(has_prev))
    def _():
        kv_prev[...] = jnp.zeros_like(kv_prev)

    for at, source in enumerate((k_ref, v_ref)):
        wide[...] = source[...].astype(f32)
        for h in range(n_head):
            head_rows = wide[pl.ds(h, rows, stride=n_head), :]
            kv_own[at, h] = head_rows.reshape(per, BLOCK, width).astype(bf16)

    pl.semaphore_wait(barrier, others + rank + outer_prev.astype(jnp.int32))

    def answer(o, c):
        pl.semaphore_signal(ready, inc=1, device_id=(o, me), device_id_type=MESH)
        return c

    lax.fori_loop(0, rank, answer, 0)

    @pl.when(outer_prev)
    def _():
        pl.semaphore_signal(ready, inc=1, device_id=prev_dev, device_id_type=MESH)

    def await_ready():
        @pl.when(rank < n_ctx - 1)
        def _():
            pl.semaphore_wait(ready, n_ctx - 1 - rank + outer_next.astype(jnp.int32))

    def kv_copy(a, p):
        return remote(
            kv_own.at[a, p],
            kv_loc[a].at[pl.ds(me * per, per)],
            kv_sem.at[0],
            kv_sem.at[1 + a],
            (rank, p),
        )

    def first_copy(a, p):
        return remote(
            kv_own.at[a, p, 0], kv_loc[a].at[0], kv_sem.at[0], kv_sem.at[1 + a], (rank, p)
        )

    def stat_copy(u, p):
        return remote(
            (log_ref, delta_ref)[u].at[:, pl.ds(pl.multiple_of(p * rows, rows), rows)],
            stat_land.at[u, me],
            stat_sem.at[0],
            stat_sem.at[1],
            (rank, p),
        )

    def prev_copy():
        return remote(
            kv_own.at[:, :, per - 1], kv_prev, prev_sem.at[0], prev_sem.at[1], next_dev
        )

    @pl.when((rank == 0) & (me == 0))
    def _():
        for a in range(2):
            for d in far_first:
                first_copy(a, peer(d)).start()
            kv_loc[a][0] = kv_own[a, 0, 0]

    for u in range(2):
        for d in far_first:
            stat_copy(u, peer(d)).start()

    @pl.when(lends)
    def _():
        for a in range(2):
            for d in far_first:
                kv_copy(a, peer(d)).start()
        for a in range(2):
            kv_loc[a][pl.ds(me * per, per)] = kv_own[a, me]

    for u, source in enumerate((log_ref, delta_ref)):
        stat_land[u, me] = source[:, pl.ds(pl.multiple_of(me * rows, rows), rows)]

    def arr_copy(a, s):
        return remote(
            outgoing.at[a, s], arrived[a].at[rank], arr_send.at[s], arr_recv.at[a, rank], (s, me)
        )

    @pl.when(rank == 0)
    def _():
        @pl.when(me > 0)
        def _():
            for a in range(2):
                arrive(kv_loc[a].at[0], kv_sem.at[1 + a])

        await_ready()

        def send_first(i, c):
            s = n_ctx - 1 - i
            for a in range(2):
                outgoing[a, s] = kv_loc[a][0]
                arr_copy(a, s).start()
            return c

        lax.fori_loop(0, n_ctx - 1, send_first, 0)
        for a in range(2):
            arrived[a][0] = kv_loc[a][0]
        prev_copy().start()

    def send_block(a):
        def send(i, c):
            s = n_ctx - 1 - i
            outgoing[a, s] = kv_loc[a][want[s]]
            arr_copy(a, s).start()
            return c

        lax.fori_loop(0, n_ctx - 2 - rank, send, 0)

    def lend(a):
        @pl.when(lends)
        def _():
            arrive(kv_loc[a].at[pl.ds(0, others * per)], kv_sem.at[1 + a])
            if a == 0:
                await_ready()
            send_block(a)
            arrived[a][rank] = kv_loc[a][0]
            if a == 1:
                prev_copy().start()

    lend(0)

    @pl.when(rank >= n_ctx - 2)
    def _():
        await_ready()
        for a in range(2):
            arrived[a][rank] = kv_own[a, 0, 0]

        @pl.when(has_next)
        def _():
            prev_copy().start()

    arrive(stat_land.at[:, pl.ds(0, others)], stat_sem.at[1])
    spread = (
        lax.broadcasted_iota(jnp.int32, (BLOCK, lanes), 1) // heads
        == lax.broadcasted_iota(jnp.int32, (BLOCK, lanes), 0)
    ).astype(bf16)
    own_row = lax.broadcasted_iota(jnp.int32, (heads, lanes), 1) % heads == lax.broadcasted_iota(
        jnp.int32, (heads, lanes), 0
    )
    stats = stat_land[...].reshape(2 * n_head * heads, rows)
    high = stats.astype(bf16)
    rest = stats - high.astype(f32)
    mid = rest.astype(bf16)
    low = (rest - mid.astype(f32)).astype(bf16)
    for j in range(per):
        at = slice(j * BLOCK, (j + 1) * BLOCK)
        by_lane = sum(
            jnp.dot(part_of[:, at], spread, preferred_element_type=f32)
            for part_of in (high, mid, low)
        ).reshape(2 * n_head, heads, lanes)
        stat_rows[j] = jnp.sum(jnp.where(own_row[None], by_lane, 0.0), axis=1)

    key_row = lax.broadcasted_iota(jnp.int32, (2 * BLOCK, lanes), 0)
    causal = (key_row >= BLOCK) | (
        key_row <= lax.broadcasted_iota(jnp.int32, (2 * BLOCK, lanes), 1) // heads
    )
    pair_row = lax.broadcasted_iota(jnp.int32, (2 * BLOCK, 1), 0)

    def grads(k, j, keys, values, live):
        return tile_grads(
            keys,
            values,
            q_flat[k, j],
            g_flat[k, j],
            stat_rows[j, pl.ds(k, 1)],
            stat_rows[j, pl.ds(n_head + k, 1)],
            live,
            scale,
        )

    def finish(lo, hi):
        def each(k, c):
            for j in range(per):
                total = dq_acc[k, j] * scale
                dq_buf[k, j] = total.reshape(BLOCK, heads, width).astype(bf16)
            return c

        lax.fori_loop(lo, hi, each, 0)

    arrive(q_raw, load_sem.at[0])
    arrive(g_raw, load_sem.at[1])

    def flatten(t, c):
        k, j = t // per, lax.rem(t, per)
        for raw, flat in ((q_raw, q_flat), (g_raw, g_flat)):
            flat[k, j] = raw[k, j].astype(f32).reshape(lanes, width).astype(bf16)
        return c

    lax.fori_loop(0, n_head * per, flatten, 0)

    own_acc[...] = jnp.zeros_like(own_acc)
    dq_acc[:, 0] = jnp.zeros((n_head, lanes, width), f32)

    def near(j, lo, hi):
        prev_kind = kind_tab[1, first + me * per + j]
        near_live = causal & (jnp.where(pair_row < BLOCK, 1, prev_kind) > 0)

        def near_step(k, c):
            keys, values = (
                jnp.concatenate(
                    [kv_own[a, k, j], kv_prev[a, k] if j == 0 else kv_own[a, k, j - 1]], axis=0
                )
                for a in range(2)
            )
            dq, dk, dv = grads(k, j, keys, values, near_live)
            dq_acc[k, j] = dq if j else dq_acc[k, j] + dq
            for u, terms in enumerate((dk, dv)):
                own_acc[u, k, j] += terms[:BLOCK]
                if j == 0:
                    prev_part[k, u] = terms[BLOCK:]
                else:
                    own_acc[u, k, j - 1] += terms[BLOCK:]
            return c

        lax.fori_loop(lo, hi, near_step, 0, unroll=2)

    half = n_head // 2

    lend(1)
    for j in range(1, per):
        near(j, 0, n_head)

    @pl.when(rank > 0)
    def _():
        for a in range(2):
            arrive(arrived[a].at[0], arr_recv.at[a, 0])

    for a in range(2):
        for d in far_first:
            remote(
                arrived[a].at[0], hub_kv.at[a, me], hub_sem.at[0], hub_sem.at[1], (rank, peer(d))
            ).start()
        hub_kv[a, me] = arrived[a][0]

    def back_copy():
        return remote(prev_part, prev_land, back_sem.at[0], back_sem.at[1], prev_dev)

    late0 = outer_prev & has_far & (lax.rem(rank, 2) == 0)
    early_back = (
        has_prev & jnp.logical_not(late0) & jnp.logical_not(has_far)
    )

    def near_first():
        @pl.when(has_prev)
        def _():
            arrive(kv_prev, prev_sem.at[1])

        near(0, 0, n_head)

    @pl.when(jnp.logical_not(late0))
    def _():
        near_first()

    @pl.when(early_back)
    def _():
        back_copy().start()

    def far_copy(a, d):
        return remote(
            far_send.at[a, peer(d)],
            far_kv.at[a, me],
            far_sem.at[0],
            far_sem.at[1 if d == 1 else 2 + a],
            (rank, peer(d)),
        )

    def fill_far(buf, a, p):
        for i in range(here_far):
            buf[a, p, i] = arrived[a][owner[p * here_far + i]]

    @pl.when(has_far)
    def _():
        for a in range(2):

            def arr_wait(o, c):
                arrive(arrived[a].at[o], arr_recv.at[a, o])
                return c

            lax.fori_loop(1, rank - 1, arr_wait, 0)
            for d in far_first:
                fill_far(far_send, a, peer(d))
                far_copy(a, d).start()
            fill_far(far_kv, a, me)

    def red_copy(c, k):
        return remote(
            far_part.at[k, c], far_land.at[me, c], red_send.at[0], red_recv.at[c], (rank, k)
        )

    def far_step(k):
        for j in range(per):
            total = dq_acc[k, j]
            for f in range(n_far):
                i = j * n_far + f
                kind = kind_tab[NEAR + f, first + me * per + j]
                dq, dk, dv = grads(k, j, far_kv[0, k, i], far_kv[1, k, i], kind > 0)
                total += dq
                for u, terms in enumerate((dk, dv)):
                    for b in range(cuts):
                        far_part[k, u * cuts + b, i] = terms[b * piece : (b + 1) * piece]
            dq_acc[k, j] = total

    @pl.when(has_far)
    def _():
        far_step(me)

    arrive(hub_kv.at[:, pl.ds(0, others)], hub_sem.at[1])

    pairs = n_head // 2
    tens = [2 * i for i in range(1, pairs)]

    def hred_copy(d):
        slot = 0 if d == 1 else d // 2
        return remote(
            hub_part.at[peer(d)], hub_land.at[slot], hred_sem.at[0], hred_sem.at[1], (rank, peer(d))
        )

    def pair_copy(d):
        return remote(
            hub_part.at[peer(d + 1)],
            hub_pair.at[d // 2],
            pair_sem.at[0],
            pair_sem.at[1],
            (rank, peer(1)),
        )

    def hub_step(k):
        for j in range(per):
            kind = kind_tab[NEAR - 1, first + me * per + j]
            dq, dk, dv = grads(k, j, hub_kv[0, k], hub_kv[1, k], kind > 0)
            dq_acc[k, j] += dq
            for u, terms in enumerate((dk, dv)):
                if j == 0:
                    hub_part[k, u] = terms
                else:
                    hub_part[k, u] += terms

    for d in tens:
        hub_step(peer(d + 1))
        pair_copy(d).start()
    for d in tens:
        hub_step(peer(d))
    arrive(hub_pair.at[pl.ds(1, pairs - 1)], pair_sem.at[1])
    for d in tens:
        hub_part[peer(d)] += hub_pair[d // 2]
        hred_copy(d).start()

    hub_step(peer(1))
    hred_copy(1).start()

    @pl.when(has_far)
    def _():
        for a in range(2):
            arrive(far_kv.at[a, pl.ds(0, others - 1)], far_sem.at[2 + a])

        for d in across:
            far_step(peer(d))
            red_copy(0, peer(d)).start()
        for c in range(1, chunks):
            for d in across:
                red_copy(c, peer(d)).start()
        arrive(far_kv.at[:, 0], far_sem.at[1])
        far_step(peer(1))
        for c in range(chunks):
            red_copy(c, peer(1)).start()


    stages = tree_recv.shape[0]

    def tree_copy(i):
        return remote(
            hub_sum, hub_tree.at[i], tree_send.at[0], tree_recv.at[i], (rank - 2**i, me)
        )

    def tree_up(i):
        if i < stages:

            @pl.when(lax.rem(rank, 2 ** (i + 1)) == 2**i)
            def _():
                tree_copy(i).start()

    def tree_take(i):
        if i < stages:

            @pl.when((lax.rem(rank, 2 ** (i + 1)) == 0) & (rank + 2**i < n_ctx))
            def _():
                arrive(hub_tree.at[i], tree_recv.at[i])
                hub_sum[...] += hub_tree[i]

    def ret_copy(c, o):
        return remote(part.at[o, c], ret.at[c, rank], ret_send.at[o], ret_recv.at[c, rank], (o, me))

    sources = [(peer(d), far_land) for d in range(1, n_head)] + [(me, far_part)]

    def reduce(c):
        @pl.when(has_far)
        def _():
            reduce_live(c)

    def reduce_live(c):
        arrive(far_land.at[pl.ds(0, others), c], red_recv.at[c])

        def send_part(o, carry):
            terms = jnp.zeros((piece, width), f32)
            for p, buf in sources:
                for i in range(here_far):
                    mine = owner[p * here_far + i] == o
                    terms += jnp.where(mine, buf[p, c, i], 0.0)
            part[o, c] = terms
            ret_copy(c, o).start()
            return carry

        lax.fori_loop(1, rank - 1, send_part, 0)

    @pl.when(late0)
    def _():
        near_first()

    hub_step(me)
    arrive(hub_land, hred_sem.at[1])
    hub_sum[...] = sum((hub_land[i] for i in range(pairs)), hub_part[me])
    tree_up(0)
    reduce(0)
    @pl.when(jnp.logical_not(lends))
    def _():
        tree_take(0)
        tree_up(1)

    finish(0, half)
    reduce(1)
    finish(half, n_head)
    for c in range(2, chunks):
        reduce(c)

    @pl.when(has_prev & jnp.logical_not((late0 & lends) | early_back))
    def _():
        back_copy().start()

    @pl.when(lends)
    def _():
        tree_take(0)
        tree_up(1)

    for i in range(1, stages):
        tree_take(i)
        tree_up(i + 1)

    @pl.when(late0 & lends)
    def _():
        back_copy().start()

    def last_copy():
        return remote(hub_sum, hub_last.at[me], last_sem.at[0], last_sem.at[1], (rank, 0))

    @pl.when((rank == 0) & (me > 0))
    def _():
        last_copy().start()

    def blk_copy(c, p):
        return remote(
            blk_part.at[p, c], blk_land.at[me, c], blk_send.at[0], blk_recv.at[c], (rank, p)
        )

    @pl.when(lends)
    def _():
        blk_part[...] = jnp.zeros_like(blk_part)
        for c in range(chunks):

            def take_part(s, carry):
                arrive(ret.at[c, s], ret_recv.at[c, s])
                for i in range(blocks):
                    blk_part[i // per, c, i % per] += jnp.where(want[s] == i, ret[c, s], 0.0)
                return carry

            lax.fori_loop(rank + 2, n_ctx, take_part, 0)
            for d in far_first:
                blk_copy(c, peer(d)).start()

    @pl.when(has_next)
    def _():
        arrive(prev_land, back_sem.at[1])
        for k in range(n_head):
            for u in range(2):
                own_acc[u, k, per - 1] += prev_land[k, u]

    @pl.when((rank == 0) & (me == 0))
    def _():
        for u in range(2):
            own_acc[u, 0, 0] += hub_sum[u]
        arrive(hub_last.at[pl.ds(0, others)], last_sem.at[1])
        for k in range(1, n_head):
            for u in range(2):
                own_acc[u, k, 0] += hub_last[k, u]

    @pl.when(lends)
    def _():
        for c in range(chunks):
            u, at = c // cuts, pl.ds(c % cuts * piece, piece)
            own_acc[u, me, :, at] += blk_part[me, c]
            arrive(blk_land.at[pl.ds(0, others), c], blk_recv.at[c])
            for d in range(1, n_head):
                own_acc[u, peer(d), :, at] += blk_land[peer(d), c]

    for u, out in ((0, dk_out), (1, dv_out)):
        for h in range(n_head):
            terms = own_acc[u, h].reshape(rows, width)
            wide[pl.ds(h, rows, stride=n_head), :] = terms * scale if u == 0 else terms
        out[...] = wide[...].astype(bf16)

    def sent_block(s, c):
        arrive(outgoing.at[:, s], arr_send.at[s])
        return c

    lax.fori_loop(jnp.where(rank == 0, 1, rank + 2), n_ctx, sent_block, 0)

    def sent_part(o, c):
        arrive(part.at[o], ret_send.at[o])
        return c

    lax.fori_loop(1, rank - 1, sent_part, 0)
    arrive(stat_land.at[:, pl.ds(0, others)], stat_sem.at[0])
    arrive(hub_kv.at[:, pl.ds(0, others)], hub_sem.at[0])
    arrive(hub_land, hred_sem.at[0])
    arrive(hub_pair.at[pl.ds(1, pairs - 1)], pair_sem.at[0])

    @pl.when(has_far)
    def _():
        arrive(far_kv.at[:, pl.ds(0, others)], far_sem.at[0])
        arrive(far_land.at[pl.ds(0, others)], red_send.at[0])

    @pl.when((rank == 0) & (me == 0))
    def _():
        arrive(hub_kv.at[:, pl.ds(0, others)], kv_sem.at[0])

    @pl.when(lends)
    def _():
        arrive(kv_own.at[:, pl.ds(0, others)], kv_sem.at[0])
        arrive(blk_land.at[pl.ds(0, others)], blk_send.at[0])

    @pl.when(rank > 0)
    def _():
        arrive(hub_sum, tree_send.at[0])

    @pl.when((rank == 0) & (me > 0))
    def _():
        arrive(hub_sum, last_sem.at[0])

    @pl.when(has_next)
    def _():
        prev_copy().wait_send()

    @pl.when(has_prev)
    def _():
        back_copy().wait_send()


def tail(dq_in, dk_in, dv_in, dq_out, dk_out, dv_out, stores):
    n_head, per, block, heads, _ = dq_in.shape
    routes = [
        (dq_in.at[k, j], dq_out.at[pl.ds(j * block, block), pl.ds(k * heads, heads)])
        for k in range(n_head)
        for j in range(per)
    ]
    routes += [(dk_in, dk_out), (dv_in, dv_out)]
    copies = [
        pltpu.make_async_copy(source, target, stores.at[i])
        for i, (source, target) in enumerate(routes)
    ]
    for copy in copies:
        copy.start()
    for copy in copies:
        copy.wait()


def shards(
    n_ctx,
    n_head,
    queries,
    key_states,
    value_states,
    out_grad,
    log_sums,
    row_deltas,
    block_pairs,
    pair_kinds,
):
    rows, all_heads, width = queries.shape
    heads = all_heads // n_head
    n_slot = block_pairs.shape[1]
    n_far = n_slot - NEAR
    per = rows // BLOCK
    blocks = per * n_head
    lanes = BLOCK * heads
    n_far_here = per * n_far
    stages = (n_ctx - 1).bit_length()
    bf16, f32 = jnp.bfloat16, jnp.float32
    flat = (rows * n_head, width)
    term = (BLOCK, width)
    piece = (BLOCK // CUTS, width)
    chunks = 2 * CUTS
    vmem = pl.BlockSpec(memory_space=pltpu.VMEM)
    smem = pl.BlockSpec(memory_space=pltpu.SMEM)
    anywhere = pl.BlockSpec(memory_space=pl.ANY)
    dma = pltpu.SemaphoreType.DMA
    raw = pltpu.VMEM((n_head, per, BLOCK, heads, width), bf16)
    rolled = pltpu.VMEM((n_head, per, lanes, width), bf16)
    dq, dk, dv = pl.pallas_call(
        partial(kernel, n_ctx, n_head, n_slot),
        out_shape=(raw, pltpu.VMEM(flat, bf16), pltpu.VMEM(flat, bf16)),
        in_specs=[smem, smem, anywhere, anywhere, vmem, vmem, vmem, vmem],
        out_specs=(vmem, vmem, vmem),
        scratch_shapes=[
            pltpu.VMEM(flat, f32),
            pltpu.VMEM((2, n_head, per) + term, bf16),
            pltpu.VMEM((blocks,) + term, bf16),
            pltpu.VMEM((blocks,) + term, bf16),
            pltpu.VMEM((2, n_head) + term, bf16),
            pltpu.VMEM((2, n_ctx) + term, bf16),
            pltpu.VMEM((n_ctx,) + term, bf16),
            pltpu.VMEM((n_ctx,) + term, bf16),
            pltpu.VMEM((2, n_head, n_far_here) + term, bf16),
            pltpu.VMEM((2, n_head, n_far_here) + term, bf16),
            pltpu.VMEM((2, n_head) + term, bf16),
            raw,
            raw,
            rolled,
            rolled,
            pltpu.VMEM((2, n_head, heads, rows), f32),
            pltpu.VMEM((per, 2 * n_head, lanes), f32),
            pltpu.VMEM((n_head, per, lanes, width), f32),
            pltpu.VMEM((2, n_head, per) + term, f32),
            pltpu.VMEM((n_head, 2) + term, f32),
            pltpu.VMEM((n_head, 2) + term, f32),
            pltpu.VMEM((n_head, chunks, n_far_here) + piece, f32),
            pltpu.VMEM((n_head, chunks, n_far_here) + piece, f32),
            pltpu.VMEM((n_head, 2) + term, f32),
            pltpu.VMEM((n_head // 2, 2) + term, f32),
            pltpu.VMEM((n_head // 2, 2) + term, f32),
            pltpu.VMEM((2,) + term, f32),
            pltpu.VMEM((stages, 2) + term, f32),
            pltpu.VMEM((n_head, 2) + term, f32),
            pltpu.VMEM((n_ctx, chunks) + piece, f32),
            pltpu.VMEM((chunks, n_ctx) + piece, f32),
            pltpu.VMEM((n_head, chunks, per) + piece, f32),
            pltpu.VMEM((n_head, chunks, per) + piece, f32),
            pltpu.SMEM((n_ctx,), jnp.int32),
            pltpu.SMEM((blocks * n_far,), jnp.int32),
            dma((2,)),
            dma((3,)),
            dma((2,)),
            dma((2,)),
            dma((n_ctx,)),
            dma((2, n_ctx)),
            dma((4,)),
            dma((2,)),
            dma((2,)),
            dma((2,)),
            dma((2,)),
            dma((1,)),
            dma((stages,)),
            dma((2,)),
            dma((1,)),
            dma((chunks,)),
            dma((n_ctx,)),
            dma((chunks, n_ctx)),
            dma((1,)),
            dma((chunks,)),
            pltpu.SemaphoreType.REGULAR,
        ],
        compiler_params=pltpu.CompilerParams(
            collective_id=0, has_side_effects=True, vmem_limit_bytes=60 * 1024 * 1024
        ),
    )(
        block_pairs.T,
        pair_kinds.T,
        queries,
        out_grad,
        key_states.reshape(flat),
        value_states.reshape(flat),
        log_sums,
        row_deltas,
    )
    dq, dk, dv = pl.pallas_call(
        tail,
        out_shape=(
            jax.ShapeDtypeStruct(queries.shape, bf16),
            jax.ShapeDtypeStruct(flat, bf16),
            jax.ShapeDtypeStruct(flat, bf16),
        ),
        in_specs=[vmem] * 3,
        out_specs=(anywhere,) * 3,
        scratch_shapes=[dma((n_head * per + 2,))],
    )(*(pltpu.with_memory_space_constraint(x, pltpu.VMEM) for x in (dq, dk, dv)))
    return dq, dk.reshape(key_states.shape), dv.reshape(value_states.shape)


def solution(mesh):
    tokens = P(("ctx", "head"), None, None)
    stats = P("head", "ctx")
    return jax.shard_map(
        partial(shards, mesh.shape["ctx"], mesh.shape["head"]),
        mesh=mesh,
        in_specs=(tokens, tokens, tokens, tokens, stats, stats, P(), P()),
        out_specs=(tokens, tokens, tokens),
        check_vma=False,
    )
```

```python
from functools import partial

import jax
import jax.numpy as jnp
from jax import lax
from jax.experimental import pallas as pl
from jax.experimental.pallas import tpu as pltpu
from jax.sharding import PartitionSpec as P

BLOCK = 64
NEAR = 3
CUTS = 2
MESH = pl.DeviceIdType.MESH
NT = (((1,), (1,)), ((), ()))
TN = (((0,), (0,)), ((), ()))


def tile_grads(keys, values, q, g, log_row, delta_row, live, scale):
    scores = lax.dot_general(keys, q, NT, preferred_element_type=jnp.float32) * scale
    weights = jnp.where(live, jnp.exp(scores - log_row), 0.0)
    prob_grad = lax.dot_general(values, g, NT, preferred_element_type=jnp.float32)
    dscore = (weights * (prob_grad - delta_row)).astype(jnp.bfloat16)
    dv = jnp.dot(weights.astype(jnp.bfloat16), g, preferred_element_type=jnp.float32)
    dk = jnp.dot(dscore, q, preferred_element_type=jnp.float32)
    dq = lax.dot_general(dscore, keys, TN, preferred_element_type=jnp.float32)
    return dq, dk, dv


def kernel(
    n_ctx,
    n_head,
    n_slot,
    pair_tab,
    kind_tab,
    q_hbm,
    g_hbm,
    k_ref,
    v_ref,
    log_ref,
    delta_ref,
    dq_buf,
    dk_out,
    dv_out,
    wide,
    kv_own,
    k_loc,
    v_loc,
    kv_prev,
    outgoing,
    k_arrived,
    v_arrived,
    far_send,
    far_kv,
    hub_kv,
    q_raw,
    g_raw,
    q_flat,
    g_flat,
    stat_land,
    stat_rows,
    dq_acc,
    own_acc,
    prev_part,
    prev_land,
    far_part,
    far_land,
    hub_part,
    hub_land,
    hub_pair,
    hub_sum,
    hub_tree,
    hub_last,
    part,
    ret,
    blk_part,
    blk_land,
    want,
    owner,
    load_sem,
    kv_sem,
    stat_sem,
    prev_sem,
    arr_send,
    arr_recv,
    far_sem,
    hub_sem,
    back_sem,
    hred_sem,
    pair_sem,
    tree_send,
    tree_recv,
    last_sem,
    red_send,
    red_recv,
    ret_send,
    ret_recv,
    blk_send,
    blk_recv,
    ready,
):
    kv_loc, arrived = (k_loc, v_loc), (k_arrived, v_arrived)
    rank = lax.axis_index("ctx")
    me = lax.axis_index("head")
    rows = q_hbm.shape[0]
    width = q_hbm.shape[2]
    heads = q_hbm.shape[1] // n_head
    per = rows // BLOCK
    blocks = per * n_head
    lanes = BLOCK * heads
    n_far = n_slot - NEAR
    here_far = per * n_far
    chunks, piece = part.shape[1], part.shape[2]
    cuts = BLOCK // piece
    others = n_head - 1
    scale = width ** (-0.5)
    first = rank * blocks
    bf16, f32 = jnp.bfloat16, jnp.float32

    def peer(d):
        return lax.rem(me // 2 + d // 2, n_head // 2) * 2 + lax.rem(
            lax.rem(me, 2) + lax.rem(d, 2), 2
        )

    def arrive(ref, sem):
        pltpu.make_async_copy(ref, ref, sem).wait()

    def remote(source, target, send, recv, device):
        return pltpu.make_async_remote_copy(
            src_ref=source,
            dst_ref=target,
            send_sem=send,
            recv_sem=recv,
            device_id=device,
            device_id_type=MESH,
        )

    far_first = list(range(2, n_head)) + [1]
    across = far_first[:-1]
    has_prev = (rank > 0) | (me > 0)
    has_next = (rank < n_ctx - 1) | (me < n_head - 1)
    prev_dev = (jnp.where(me > 0, rank, rank - 1), jnp.where(me > 0, me - 1, n_head - 1))
    next_dev = (
        jnp.where(me < n_head - 1, rank, rank + 1),
        jnp.where(me < n_head - 1, me + 1, 0),
    )
    outer_prev = (me == 0) & (rank > 0)
    outer_next = (me == n_head - 1) & (rank < n_ctx - 1)
    lends = (rank > 0) & (rank < n_ctx - 2)
    has_far = rank > 2

    barrier = pltpu.get_barrier_semaphore()
    for d in range(1, n_head):
        pl.semaphore_signal(barrier, inc=1, device_id=(rank, peer(d)), device_id_type=MESH)

    def greet(s, c):
        pl.semaphore_signal(barrier, inc=1, device_id=(s, me), device_id_type=MESH)
        return c

    lax.fori_loop(rank + 1, n_ctx, greet, 0)

    @pl.when(outer_next)
    def _():
        pl.semaphore_signal(barrier, inc=1, device_id=next_dev, device_id_type=MESH)

    for u, (source, raw) in enumerate(((q_hbm, q_raw), (g_hbm, g_raw))):
        for k in range(n_head):
            for j in range(per):
                pltpu.make_async_copy(
                    source.at[pl.ds(j * BLOCK, BLOCK), pl.ds(k * heads, heads)],
                    raw.at[k, j],
                    load_sem.at[u],
                ).start()

    def wanted_by(s, c):
        best = jnp.int32(0)
        for i in range(blocks):
            at = s * blocks + i
            for j in range(NEAR, n_slot):
                local = pair_tab[j, at] - first
                named = (kind_tab[j, at] > 0) & (local >= 0) & (local < blocks)
                best = jnp.where(named, jnp.maximum(best, local), best)
        want[s] = best
        return c

    @pl.when(lends)
    def _():
        lax.fori_loop(rank + 2, n_ctx, wanted_by, 0)

    for i in range(blocks):
        for f in range(n_far):
            at = first + i
            owner[i * n_far + f] = jnp.where(
                kind_tab[NEAR + f, at] > 0, lax.div(pair_tab[NEAR + f, at], blocks), rank
            )

    @pl.when(jnp.logical_not(has_prev))
    def _():
        kv_prev[...] = jnp.zeros_like(kv_prev)

    for at, source in enumerate((k_ref, v_ref)):
        wide[...] = source[...].astype(f32)
        for h in range(n_head):
            head_rows = wide[pl.ds(h, rows, stride=n_head), :]
            kv_own[at, h] = head_rows.reshape(per, BLOCK, width).astype(bf16)

    pl.semaphore_wait(barrier, others + rank + outer_prev.astype(jnp.int32))

    def answer(o, c):
        pl.semaphore_signal(ready, inc=1, device_id=(o, me), device_id_type=MESH)
        return c

    lax.fori_loop(0, rank, answer, 0)

    @pl.when(outer_prev)
    def _():
        pl.semaphore_signal(ready, inc=1, device_id=prev_dev, device_id_type=MESH)

    def await_ready():
        @pl.when(rank < n_ctx - 1)
        def _():
            pl.semaphore_wait(ready, n_ctx - 1 - rank + outer_next.astype(jnp.int32))

    def kv_copy(a, p):
        return remote(
            kv_own.at[a, p],
            kv_loc[a].at[pl.ds(me * per, per)],
            kv_sem.at[0],
            kv_sem.at[1 + a],
            (rank, p),
        )

    def first_copy(a, p):
        return remote(
            kv_own.at[a, p, 0], kv_loc[a].at[0], kv_sem.at[0], kv_sem.at[1 + a], (rank, p)
        )

    def stat_copy(u, p):
        return remote(
            (log_ref, delta_ref)[u].at[:, pl.ds(pl.multiple_of(p * rows, rows), rows)],
            stat_land.at[u, me],
            stat_sem.at[0],
            stat_sem.at[1],
            (rank, p),
        )

    def prev_copy():
        return remote(
            kv_own.at[:, :, per - 1], kv_prev, prev_sem.at[0], prev_sem.at[1], next_dev
        )

    @pl.when((rank == 0) & (me == 0))
    def _():
        for a in range(2):
            for d in far_first:
                first_copy(a, peer(d)).start()
            kv_loc[a][0] = kv_own[a, 0, 0]

    for u in range(2):
        for d in far_first:
            stat_copy(u, peer(d)).start()

    @pl.when(lends)
    def _():
        for a in range(2):
            for d in far_first:
                kv_copy(a, peer(d)).start()
        for a in range(2):
            kv_loc[a][pl.ds(me * per, per)] = kv_own[a, me]

    for u, source in enumerate((log_ref, delta_ref)):
        stat_land[u, me] = source[:, pl.ds(pl.multiple_of(me * rows, rows), rows)]

    def arr_copy(a, s):
        return remote(
            outgoing.at[a, s], arrived[a].at[rank], arr_send.at[s], arr_recv.at[a, rank], (s, me)
        )

    @pl.when(rank == 0)
    def _():
        @pl.when(me > 0)
        def _():
            for a in range(2):
                arrive(kv_loc[a].at[0], kv_sem.at[1 + a])

        await_ready()

        def send_first(i, c):
            s = n_ctx - 1 - i
            for a in range(2):
                outgoing[a, s] = kv_loc[a][0]
                arr_copy(a, s).start()
            return c

        lax.fori_loop(0, n_ctx - 1, send_first, 0)
        for a in range(2):
            arrived[a][0] = kv_loc[a][0]
        prev_copy().start()

    def send_block(a):
        def send(i, c):
            s = n_ctx - 1 - i
            outgoing[a, s] = kv_loc[a][want[s]]
            arr_copy(a, s).start()
            return c

        lax.fori_loop(0, n_ctx - 2 - rank, send, 0)

    def lend(a):
        @pl.when(lends)
        def _():
            arrive(kv_loc[a].at[pl.ds(0, others * per)], kv_sem.at[1 + a])
            if a == 0:
                await_ready()
            send_block(a)
            arrived[a][rank] = kv_loc[a][0]
            if a == 1:
                prev_copy().start()

    lend(0)

    @pl.when(rank >= n_ctx - 2)
    def _():
        await_ready()
        for a in range(2):
            arrived[a][rank] = kv_own[a, 0, 0]

        @pl.when(has_next)
        def _():
            prev_copy().start()

    arrive(stat_land.at[:, pl.ds(0, others)], stat_sem.at[1])
    spread = (
        lax.broadcasted_iota(jnp.int32, (BLOCK, lanes), 1) // heads
        == lax.broadcasted_iota(jnp.int32, (BLOCK, lanes), 0)
    ).astype(bf16)
    own_row = lax.broadcasted_iota(jnp.int32, (heads, lanes), 1) % heads == lax.broadcasted_iota(
        jnp.int32, (heads, lanes), 0
    )
    stats = stat_land[...].reshape(2 * n_head * heads, rows)
    high = stats.astype(bf16)
    rest = stats - high.astype(f32)
    mid = rest.astype(bf16)
    low = (rest - mid.astype(f32)).astype(bf16)
    for j in range(per):
        at = slice(j * BLOCK, (j + 1) * BLOCK)
        by_lane = sum(
            jnp.dot(part_of[:, at], spread, preferred_element_type=f32)
            for part_of in (high, mid, low)
        ).reshape(2 * n_head, heads, lanes)
        stat_rows[j] = jnp.sum(jnp.where(own_row[None], by_lane, 0.0), axis=1)

    key_row = lax.broadcasted_iota(jnp.int32, (2 * BLOCK, lanes), 0)
    causal = (key_row >= BLOCK) | (
        key_row <= lax.broadcasted_iota(jnp.int32, (2 * BLOCK, lanes), 1) // heads
    )
    pair_row = lax.broadcasted_iota(jnp.int32, (2 * BLOCK, 1), 0)

    def grads(k, j, keys, values, live):
        return tile_grads(
            keys,
            values,
            q_flat[k, j],
            g_flat[k, j],
            stat_rows[j, pl.ds(k, 1)],
            stat_rows[j, pl.ds(n_head + k, 1)],
            live,
            scale,
        )

    def finish(lo, hi):
        def each(k, c):
            for j in range(per):
                total = dq_acc[k, j] * scale
                dq_buf[k, j] = total.reshape(BLOCK, heads, width).astype(bf16)
            return c

        lax.fori_loop(lo, hi, each, 0)

    arrive(q_raw, load_sem.at[0])
    arrive(g_raw, load_sem.at[1])

    def flatten(t, c):
        k, j = t // per, lax.rem(t, per)
        for raw, flat in ((q_raw, q_flat), (g_raw, g_flat)):
            flat[k, j] = raw[k, j].astype(f32).reshape(lanes, width).astype(bf16)
        return c

    lax.fori_loop(0, n_head * per, flatten, 0)

    own_acc[...] = jnp.zeros_like(own_acc)
    dq_acc[:, 0] = jnp.zeros((n_head, lanes, width), f32)

    def near(j, lo, hi):
        prev_kind = kind_tab[1, first + me * per + j]
        near_live = causal & (jnp.where(pair_row < BLOCK, 1, prev_kind) > 0)

        def near_step(k, c):
            keys, values = (
                jnp.concatenate(
                    [kv_own[a, k, j], kv_prev[a, k] if j == 0 else kv_own[a, k, j - 1]], axis=0
                )
                for a in range(2)
            )
            dq, dk, dv = grads(k, j, keys, values, near_live)
            dq_acc[k, j] = dq if j else dq_acc[k, j] + dq
            for u, terms in enumerate((dk, dv)):
                own_acc[u, k, j] += terms[:BLOCK]
                if j == 0:
                    prev_part[k, u] = terms[BLOCK:]
                else:
                    own_acc[u, k, j - 1] += terms[BLOCK:]
            return c

        lax.fori_loop(lo, hi, near_step, 0, unroll=2)

    half = n_head // 2

    lend(1)
    for j in range(1, per):
        near(j, 0, n_head)

    @pl.when(rank > 0)
    def _():
        for a in range(2):
            arrive(arrived[a].at[0], arr_recv.at[a, 0])

    for a in range(2):
        for d in far_first:
            remote(
                arrived[a].at[0], hub_kv.at[a, me], hub_sem.at[0], hub_sem.at[1], (rank, peer(d))
            ).start()
        hub_kv[a, me] = arrived[a][0]

    def back_copy():
        return remote(prev_part, prev_land, back_sem.at[0], back_sem.at[1], prev_dev)

    late0 = outer_prev & has_far & (lax.rem(rank, 2) == 0)
    early_back = (
        has_prev & jnp.logical_not(late0) & jnp.logical_not(has_far)
    )

    def near_first():
        @pl.when(has_prev)
        def _():
            arrive(kv_prev, prev_sem.at[1])

        near(0, 0, n_head)

    @pl.when(jnp.logical_not(late0))
    def _():
        near_first()

    @pl.when(early_back)
    def _():
        back_copy().start()

    def far_copy(a, d):
        return remote(
            far_send.at[a, peer(d)],
            far_kv.at[a, me],
            far_sem.at[0],
            far_sem.at[1 if d == 1 else 2 + a],
            (rank, peer(d)),
        )

    def fill_far(buf, a, p):
        for i in range(here_far):
            buf[a, p, i] = arrived[a][owner[p * here_far + i]]

    @pl.when(has_far)
    def _():
        for a in range(2):

            def arr_wait(o, c):
                arrive(arrived[a].at[o], arr_recv.at[a, o])
                return c

            lax.fori_loop(1, rank - 1, arr_wait, 0)
            for d in far_first:
                fill_far(far_send, a, peer(d))
                far_copy(a, d).start()
            fill_far(far_kv, a, me)

    def red_copy(c, k):
        return remote(
            far_part.at[k, c], far_land.at[me, c], red_send.at[0], red_recv.at[c], (rank, k)
        )

    def far_step(k):
        for j in range(per):
            total = dq_acc[k, j]
            for f in range(n_far):
                i = j * n_far + f
                kind = kind_tab[NEAR + f, first + me * per + j]
                dq, dk, dv = grads(k, j, far_kv[0, k, i], far_kv[1, k, i], kind > 0)
                total += dq
                for u, terms in enumerate((dk, dv)):
                    for b in range(cuts):
                        far_part[k, u * cuts + b, i] = terms[b * piece : (b + 1) * piece]
            dq_acc[k, j] = total

    @pl.when(has_far)
    def _():
        far_step(me)

    arrive(hub_kv.at[:, pl.ds(0, others)], hub_sem.at[1])

    pairs = n_head // 2
    tens = [2 * i for i in range(1, pairs)]

    def hred_copy(d):
        slot = 0 if d == 1 else d // 2
        return remote(
            hub_part.at[peer(d)], hub_land.at[slot], hred_sem.at[0], hred_sem.at[1], (rank, peer(d))
        )

    def pair_copy(d):
        return remote(
            hub_part.at[peer(d + 1)],
            hub_pair.at[d // 2],
            pair_sem.at[0],
            pair_sem.at[1],
            (rank, peer(1)),
        )

    def hub_step(k):
        for j in range(per):
            kind = kind_tab[NEAR - 1, first + me * per + j]
            dq, dk, dv = grads(k, j, hub_kv[0, k], hub_kv[1, k], kind > 0)
            dq_acc[k, j] += dq
            for u, terms in enumerate((dk, dv)):
                if j == 0:
                    hub_part[k, u] = terms
                else:
                    hub_part[k, u] += terms

    for d in tens:
        hub_step(peer(d + 1))
        pair_copy(d).start()
    for d in tens:
        hub_step(peer(d))
    arrive(hub_pair.at[pl.ds(1, pairs - 1)], pair_sem.at[1])
    for d in tens:
        hub_part[peer(d)] += hub_pair[d // 2]
        hred_copy(d).start()

    hub_step(peer(1))
    hred_copy(1).start()

    @pl.when(late0 & lends)
    def _():
        near_first()
        back_copy().start()

    @pl.when(has_far)
    def _():
        for a in range(2):
            arrive(far_kv.at[a, pl.ds(0, others - 1)], far_sem.at[2 + a])

        for d in across:
            far_step(peer(d))
            red_copy(0, peer(d)).start()
        for c in range(1, chunks):
            for d in across:
                red_copy(c, peer(d)).start()
        arrive(far_kv.at[:, 0], far_sem.at[1])
        far_step(peer(1))
        for c in range(chunks):
            red_copy(c, peer(1)).start()


    stages = tree_recv.shape[0]

    def tree_copy(i, u):
        return remote(
            hub_sum.at[u],
            hub_tree.at[i, u],
            tree_send.at[0],
            tree_recv.at[i, u],
            (rank - 2**i, me),
        )

    def tree_up(i, u):
        if i < stages:

            @pl.when(lax.rem(rank, 2 ** (i + 1)) == 2**i)
            def _():
                tree_copy(i, u).start()

    def tree_step(i):
        for u in range(2):
            if i < stages:

                @pl.when((lax.rem(rank, 2 ** (i + 1)) == 0) & (rank + 2**i < n_ctx))
                def _():
                    arrive(hub_tree.at[i, u], tree_recv.at[i, u])
                    hub_sum[u] += hub_tree[i, u]

            tree_up(i + 1, u)
            if i == stages - 1:

                @pl.when((rank == 0) & (me > 0))
                def _():
                    last_copy(u).start()

    def last_copy(u):
        return remote(
            hub_sum.at[u], hub_last.at[me, u], last_sem.at[0], last_sem.at[1 + u], (rank, 0)
        )

    def ret_copy(c, o):
        return remote(part.at[o, c], ret.at[c, rank], ret_send.at[o - 1], ret_recv.at[c, rank - NEAR], (o, me))

    sources = [(peer(d), far_land) for d in range(1, n_head)] + [(me, far_part)]

    def reduce(c):
        @pl.when(has_far)
        def _():
            reduce_live(c)

    def reduce_live(c):
        arrive(far_land.at[pl.ds(0, others), c], red_recv.at[c])

        def send_part(o, carry):
            terms = jnp.zeros((piece, width), f32)
            for p, buf in sources:
                for i in range(here_far):
                    mine = owner[p * here_far + i] == o
                    terms += jnp.where(mine, buf[p, c, i], 0.0)
            part[o, c] = terms
            ret_copy(c, o).start()
            return carry

        lax.fori_loop(1, rank - 1, send_part, 0)

    @pl.when(late0 & jnp.logical_not(lends))
    def _():
        near_first()

    hub_step(me)
    arrive(hub_land, hred_sem.at[1])
    hub_sum[...] = sum((hub_land[i] for i in range(pairs)), hub_part[me])
    for u in range(2):
        tree_up(0, u)
    reduce(0)
    @pl.when(jnp.logical_not(lends))
    def _():
        tree_step(0)

    finish(0, half)
    reduce(1)
    finish(half, n_head)
    for c in range(2, chunks):
        reduce(c)

    @pl.when(has_prev & jnp.logical_not((late0 & lends) | early_back))
    def _():
        back_copy().start()

    @pl.when(lends)
    def _():
        tree_step(0)

    for i in range(1, stages):
        tree_step(i)

    def blk_copy(c, p):
        return remote(
            blk_part.at[p, c], blk_land.at[me, c], blk_send.at[0], blk_recv.at[c], (rank, p)
        )

    @pl.when(lends)
    def _():
        blk_part[...] = jnp.zeros_like(blk_part)
        for c in range(chunks):

            def take_part(s, carry):
                arrive(ret.at[c, s], ret_recv.at[c, s - NEAR])
                for i in range(blocks):
                    blk_part[i // per, c, i % per] += jnp.where(want[s] == i, ret[c, s], 0.0)
                return carry

            lax.fori_loop(rank + 2, n_ctx, take_part, 0)
            for d in far_first:
                blk_copy(c, peer(d)).start()

    @pl.when(has_next)
    def _():
        arrive(prev_land, back_sem.at[1])
        for k in range(n_head):
            for u in range(2):
                own_acc[u, k, per - 1] += prev_land[k, u]

    @pl.when((rank == 0) & (me == 0))
    def _():
        for u in range(2):
            own_acc[u, 0, 0] += hub_sum[u]
            arrive(hub_last.at[pl.ds(0, others), u], last_sem.at[1 + u])
            for k in range(1, n_head):
                own_acc[u, k, 0] += hub_last[k, u]

    @pl.when(lends)
    def _():
        for c in range(chunks):
            u, at = c // cuts, pl.ds(c % cuts * piece, piece)
            own_acc[u, me, :, at] += blk_part[me, c]
            arrive(blk_land.at[pl.ds(0, others), c], blk_recv.at[c])
            for d in range(1, n_head):
                own_acc[u, peer(d), :, at] += blk_land[peer(d), c]

    for u, out in ((0, dk_out), (1, dv_out)):
        for h in range(n_head):
            terms = own_acc[u, h].reshape(rows, width)
            wide[pl.ds(h, rows, stride=n_head), :] = terms * scale if u == 0 else terms
        out[...] = wide[...].astype(bf16)

    def sent_block(s, c):
        arrive(outgoing.at[:, s], arr_send.at[s])
        return c

    lax.fori_loop(jnp.where(rank == 0, 1, rank + 2), n_ctx, sent_block, 0)

    def sent_part(o, c):
        arrive(part.at[o], ret_send.at[o - 1])
        return c

    lax.fori_loop(1, rank - 1, sent_part, 0)
    arrive(stat_land.at[:, pl.ds(0, others)], stat_sem.at[0])
    arrive(hub_kv.at[:, pl.ds(0, others)], hub_sem.at[0])
    arrive(hub_land, hred_sem.at[0])
    arrive(hub_pair.at[pl.ds(1, pairs - 1)], pair_sem.at[0])

    @pl.when(has_far)
    def _():
        arrive(far_kv.at[:, pl.ds(0, others)], far_sem.at[0])
        arrive(far_land.at[pl.ds(0, others)], red_send.at[0])

    @pl.when((rank == 0) & (me == 0))
    def _():
        arrive(hub_kv.at[:, pl.ds(0, others)], kv_sem.at[0])

    @pl.when(lends)
    def _():
        arrive(kv_own.at[:, pl.ds(0, others)], kv_sem.at[0])
        arrive(blk_land.at[pl.ds(0, others)], blk_send.at[0])

    @pl.when(rank > 0)
    def _():
        arrive(hub_sum, tree_send.at[0])

    @pl.when((rank == 0) & (me > 0))
    def _():
        arrive(hub_sum, last_sem.at[0])

    @pl.when(has_next)
    def _():
        prev_copy().wait_send()

    @pl.when(has_prev)
    def _():
        back_copy().wait_send()


def tail(dq_in, dk_in, dv_in, dq_out, dk_out, dv_out, stores):
    n_head, per, block, heads, _ = dq_in.shape
    routes = [
        (dq_in.at[k, j], dq_out.at[pl.ds(j * block, block), pl.ds(k * heads, heads)])
        for k in range(n_head)
        for j in range(per)
    ]
    routes += [(dk_in, dk_out), (dv_in, dv_out)]
    copies = [
        pltpu.make_async_copy(source, target, stores.at[i])
        for i, (source, target) in enumerate(routes)
    ]
    for copy in copies:
        copy.start()
    for copy in copies:
        copy.wait()


def shards(
    n_ctx,
    n_head,
    queries,
    key_states,
    value_states,
    out_grad,
    log_sums,
    row_deltas,
    block_pairs,
    pair_kinds,
):
    rows, all_heads, width = queries.shape
    heads = all_heads // n_head
    n_slot = block_pairs.shape[1]
    n_far = n_slot - NEAR
    per = rows // BLOCK
    blocks = per * n_head
    lanes = BLOCK * heads
    n_far_here = per * n_far
    stages = (n_ctx - 1).bit_length()
    bf16, f32 = jnp.bfloat16, jnp.float32
    flat = (rows * n_head, width)
    term = (BLOCK, width)
    piece = (BLOCK // CUTS, width)
    chunks = 2 * CUTS
    vmem = pl.BlockSpec(memory_space=pltpu.VMEM)
    smem = pl.BlockSpec(memory_space=pltpu.SMEM)
    anywhere = pl.BlockSpec(memory_space=pl.ANY)
    dma = pltpu.SemaphoreType.DMA
    raw = pltpu.VMEM((n_head, per, BLOCK, heads, width), bf16)
    rolled = pltpu.VMEM((n_head, per, lanes, width), bf16)
    dq, dk, dv = pl.pallas_call(
        partial(kernel, n_ctx, n_head, n_slot),
        out_shape=(raw, pltpu.VMEM(flat, bf16), pltpu.VMEM(flat, bf16)),
        in_specs=[smem, smem, anywhere, anywhere, vmem, vmem, vmem, vmem],
        out_specs=(vmem, vmem, vmem),
        scratch_shapes=[
            pltpu.VMEM(flat, f32),
            pltpu.VMEM((2, n_head, per) + term, bf16),
            pltpu.VMEM((blocks,) + term, bf16),
            pltpu.VMEM((blocks,) + term, bf16),
            pltpu.VMEM((2, n_head) + term, bf16),
            pltpu.VMEM((2, n_ctx) + term, bf16),
            pltpu.VMEM((n_ctx,) + term, bf16),
            pltpu.VMEM((n_ctx,) + term, bf16),
            pltpu.VMEM((2, n_head, n_far_here) + term, bf16),
            pltpu.VMEM((2, n_head, n_far_here) + term, bf16),
            pltpu.VMEM((2, n_head) + term, bf16),
            raw,
            raw,
            rolled,
            rolled,
            pltpu.VMEM((2, n_head, heads, rows), f32),
            pltpu.VMEM((per, 2 * n_head, lanes), f32),
            pltpu.VMEM((n_head, per, lanes, width), f32),
            pltpu.VMEM((2, n_head, per) + term, f32),
            pltpu.VMEM((n_head, 2) + term, f32),
            pltpu.VMEM((n_head, 2) + term, f32),
            pltpu.VMEM((n_head, chunks, n_far_here) + piece, f32),
            pltpu.VMEM((n_head, chunks, n_far_here) + piece, f32),
            pltpu.VMEM((n_head, 2) + term, f32),
            pltpu.VMEM((n_head // 2, 2) + term, f32),
            pltpu.VMEM((n_head // 2, 2) + term, f32),
            pltpu.VMEM((2,) + term, f32),
            pltpu.VMEM((stages, 2) + term, f32),
            pltpu.VMEM((n_head, 2) + term, f32),
            pltpu.VMEM((n_ctx, chunks) + piece, f32),
            pltpu.VMEM((chunks, n_ctx) + piece, f32),
            pltpu.VMEM((n_head, chunks, per) + piece, f32),
            pltpu.VMEM((n_head, chunks, per) + piece, f32),
            pltpu.SMEM((n_ctx,), jnp.int32),
            pltpu.SMEM((blocks * n_far,), jnp.int32),
            dma((2,)),
            dma((3,)),
            dma((2,)),
            dma((2,)),
            dma((n_ctx,)),
            dma((2, n_ctx - 2)),
            dma((4,)),
            dma((2,)),
            dma((2,)),
            dma((2,)),
            dma((2,)),
            dma((1,)),
            dma((stages, 2)),
            dma((3,)),
            dma((1,)),
            dma((chunks,)),
            dma((n_ctx - NEAR,)),
            dma((chunks, n_ctx - NEAR)),
            dma((1,)),
            dma((chunks,)),
            pltpu.SemaphoreType.REGULAR,
        ],
        compiler_params=pltpu.CompilerParams(
            collective_id=0, has_side_effects=True, vmem_limit_bytes=60 * 1024 * 1024
        ),
    )(
        block_pairs.T,
        pair_kinds.T,
        queries,
        out_grad,
        key_states.reshape(flat),
        value_states.reshape(flat),
        log_sums,
        row_deltas,
    )
    dq, dk, dv = pl.pallas_call(
        tail,
        out_shape=(
            jax.ShapeDtypeStruct(queries.shape, bf16),
            jax.ShapeDtypeStruct(flat, bf16),
            jax.ShapeDtypeStruct(flat, bf16),
        ),
        in_specs=[vmem] * 3,
        out_specs=(anywhere,) * 3,
        scratch_shapes=[dma((n_head * per + 2,))],
    )(*(pltpu.with_memory_space_constraint(x, pltpu.VMEM) for x in (dq, dk, dv)))
    return dq, dk.reshape(key_states.shape), dv.reshape(value_states.shape)


def solution(mesh):
    tokens = P(("ctx", "head"), None, None)
    stats = P("head", "ctx")
    return jax.shard_map(
        partial(shards, mesh.shape["ctx"], mesh.shape["head"]),
        mesh=mesh,
        in_specs=(tokens, tokens, tokens, tokens, stats, stats, P(), P()),
        out_specs=(tokens, tokens, tokens),
        check_vma=False,
    )
```

```python
from functools import partial

import jax
import jax.numpy as jnp
from jax import lax
from jax.experimental import pallas as pl
from jax.experimental.pallas import tpu as pltpu
from jax.sharding import PartitionSpec as P

BLOCK = 64
NEAR = 3
CUTS = 2
MESH = pl.DeviceIdType.MESH
NT = (((1,), (1,)), ((), ()))
TN = (((0,), (0,)), ((), ()))


def tile_grads(keys, values, q, g, log_row, delta_row, live, scale):
    scores = lax.dot_general(keys, q, NT, preferred_element_type=jnp.float32) * scale
    weights = jnp.where(live, jnp.exp(scores - log_row), 0.0)
    prob_grad = lax.dot_general(values, g, NT, preferred_element_type=jnp.float32)
    dscore = (weights * (prob_grad - delta_row)).astype(jnp.bfloat16)
    dv = jnp.dot(weights.astype(jnp.bfloat16), g, preferred_element_type=jnp.float32)
    dk = jnp.dot(dscore, q, preferred_element_type=jnp.float32)
    dq = lax.dot_general(dscore, keys, TN, preferred_element_type=jnp.float32)
    return dq, dk, dv


def kernel(
    n_ctx,
    n_head,
    n_slot,
    pair_tab,
    kind_tab,
    q_hbm,
    g_hbm,
    k_ref,
    v_ref,
    log_ref,
    delta_ref,
    dq_buf,
    dk_out,
    dv_out,
    wide,
    kv_own,
    k_loc,
    v_loc,
    kv_prev,
    outgoing,
    k_arrived,
    v_arrived,
    far_send,
    far_kv,
    hub_kv,
    q_raw,
    g_raw,
    q_flat,
    g_flat,
    stat_land,
    stat_rows,
    dq_acc,
    own_acc,
    prev_part,
    prev_land,
    far_part,
    far_land,
    hub_part,
    hub_land,
    hub_pair,
    hub_sum,
    hub_tree,
    hub_last,
    part,
    ret,
    blk_part,
    blk_land,
    want,
    owner,
    load_sem,
    kv_sem,
    stat_sem,
    prev_sem,
    arr_send,
    arr_recv,
    far_sem,
    hub_sem,
    back_sem,
    hred_sem,
    pair_sem,
    tree_send,
    tree_recv,
    last_sem,
    red_send,
    red_recv,
    ret_send,
    ret_recv,
    blk_send,
    blk_recv,
    ready,
):
    kv_loc, arrived = (k_loc, v_loc), (k_arrived, v_arrived)
    rank = lax.axis_index("ctx")
    me = lax.axis_index("head")
    rows = q_hbm.shape[0]
    width = q_hbm.shape[2]
    heads = q_hbm.shape[1] // n_head
    per = rows // BLOCK
    blocks = per * n_head
    lanes = BLOCK * heads
    n_far = n_slot - NEAR
    here_far = per * n_far
    chunks, piece = part.shape[1], part.shape[2]
    cuts = BLOCK // piece
    others = n_head - 1
    scale = width ** (-0.5)
    first = rank * blocks
    bf16, f32 = jnp.bfloat16, jnp.float32

    def peer(d):
        return lax.rem(me // 2 + d // 2, n_head // 2) * 2 + lax.rem(
            lax.rem(me, 2) + lax.rem(d, 2), 2
        )

    def arrive(ref, sem):
        pltpu.make_async_copy(ref, ref, sem).wait()

    def remote(source, target, send, recv, device):
        return pltpu.make_async_remote_copy(
            src_ref=source,
            dst_ref=target,
            send_sem=send,
            recv_sem=recv,
            device_id=device,
            device_id_type=MESH,
        )

    far_first = list(range(2, n_head)) + [1]
    across = far_first[:-1]
    has_prev = (rank > 0) | (me > 0)
    has_next = (rank < n_ctx - 1) | (me < n_head - 1)
    prev_dev = (jnp.where(me > 0, rank, rank - 1), jnp.where(me > 0, me - 1, n_head - 1))
    next_dev = (
        jnp.where(me < n_head - 1, rank, rank + 1),
        jnp.where(me < n_head - 1, me + 1, 0),
    )
    outer_prev = (me == 0) & (rank > 0)
    outer_next = (me == n_head - 1) & (rank < n_ctx - 1)
    lends = (rank > 0) & (rank < n_ctx - 2)
    has_far = rank > 2

    barrier = pltpu.get_barrier_semaphore()
    for d in range(1, n_head):
        pl.semaphore_signal(barrier, inc=1, device_id=(rank, peer(d)), device_id_type=MESH)

    def greet(s, c):
        pl.semaphore_signal(barrier, inc=1, device_id=(s, me), device_id_type=MESH)
        return c

    lax.fori_loop(rank + 1, n_ctx, greet, 0)

    @pl.when(outer_next)
    def _():
        pl.semaphore_signal(barrier, inc=1, device_id=next_dev, device_id_type=MESH)

    for u, (source, raw) in enumerate(((q_hbm, q_raw), (g_hbm, g_raw))):
        for k in range(n_head):
            for j in range(per):
                pltpu.make_async_copy(
                    source.at[pl.ds(j * BLOCK, BLOCK), pl.ds(k * heads, heads)],
                    raw.at[k, j],
                    load_sem.at[u],
                ).start()

    def wanted_by(s, c):
        best = jnp.int32(0)
        for i in range(blocks):
            at = s * blocks + i
            for j in range(NEAR, n_slot):
                local = pair_tab[j, at] - first
                named = (kind_tab[j, at] > 0) & (local >= 0) & (local < blocks)
                best = jnp.where(named, jnp.maximum(best, local), best)
        want[s] = best
        return c

    @pl.when(lends)
    def _():
        lax.fori_loop(rank + 2, n_ctx, wanted_by, 0)

    for i in range(blocks):
        for f in range(n_far):
            at = first + i
            owner[i * n_far + f] = jnp.where(
                kind_tab[NEAR + f, at] > 0, lax.div(pair_tab[NEAR + f, at], blocks), rank
            )

    @pl.when(jnp.logical_not(has_prev))
    def _():
        kv_prev[...] = jnp.zeros_like(kv_prev)

    for at, source in enumerate((k_ref, v_ref)):
        wide[...] = source[...].astype(f32)
        for h in range(n_head):
            head_rows = wide[pl.ds(h, rows, stride=n_head), :]
            kv_own[at, h] = head_rows.reshape(per, BLOCK, width).astype(bf16)

    pl.semaphore_wait(barrier, others + rank + outer_prev.astype(jnp.int32))

    def answer(o, c):
        pl.semaphore_signal(ready, inc=1, device_id=(o, me), device_id_type=MESH)
        return c

    lax.fori_loop(0, rank, answer, 0)

    @pl.when(outer_prev)
    def _():
        pl.semaphore_signal(ready, inc=1, device_id=prev_dev, device_id_type=MESH)

    def await_ready():
        @pl.when(rank < n_ctx - 1)
        def _():
            pl.semaphore_wait(ready, n_ctx - 1 - rank + outer_next.astype(jnp.int32))

    def kv_copy(a, p):
        return remote(
            kv_own.at[a, p],
            kv_loc[a].at[pl.ds(me * per, per)],
            kv_sem.at[0],
            kv_sem.at[1 + a],
            (rank, p),
        )

    def first_copy(a, p):
        return remote(
            kv_own.at[a, p, 0], kv_loc[a].at[0], kv_sem.at[0], kv_sem.at[1 + a], (rank, p)
        )

    def stat_copy(u, p):
        return remote(
            (log_ref, delta_ref)[u].at[:, pl.ds(pl.multiple_of(p * rows, rows), rows)],
            stat_land.at[u, me],
            stat_sem.at[0],
            stat_sem.at[1],
            (rank, p),
        )

    def prev_copy():
        return remote(
            kv_own.at[:, :, per - 1], kv_prev, prev_sem.at[0], prev_sem.at[1], next_dev
        )

    @pl.when((rank == 0) & (me == 0))
    def _():
        for a in range(2):
            for d in far_first:
                first_copy(a, peer(d)).start()
            kv_loc[a][0] = kv_own[a, 0, 0]

    for u in range(2):
        for d in far_first:
            stat_copy(u, peer(d)).start()

    @pl.when(lends)
    def _():
        for a in range(2):
            for d in far_first:
                kv_copy(a, peer(d)).start()
        for a in range(2):
            kv_loc[a][pl.ds(me * per, per)] = kv_own[a, me]

    for u, source in enumerate((log_ref, delta_ref)):
        stat_land[u, me] = source[:, pl.ds(pl.multiple_of(me * rows, rows), rows)]

    def arr_copy(a, s):
        return remote(
            outgoing.at[a, s], arrived[a].at[rank], arr_send.at[s], arr_recv.at[a, rank], (s, me)
        )

    @pl.when(rank == 0)
    def _():
        @pl.when(me > 0)
        def _():
            for a in range(2):
                arrive(kv_loc[a].at[0], kv_sem.at[1 + a])

        await_ready()

        def send_first(i, c):
            s = n_ctx - 1 - i
            for a in range(2):
                outgoing[a, s] = kv_loc[a][0]
                arr_copy(a, s).start()
            return c

        lax.fori_loop(0, n_ctx - 1, send_first, 0)
        for a in range(2):
            arrived[a][0] = kv_loc[a][0]
        prev_copy().start()

    def send_block(a):
        def send(i, c):
            s = n_ctx - 1 - i
            outgoing[a, s] = kv_loc[a][want[s]]
            arr_copy(a, s).start()
            return c

        lax.fori_loop(0, n_ctx - 2 - rank, send, 0)

    def lend(a):
        @pl.when(lends)
        def _():
            arrive(kv_loc[a].at[pl.ds(0, others * per)], kv_sem.at[1 + a])
            if a == 0:
                await_ready()
            send_block(a)
            arrived[a][rank] = kv_loc[a][0]
            if a == 1:
                prev_copy().start()

    lend(0)

    @pl.when(rank >= n_ctx - 2)
    def _():
        await_ready()
        for a in range(2):
            arrived[a][rank] = kv_own[a, 0, 0]

        @pl.when(has_next)
        def _():
            prev_copy().start()

    arrive(stat_land.at[:, pl.ds(0, others)], stat_sem.at[1])
    spread = (
        lax.broadcasted_iota(jnp.int32, (BLOCK, lanes), 1) // heads
        == lax.broadcasted_iota(jnp.int32, (BLOCK, lanes), 0)
    ).astype(bf16)
    own_row = lax.broadcasted_iota(jnp.int32, (heads, lanes), 1) % heads == lax.broadcasted_iota(
        jnp.int32, (heads, lanes), 0
    )
    stats = stat_land[...].reshape(2 * n_head * heads, rows)
    high = stats.astype(bf16)
    rest = stats - high.astype(f32)
    mid = rest.astype(bf16)
    low = (rest - mid.astype(f32)).astype(bf16)
    for j in range(per):
        at = slice(j * BLOCK, (j + 1) * BLOCK)
        by_lane = sum(
            jnp.dot(part_of[:, at], spread, preferred_element_type=f32)
            for part_of in (high, mid, low)
        ).reshape(2 * n_head, heads, lanes)
        stat_rows[j] = jnp.sum(jnp.where(own_row[None], by_lane, 0.0), axis=1)

    key_row = lax.broadcasted_iota(jnp.int32, (2 * BLOCK, lanes), 0)
    causal = (key_row >= BLOCK) | (
        key_row <= lax.broadcasted_iota(jnp.int32, (2 * BLOCK, lanes), 1) // heads
    )
    pair_row = lax.broadcasted_iota(jnp.int32, (2 * BLOCK, 1), 0)

    def grads(k, j, keys, values, live):
        return tile_grads(
            keys,
            values,
            q_flat[k, j],
            g_flat[k, j],
            stat_rows[j, pl.ds(k, 1)],
            stat_rows[j, pl.ds(n_head + k, 1)],
            live,
            scale,
        )

    def finish(lo, hi):
        def each(k, c):
            for j in range(per):
                total = dq_acc[k, j] * scale
                dq_buf[k, j] = total.reshape(BLOCK, heads, width).astype(bf16)
            return c

        lax.fori_loop(lo, hi, each, 0)

    arrive(q_raw, load_sem.at[0])
    arrive(g_raw, load_sem.at[1])

    def flatten(t, c):
        k, j = t // per, lax.rem(t, per)
        for raw, flat in ((q_raw, q_flat), (g_raw, g_flat)):
            flat[k, j] = raw[k, j].astype(f32).reshape(lanes, width).astype(bf16)
        return c

    lax.fori_loop(0, n_head * per, flatten, 0)

    own_acc[...] = jnp.zeros_like(own_acc)
    dq_acc[:, 0] = jnp.zeros((n_head, lanes, width), f32)

    def near(j, lo, hi):
        prev_kind = kind_tab[1, first + me * per + j]
        near_live = causal & (jnp.where(pair_row < BLOCK, 1, prev_kind) > 0)

        def near_step(k, c):
            keys, values = (
                jnp.concatenate(
                    [kv_own[a, k, j], kv_prev[a, k] if j == 0 else kv_own[a, k, j - 1]], axis=0
                )
                for a in range(2)
            )
            dq, dk, dv = grads(k, j, keys, values, near_live)
            dq_acc[k, j] = dq if j else dq_acc[k, j] + dq
            for u, terms in enumerate((dk, dv)):
                own_acc[u, k, j] += terms[:BLOCK]
                if j == 0:
                    prev_part[k, u] = terms[BLOCK:]
                else:
                    own_acc[u, k, j - 1] += terms[BLOCK:]
            return c

        lax.fori_loop(lo, hi, near_step, 0, unroll=2)

    half = n_head // 2

    lend(1)
    for j in range(1, per):
        near(j, 0, n_head)

    @pl.when(rank > 0)
    def _():
        for a in range(2):
            arrive(arrived[a].at[0], arr_recv.at[a, 0])

    for a in range(2):
        for d in far_first:
            remote(
                arrived[a].at[0], hub_kv.at[a, me], hub_sem.at[0], hub_sem.at[1], (rank, peer(d))
            ).start()
        hub_kv[a, me] = arrived[a][0]

    def back_copy():
        return remote(prev_part, prev_land, back_sem.at[0], back_sem.at[1], prev_dev)

    late0 = outer_prev & has_far & (lax.rem(rank, 2) == 0)
    early_back = (
        has_prev & jnp.logical_not(late0) & jnp.logical_not(has_far)
    )

    def near_first():
        @pl.when(has_prev)
        def _():
            arrive(kv_prev, prev_sem.at[1])

        near(0, 0, n_head)

    @pl.when(jnp.logical_not(late0))
    def _():
        near_first()

    @pl.when(early_back)
    def _():
        back_copy().start()

    def far_copy(a, d):
        return remote(
            far_send.at[a, peer(d)],
            far_kv.at[a, me],
            far_sem.at[0],
            far_sem.at[1 if d == 1 else 2 + a],
            (rank, peer(d)),
        )

    def fill_far(buf, a, p):
        for i in range(here_far):
            buf[a, p, i] = arrived[a][owner[p * here_far + i]]

    @pl.when(has_far)
    def _():
        for a in range(2):

            def arr_wait(o, c):
                arrive(arrived[a].at[o], arr_recv.at[a, o])
                return c

            lax.fori_loop(1, rank - 1, arr_wait, 0)
            for d in far_first:
                fill_far(far_send, a, peer(d))
                far_copy(a, d).start()
            fill_far(far_kv, a, me)

    def red_copy(c, k):
        return remote(
            far_part.at[k, c], far_land.at[me, c], red_send.at[0], red_recv.at[c], (rank, k)
        )

    def far_step(k):
        for j in range(per):
            total = dq_acc[k, j]
            for f in range(n_far):
                i = j * n_far + f
                kind = kind_tab[NEAR + f, first + me * per + j]
                dq, dk, dv = grads(k, j, far_kv[0, k, i], far_kv[1, k, i], kind > 0)
                total += dq
                for u, terms in enumerate((dk, dv)):
                    for b in range(cuts):
                        far_part[k, u * cuts + b, i] = terms[b * piece : (b + 1) * piece]
            dq_acc[k, j] = total

    @pl.when(has_far)
    def _():
        far_step(me)

    arrive(hub_kv.at[:, pl.ds(0, others)], hub_sem.at[1])

    pairs = n_head // 2
    tens = [2 * i for i in range(1, pairs)]

    def hred_copy(d):
        slot = 0 if d == 1 else d // 2
        return remote(
            hub_part.at[peer(d)], hub_land.at[slot], hred_sem.at[0], hred_sem.at[1], (rank, peer(d))
        )

    def pair_copy(d):
        return remote(
            hub_part.at[peer(d + 1)],
            hub_pair.at[d // 2],
            pair_sem.at[0],
            pair_sem.at[1],
            (rank, peer(1)),
        )

    def hub_step(k):
        for j in range(per):
            kind = kind_tab[NEAR - 1, first + me * per + j]
            dq, dk, dv = grads(k, j, hub_kv[0, k], hub_kv[1, k], kind > 0)
            dq_acc[k, j] += dq
            for u, terms in enumerate((dk, dv)):
                if j == 0:
                    hub_part[k, u] = terms
                else:
                    hub_part[k, u] += terms

    for d in tens:
        hub_step(peer(d + 1))
        pair_copy(d).start()
    for d in tens:
        hub_step(peer(d))
    arrive(hub_pair.at[pl.ds(1, pairs - 1)], pair_sem.at[1])
    for d in tens:
        hub_part[peer(d)] += hub_pair[d // 2]
        hred_copy(d).start()

    hub_step(peer(1))
    hred_copy(1).start()

    @pl.when(late0 & lends)
    def _():
        near_first()
        back_copy().start()

    @pl.when(has_far)
    def _():
        for a in range(2):
            arrive(far_kv.at[a, pl.ds(0, others - 1)], far_sem.at[2 + a])

        for d in across:
            far_step(peer(d))
            red_copy(0, peer(d)).start()
        for c in range(1, chunks):
            for d in across:
                red_copy(c, peer(d)).start()
        arrive(far_kv.at[:, 0], far_sem.at[1])
        far_step(peer(1))
        for c in range(chunks):
            red_copy(c, peer(1)).start()


    stages = tree_recv.shape[0]

    def tree_copy(i, u):
        return remote(
            hub_sum.at[u],
            hub_tree.at[i, u],
            tree_send.at[0],
            tree_recv.at[i, u],
            (rank - 2**i, me),
        )

    def tree_up(i, u):
        if i < stages:

            @pl.when(lax.rem(rank, 2 ** (i + 1)) == 2**i)
            def _():
                tree_copy(i, u).start()

    def tree_step(i):
        for u in range(2):
            if i < stages:

                @pl.when((lax.rem(rank, 2 ** (i + 1)) == 0) & (rank + 2**i < n_ctx))
                def _():
                    arrive(hub_tree.at[i, u], tree_recv.at[i, u])
                    hub_sum[u] += hub_tree[i, u]

            tree_up(i + 1, u)
            if i == stages - 1:

                @pl.when((rank == 0) & (me > 0))
                def _():
                    last_copy(u).start()

    def last_copy(u):
        return remote(
            hub_sum.at[u], hub_last.at[me, u], last_sem.at[0], last_sem.at[1 + u], (rank, 0)
        )

    def ret_copy(c, o):
        return remote(part.at[o, c], ret.at[c, rank], ret_send.at[o - 1], ret_recv.at[c, rank - NEAR], (o, me))

    sources = [(peer(d), far_land) for d in range(1, n_head)] + [(me, far_part)]

    def reduce(c):
        @pl.when(has_far)
        def _():
            reduce_live(c)

    def reduce_live(c):
        arrive(far_land.at[pl.ds(0, others), c], red_recv.at[c])

        def send_part(o, carry):
            terms = jnp.zeros((piece, width), f32)
            for p, buf in sources:
                for i in range(here_far):
                    mine = owner[p * here_far + i] == o
                    terms += jnp.where(mine, buf[p, c, i], 0.0)
            part[o, c] = terms
            ret_copy(c, o).start()
            return carry

        lax.fori_loop(1, rank - 1, send_part, 0)

    @pl.when(late0 & jnp.logical_not(lends))
    def _():
        near_first()

    hub_step(me)
    arrive(hub_land, hred_sem.at[1])
    hub_sum[...] = sum((hub_land[i] for i in range(pairs)), hub_part[me])
    for u in range(2):
        tree_up(0, u)
    reduce(0)
    @pl.when(jnp.logical_not(lends))
    def _():
        tree_step(0)

    finish(0, half)
    reduce(1)
    finish(half, n_head)
    for c in range(2, chunks - 1):
        reduce(c)
    @pl.when(lends)
    def _():
        tree_step(0)
        tree_step(1)

    reduce(chunks - 1)

    @pl.when(has_prev & jnp.logical_not((late0 & lends) | early_back))
    def _():
        back_copy().start()


    @pl.when(jnp.logical_not(lends))
    def _():
        tree_step(1)

    for i in range(2, stages):
        tree_step(i)

    def blk_copy(c, p):
        return remote(
            blk_part.at[p, c], blk_land.at[me, c], blk_send.at[0], blk_recv.at[c], (rank, p)
        )

    @pl.when(lends)
    def _():
        blk_part[...] = jnp.zeros_like(blk_part)
        for c in range(chunks):

            def take_part(s, carry):
                arrive(ret.at[c, s], ret_recv.at[c, s - NEAR])
                for i in range(blocks):
                    blk_part[i // per, c, i % per] += jnp.where(want[s] == i, ret[c, s], 0.0)
                return carry

            lax.fori_loop(rank + 2, n_ctx, take_part, 0)
            for d in far_first:
                blk_copy(c, peer(d)).start()

    @pl.when(has_next)
    def _():
        arrive(prev_land, back_sem.at[1])
        for k in range(n_head):
            for u in range(2):
                own_acc[u, k, per - 1] += prev_land[k, u]

    @pl.when((rank == 0) & (me == 0))
    def _():
        for u in range(2):
            own_acc[u, 0, 0] += hub_sum[u]
            arrive(hub_last.at[pl.ds(0, others), u], last_sem.at[1 + u])
            for k in range(1, n_head):
                own_acc[u, k, 0] += hub_last[k, u]

    @pl.when(lends)
    def _():
        for c in range(chunks):
            u, at = c // cuts, pl.ds(c % cuts * piece, piece)
            own_acc[u, me, :, at] += blk_part[me, c]
            arrive(blk_land.at[pl.ds(0, others), c], blk_recv.at[c])
            for d in range(1, n_head):
                own_acc[u, peer(d), :, at] += blk_land[peer(d), c]

    for u, out in ((0, dk_out), (1, dv_out)):
        for h in range(n_head):
            terms = own_acc[u, h].reshape(rows, width)
            wide[pl.ds(h, rows, stride=n_head), :] = terms * scale if u == 0 else terms
        out[...] = wide[...].astype(bf16)

    def sent_block(s, c):
        arrive(outgoing.at[:, s], arr_send.at[s])
        return c

    lax.fori_loop(jnp.where(rank == 0, 1, rank + 2), n_ctx, sent_block, 0)

    def sent_part(o, c):
        arrive(part.at[o], ret_send.at[o - 1])
        return c

    lax.fori_loop(1, rank - 1, sent_part, 0)
    arrive(stat_land.at[:, pl.ds(0, others)], stat_sem.at[0])
    arrive(hub_kv.at[:, pl.ds(0, others)], hub_sem.at[0])
    arrive(hub_land, hred_sem.at[0])
    arrive(hub_pair.at[pl.ds(1, pairs - 1)], pair_sem.at[0])

    @pl.when(has_far)
    def _():
        arrive(far_kv.at[:, pl.ds(0, others)], far_sem.at[0])
        arrive(far_land.at[pl.ds(0, others)], red_send.at[0])

    @pl.when((rank == 0) & (me == 0))
    def _():
        arrive(hub_kv.at[:, pl.ds(0, others)], kv_sem.at[0])

    @pl.when(lends)
    def _():
        arrive(kv_own.at[:, pl.ds(0, others)], kv_sem.at[0])
        arrive(blk_land.at[pl.ds(0, others)], blk_send.at[0])

    @pl.when(rank > 0)
    def _():
        arrive(hub_sum, tree_send.at[0])

    @pl.when((rank == 0) & (me > 0))
    def _():
        arrive(hub_sum, last_sem.at[0])

    @pl.when(has_next)
    def _():
        prev_copy().wait_send()

    @pl.when(has_prev)
    def _():
        back_copy().wait_send()


def tail(dq_in, dk_in, dv_in, dq_out, dk_out, dv_out, stores):
    n_head, per, block, heads, _ = dq_in.shape
    routes = [
        (dq_in.at[k, j], dq_out.at[pl.ds(j * block, block), pl.ds(k * heads, heads)])
        for k in range(n_head)
        for j in range(per)
    ]
    routes += [(dk_in, dk_out), (dv_in, dv_out)]
    copies = [
        pltpu.make_async_copy(source, target, stores.at[i])
        for i, (source, target) in enumerate(routes)
    ]
    for copy in copies:
        copy.start()
    for copy in copies:
        copy.wait()


def shards(
    n_ctx,
    n_head,
    queries,
    key_states,
    value_states,
    out_grad,
    log_sums,
    row_deltas,
    block_pairs,
    pair_kinds,
):
    rows, all_heads, width = queries.shape
    heads = all_heads // n_head
    n_slot = block_pairs.shape[1]
    n_far = n_slot - NEAR
    per = rows // BLOCK
    blocks = per * n_head
    lanes = BLOCK * heads
    n_far_here = per * n_far
    stages = (n_ctx - 1).bit_length()
    bf16, f32 = jnp.bfloat16, jnp.float32
    flat = (rows * n_head, width)
    term = (BLOCK, width)
    piece = (BLOCK // CUTS, width)
    chunks = 2 * CUTS
    vmem = pl.BlockSpec(memory_space=pltpu.VMEM)
    smem = pl.BlockSpec(memory_space=pltpu.SMEM)
    anywhere = pl.BlockSpec(memory_space=pl.ANY)
    dma = pltpu.SemaphoreType.DMA
    raw = pltpu.VMEM((n_head, per, BLOCK, heads, width), bf16)
    rolled = pltpu.VMEM((n_head, per, lanes, width), bf16)
    dq, dk, dv = pl.pallas_call(
        partial(kernel, n_ctx, n_head, n_slot),
        out_shape=(raw, pltpu.VMEM(flat, bf16), pltpu.VMEM(flat, bf16)),
        in_specs=[smem, smem, anywhere, anywhere, vmem, vmem, vmem, vmem],
        out_specs=(vmem, vmem, vmem),
        scratch_shapes=[
            pltpu.VMEM(flat, f32),
            pltpu.VMEM((2, n_head, per) + term, bf16),
            pltpu.VMEM((blocks,) + term, bf16),
            pltpu.VMEM((blocks,) + term, bf16),
            pltpu.VMEM((2, n_head) + term, bf16),
            pltpu.VMEM((2, n_ctx) + term, bf16),
            pltpu.VMEM((n_ctx,) + term, bf16),
            pltpu.VMEM((n_ctx,) + term, bf16),
            pltpu.VMEM((2, n_head, n_far_here) + term, bf16),
            pltpu.VMEM((2, n_head, n_far_here) + term, bf16),
            pltpu.VMEM((2, n_head) + term, bf16),
            raw,
            raw,
            rolled,
            rolled,
            pltpu.VMEM((2, n_head, heads, rows), f32),
            pltpu.VMEM((per, 2 * n_head, lanes), f32),
            pltpu.VMEM((n_head, per, lanes, width), f32),
            pltpu.VMEM((2, n_head, per) + term, f32),
            pltpu.VMEM((n_head, 2) + term, f32),
            pltpu.VMEM((n_head, 2) + term, f32),
            pltpu.VMEM((n_head, chunks, n_far_here) + piece, f32),
            pltpu.VMEM((n_head, chunks, n_far_here) + piece, f32),
            pltpu.VMEM((n_head, 2) + term, f32),
            pltpu.VMEM((n_head // 2, 2) + term, f32),
            pltpu.VMEM((n_head // 2, 2) + term, f32),
            pltpu.VMEM((2,) + term, f32),
            pltpu.VMEM((stages, 2) + term, f32),
            pltpu.VMEM((n_head, 2) + term, f32),
            pltpu.VMEM((n_ctx, chunks) + piece, f32),
            pltpu.VMEM((chunks, n_ctx) + piece, f32),
            pltpu.VMEM((n_head, chunks, per) + piece, f32),
            pltpu.VMEM((n_head, chunks, per) + piece, f32),
            pltpu.SMEM((n_ctx,), jnp.int32),
            pltpu.SMEM((blocks * n_far,), jnp.int32),
            dma((2,)),
            dma((3,)),
            dma((2,)),
            dma((2,)),
            dma((n_ctx,)),
            dma((2, n_ctx - 2)),
            dma((4,)),
            dma((2,)),
            dma((2,)),
            dma((2,)),
            dma((2,)),
            dma((1,)),
            dma((stages, 2)),
            dma((3,)),
            dma((1,)),
            dma((chunks,)),
            dma((n_ctx - NEAR,)),
            dma((chunks, n_ctx - NEAR)),
            dma((1,)),
            dma((chunks,)),
            pltpu.SemaphoreType.REGULAR,
        ],
        compiler_params=pltpu.CompilerParams(
            collective_id=0, has_side_effects=True, vmem_limit_bytes=60 * 1024 * 1024
        ),
    )(
        block_pairs.T,
        pair_kinds.T,
        queries,
        out_grad,
        key_states.reshape(flat),
        value_states.reshape(flat),
        log_sums,
        row_deltas,
    )
    dq, dk, dv = pl.pallas_call(
        tail,
        out_shape=(
            jax.ShapeDtypeStruct(queries.shape, bf16),
            jax.ShapeDtypeStruct(flat, bf16),
            jax.ShapeDtypeStruct(flat, bf16),
        ),
        in_specs=[vmem] * 3,
        out_specs=(anywhere,) * 3,
        scratch_shapes=[dma((n_head * per + 2,))],
    )(*(pltpu.with_memory_space_constraint(x, pltpu.VMEM) for x in (dq, dk, dv)))
    return dq, dk.reshape(key_states.shape), dv.reshape(value_states.shape)


def solution(mesh):
    tokens = P(("ctx", "head"), None, None)
    stats = P("head", "ctx")
    return jax.shard_map(
        partial(shards, mesh.shape["ctx"], mesh.shape["head"]),
        mesh=mesh,
        in_specs=(tokens, tokens, tokens, tokens, stats, stats, P(), P()),
        out_specs=(tokens, tokens, tokens),
        check_vma=False,
    )
```
